32 devices in a mesh: rep: 4 (over x, core), fsdp: 4 (over z), seq: 2 (over y).
Axes of the slice: x: 2, y: 2, z: 4, core: 2. Of those that a mesh axis runs over, the one named last changes fastest.
Arguments:
- tokens: bfloat16 [16, 592, 1024], P(('rep', 'fsdp'), 'seq'), may hold values from -6 to 6
- slot_mask: int32 [16], P(('rep', 'fsdp')), may hold values 0 or 1
- cotangent: bfloat16 [16, 592, 1024], P(('rep', 'fsdp'), 'seq'), may hold values from -6 to 6
- w_qkv: float32 [1024, 3072], P('fsdp'), may hold values from -0.25 to 0.25
- w_out: float32 [1024, 1024], P('fsdp'), may hold values from -0.75 to 0.75
- w_fc1: float32 [1024, 4096], P('fsdp'), may hold values from -0.1875 to 0.1875
- w_fc2: float32 [4096, 1024], P('fsdp'), may hold values from -0.125 to 0.125
- ln_gains: float32 [2, 1024], P(None, 'fsdp'), may hold values from 0.5 to 1.5
- biases: float32 [6, 1024], P(None, 'fsdp'), may hold values from -2 to 2
- fc1_bias: float32 [4096], P('fsdp'), may hold values from -2 to 2
Outputs:
- output: bfloat16 [16, 592, 1024], P(('rep', 'fsdp'), 'seq')
- grad_tokens: bfloat16 [16, 592, 1024], P(('rep', 'fsdp'), 'seq')
- grad_w_qkv: float32 [1024, 3072], P('fsdp')
- grad_w_out: float32 [1024, 1024], P('fsdp')
- grad_w_fc1: float32 [1024, 4096], P('fsdp')
- grad_w_fc2: float32 [4096, 1024], P('fsdp')
- grad_ln_gains: float32 [2, 1024], P(None, 'fsdp')
- grad_biases: float32 [6, 1024], P(None, 'fsdp')
- grad_fc1_bias: float32 [4096], P('fsdp')
The draws below stay inside these ranges and needn't reach their ends.
All inputs are finite; a program needn't handle non-finite values. No bound on the sum of `slot_mask` on one device may be relied on, other than what follows from the above.
Results may differ from the reference program's by a relative error of at most 0.02.
The reference program's roundings to bfloat16 on the way count: a program that leaves them out, or rounds other values in their place, can miss the bound.
Values may be sent and summed in bfloat16 or wider, within the bound.
No kernel may reach another device: no remote copies, remote signals or barrier semaphores. Data moves between devices by JAX's collectives and lax.ppermute only.
A program may use at most 192 MiB of HBM per device.

```python
import jax
import jax.numpy as jnp
from jax import lax

D = 1024
HEADS = 16
HEAD_DIM = 64
FF = 4096
IMG_TOK = 577
SLOT_LEN = 592
SLOTS = 16


def place_ends(values, own_key, low, high):
    index_at = [jax.random.randint(jax.random.fold_in(own_key, axis), (), 0, length) for axis, length in enumerate(values.shape)]
    main_axis = values.shape.index(max(values.shape))
    neighbour = index_at[:main_axis] + [(index_at[main_axis] + 1) % values.shape[main_axis]] + index_at[main_axis + 1:]
    return values.at[tuple(index_at)].set(low).at[tuple(neighbour)].set(high)


def block_scale(stream_key, dims, shards, least, high):
    factor_of, own = 1.0, jax.random.fold_in(stream_key, 6)
    for position, blocks in shards:
        draws = jnp.exp(jax.random.uniform(jax.random.fold_in(own, position), (blocks,), jnp.float32, least / len(shards), high / len(shards)))
        factor_of = factor_of * jnp.repeat(draws, dims[position] // blocks).reshape([-1 if axis == position else 1 for axis in range(len(dims))])
    return factor_of


def normal_values(stream_key, shape, spread, reach, split=(), held_as=jnp.bfloat16):
    values = jax.random.normal(stream_key, shape, jnp.float32) * spread
    if len(split) > 0:
        values = block_scale(stream_key, shape, split, -0.22, 0.18) * values
    return jnp.clip(values, min=-reach, max=reach).astype(held_as)


def setup_inputs(seed: int = 0) -> dict:
    key_list = jax.random.split(jax.random.key(seed), 11)
    tokens = normal_values(key_list[0], (SLOTS, SLOT_LEN, D), 1.0, 6.0, ((0, 16), (1, 2)))
    slot_mask = place_ends((jax.random.randint(key_list[1], (SLOTS,), 0, 8) < 7).astype(jnp.int32), jax.random.fold_in(key_list[1], 1), 0, 1)
    cotangent = normal_values(key_list[2], (SLOTS, SLOT_LEN, D), 1.0, 6.0, ((0, 16), (1, 2)))
    w_qkv = normal_values(key_list[3], (D, 3 * D), (D // 2) ** -0.5, 0.25, ((0, 4),), jnp.float32)
    w_out = normal_values(key_list[4], (D, D), (D // 16) ** -0.5, 0.75, ((0, 4),), jnp.float32)
    w_fc1 = normal_values(key_list[5], (D, FF), D ** -0.5, 0.1875, ((0, 4),), jnp.float32)
    w_fc2 = normal_values(key_list[6], (FF, D), (FF // 2) ** -0.5, 0.125, ((0, 4),), jnp.float32)
    ln_gains = jnp.clip(1.0 + 0.1 * jax.random.normal(key_list[7], (2, D), jnp.float32), 0.5, 1.5)
    biases = normal_values(key_list[8], (6, D), 0.3, 2.0, ((1, 4),), jnp.float32)
    fc1_bias = normal_values(key_list[9], (FF,), 0.3, 2.0, ((0, 4),), jnp.float32)
    return dict(tokens=tokens, slot_mask=slot_mask, cotangent=cotangent, w_qkv=w_qkv, w_out=w_out, w_fc1=w_fc1, w_fc2=w_fc2, ln_gains=ln_gains, biases=biases, fc1_bias=fc1_bias)


@jax.custom_vjp
def low(v):
    return lax.optimization_barrier(v.astype(jnp.bfloat16)).astype(jnp.float32)

@jax.custom_vjp
def low_back(v):
    return v

def low_keep(v):
    return (low(v), None)

def low_pass(kept, grad):
    return (grad,)

def back_keep(v):
    return (v, None)

def back_low(kept, grad):
    return (low(grad),)
low.defvjp(low_keep, low_pass)
low_back.defvjp(back_keep, back_low)
EPSILON = 1e-05

def product(left_rows, right_rows):
    return jnp.dot(left_rows, right_rows, precision=lax.Precision.HIGHEST)

def normalize(inputs, gain_row, shift_row):
    center = inputs - lax.optimization_barrier(jnp.mean(inputs, axis=-1, keepdims=True))
    scaled = center * lax.rsqrt(lax.optimization_barrier(jnp.mean(center * center, axis=-1, keepdims=True)) + EPSILON)
    return scaled * gain_row + shift_row

def attend(queries, keys_all, values_all):
    length = queries.shape[0]
    query_heads = queries.reshape(length, HEADS, HEAD_DIM)
    key_heads = keys_all.reshape(length, HEADS, HEAD_DIM)
    value_heads = values_all.reshape(length, HEADS, HEAD_DIM)
    scores = low_back(jnp.einsum('qhd,khd->hqk', query_heads, key_heads, precision=lax.Precision.HIGHEST))
    valid_keys = jnp.arange(length) < IMG_TOK
    scores = jnp.where(valid_keys[None, None, :], scores, -1e+30)
    weights = low(jax.nn.softmax(scores, axis=-1))
    mixed_rows = jnp.einsum('hqk,khd->qhd', weights, value_heads, precision=lax.Precision.HIGHEST)
    return mixed_rows.reshape(length, D)

def block(inputs, keep_mask, w_qkv, w_out, w_fc1, w_fc2, ln_gains, biases, fc1_bias):
    w_qkv = low(w_qkv)
    w_out = low(w_out)
    w_fc1 = low(w_fc1)
    w_fc2 = low(w_fc2)
    ln_gains = low(ln_gains)
    biases = low(biases)
    fc1_bias = low(fc1_bias)
    head_scale = HEAD_DIM ** (-0.5)
    normed = low(normalize(inputs, ln_gains[0], biases[0]))
    joined = product(normed, w_qkv)
    queries = low(low_back((joined[:, :D] + biases[1]) * head_scale))
    keys_all = low(low_back(joined[:, D:2 * D]))
    values_all = low(low_back(joined[:, 2 * D:] + biases[2]))
    mixed_rows = low(low_back(jax.checkpoint(attend)(queries, keys_all, values_all)))
    branch = low_back(product(mixed_rows, w_out) + biases[3])
    middle = inputs + branch
    normed_two = low(normalize(middle, ln_gains[1], biases[4]))
    hidden = low_back(product(normed_two, w_fc1) + fc1_bias)
    active = low(hidden * jax.nn.sigmoid(1.702 * hidden))
    result = low_back(product(active, w_fc2) + biases[5])
    return (middle + result) * keep_mask[:, None]

def reference(tokens, slot_mask, cotangent, w_qkv, w_out, w_fc1, w_fc2, ln_gains, biases, fc1_bias):
    weight_list = (w_qkv, w_out, w_fc1, w_fc2, ln_gains, biases, fc1_bias)
    positions = (jnp.arange(SLOT_LEN) < IMG_TOK).astype(jnp.float32)

    def one_slot(totals, blocks_in):
        inputs, valid_flag, incoming = blocks_in
        keep_mask = positions * valid_flag.astype(jnp.float32)

        def forward(source, *weights):
            return block(source, keep_mask, *weights)
        output, pullback = jax.vjp(forward, inputs.astype(jnp.float32), *weight_list)
        gradients = pullback(incoming.astype(jnp.float32))
        totals = tuple((total_now + grad_now for total_now, grad_now in zip(totals, gradients[1:])))
        return (totals, (output.astype(jnp.bfloat16), gradients[0].astype(jnp.bfloat16)))
    initial = tuple((jnp.zeros_like(weight) for weight in weight_list))
    totals, (outputs, input_grads) = lax.scan(one_slot, initial, (tokens, slot_mask, cotangent))
    return (outputs, input_grads, totals[0], totals[1], totals[2], totals[3], totals[4], totals[5], totals[6])
```

```python
import functools

import jax
import jax.numpy as jnp
from jax import lax
from jax.experimental import pallas as pl
from jax.experimental.pallas import tpu as pltpu
from jax.sharding import PartitionSpec as P

HEADS = 16
HEAD_DIM = 64
IMG_TOK = 577
EPSILON = 1e-05
NEGATIVE = -1e30
LANES = 128
BF = jnp.bfloat16
F32 = jnp.float32

ANY = pl.BlockSpec(memory_space=pl.ANY)
VM = pl.BlockSpec(memory_space=pltpu.VMEM)
SM = pl.BlockSpec(memory_space=pltpu.SMEM)

ORDER = (0, 2, 1, 3)


def mm(a, b):
    return lax.dot_general(a, b, (((1,), (0,)), ((), ())), preferred_element_type=F32)


def mmt(a, b):
    return lax.dot_general(a, b, (((1,), (1,)), ((), ())), preferred_element_type=F32)


def tmm(a, b):
    return lax.dot_general(a, b, (((0,), (0,)), ((), ())), preferred_element_type=F32)


def normalize(inputs):
    center = inputs - jnp.mean(inputs, axis=-1, keepdims=True)
    inverse = lax.rsqrt(jnp.mean(center * center, axis=-1, keepdims=True) + EPSILON)
    return center * inverse, inverse


def norm_back(grad_in, scaled, inverse, gain_row):
    weighted = grad_in * gain_row
    return inverse * (
        weighted
        - jnp.mean(weighted, axis=-1, keepdims=True)
        - scaled * jnp.mean(weighted * scaled, axis=-1, keepdims=True)
    )


def at(index, size):
    return pl.ds(pl.multiple_of(index * size, size), size)


def flip(r, d):
    return jnp.bitwise_xor(r, d) if d else r


def fetch(copies, sems):
    handles = [pltpu.make_async_copy(s, t, sems.at[i]) for i, (s, t) in enumerate(copies)]
    for handle in handles:
        handle.start()
    return handles


def finish(handles):
    for handle in handles:
        handle.wait()


def call(body, ins, specs, outs, scratch, flops, name, out_specs=None):
    moved = sum(a.size * a.dtype.itemsize for a in ins)
    moved += sum(s.size * s.dtype.itemsize for s in outs)
    return pl.pallas_call(
        body,
        out_shape=outs,
        in_specs=specs,
        out_specs=out_specs or [VM] * len(outs),
        scratch_shapes=scratch,
        compiler_params=pltpu.CompilerParams(vmem_limit_bytes=56 << 20),
        cost_estimate=pl.CostEstimate(flops=flops, bytes_accessed=moved, transcendentals=0),
        name=name,
    )(*ins)


def shape(dims, dtype):
    return jax.ShapeDtypeStruct(dims, dtype)


def column_copies(refs, w, ids, n, relative=False):
    r, z = ids[0], ids[2]
    q = w.shape[1] // 4
    slots = [(ORDER.index(d), d) for d in range(4)]
    if len(refs) == 1:
        if not relative:
            return [(refs[0], w)]
        return [
            (refs[0].at[:, at(flip(r, d), q)], w.at[:, pl.ds(s * q, q)]) for s, d in slots
        ]
    rows = w.shape[0] // n
    here = at(z, rows)
    if relative:
        copies = [
            (refs[0].at[:, at(flip(r, d), q)], w.at[here, pl.ds(s * q, q)]) for s, d in slots
        ]
    else:
        copies = [(refs[0], w.at[here, :])]
    for k in range(1, n):
        there = at(lax.rem(z - k + n, n), rows)
        for s, d in slots:
            columns = pl.ds(s * q, q) if relative else at(flip(r, d), q)
            copies.append((refs[1 + (k - 1) * 4 + d], w.at[there, columns]))
    return copies


def row_copies(refs, w, ids, n):
    r, z = ids[0], ids[2]
    if len(refs) == 1:
        return [(refs[0], w)]
    h = w.shape[0] // (4 * n)
    copies = [(refs[0].at[i], w.at[at(i * n + z, h), :]) for i in range(4)]
    for k in range(1, n):
        there = lax.rem(z - k + n, n)
        for d in range(4):
            copies.append(
                (refs[1 + (k - 1) * 4 + d], w.at[at(flip(r, d) * n + there, h), :])
            )
    return copies


def split(refs, *counts):
    refs = list(refs)
    out = []
    for count in counts:
        out.append(refs[:count])
        refs = refs[count:]
    return out + [refs]


def qkv_kernel(n, pieces, ids, own, near, vec, qb, vb, *refs):
    weights, (normed, queries, keys, values), (w, sems) = split(refs, pieces, 4)
    handles = fetch(column_copies(weights, w, ids, n), sems)
    rows = own.shape[0]
    for i, part in enumerate((own, near)):
        scaled, _ = normalize(part[...].astype(F32))
        normed[i * rows : (i + 1) * rows, :] = (scaled * vec[0:1, :] + vec[2:3, :]).astype(BF)
    finish(handles)
    scale = HEAD_DIM ** (-0.5)

    def step(i, carry):
        joined = mm(normed[...], w[:, at(i, 3 * LANES)])
        here = at(i, LANES)
        queries[:, here] = ((joined[:, :LANES] + qb[:, here]) * scale).astype(BF)
        keys[:, here] = joined[:, LANES : 2 * LANES].astype(BF)
        values[:, here] = (joined[:, 2 * LANES :] + vb[:, here]).astype(BF)
        return carry

    lax.fori_loop(0, 4, step, 0)


def valid_keys(ids, rows, real):
    index = lax.broadcasted_iota(jnp.int32, (1, 2 * rows), 1)
    second = (index >= rows).astype(jnp.int32)
    local = index - second * rows
    position = jnp.bitwise_xor(second, ids[1]) * real + local
    return (local < real) & (position < IMG_TOK)


def head_half(value, half):
    lane = lax.broadcasted_iota(jnp.int32, value.shape, 1)
    keep = (lane < HEAD_DIM) if half == 0 else (lane >= HEAD_DIM)
    return jnp.where(keep, value, jnp.zeros_like(value))


def softmax(scores, valid):
    scores = jnp.where(valid, scores, NEGATIVE)
    exponent = jnp.exp(scores - jnp.max(scores, axis=-1, keepdims=True))
    return exponent * (1.0 / jnp.sum(exponent, axis=-1, keepdims=True))


def attend_kernel(rows, real, ids, queries, keys, values, mixed_own, mixed_near):
    valid = valid_keys(ids, rows, real)
    keys_of = [head_half(keys[...], half) for half in range(2)]
    values_of = [head_half(values[...], half) for half in range(2)]
    for i, target in enumerate((mixed_own, mixed_near)):
        block = queries[i * rows : (i + 1) * rows, :]
        total = None
        for half in range(2):
            weights = softmax(mmt(block, keys_of[half]), valid).astype(BF)
            part = mm(weights, values_of[half])
            total = part if total is None else total + part
        target[...] = total.astype(BF)


def attend(ids, queries, keys, values, rows, real):
    wide = queries.shape[1]
    block = pl.BlockSpec((2 * rows, LANES), lambda i, ids: (0, i))
    half = pl.BlockSpec((rows, LANES), lambda i, ids: (0, i))
    return pl.pallas_call(
        functools.partial(attend_kernel, rows, real),
        grid_spec=pltpu.PrefetchScalarGridSpec(
            num_scalar_prefetch=1,
            grid=(wide // LANES,),
            in_specs=[block] * 3,
            out_specs=[half] * 2,
        ),
        out_shape=[shape((rows, wide), BF)] * 2,
        compiler_params=pltpu.CompilerParams(vmem_limit_bytes=56 << 20),
        cost_estimate=pl.CostEstimate(
            flops=8 * (2 * rows) ** 2 * wide,
            bytes_accessed=8 * rows * wide * 2,
            transcendentals=0,
        ),
        name="attend",
    )(ids, queries, keys, values)


def slot_of(i):
    return ((i & 1) << 1) | (i >> 1)


def attend_back_kernel(
    rows, real, ids, queries, keys, values, grad_own, grad_near, near, far, sums
):
    i = pl.program_id(0)
    valid = valid_keys(ids, rows, real)
    keys_of = [head_half(keys[...], half) for half in range(2)]
    values_of = [head_half(values[...], half) for half in range(2)]
    grad_k = grad_v = None
    grad_q = []
    for part, grad_ref in enumerate((grad_own, grad_near)):
        block = queries[part * rows : (part + 1) * rows, :]
        grad = grad_ref[...]
        total = None
        for half in range(2):
            probs = softmax(mmt(block, keys_of[half]), valid)
            grad_probs = mmt(grad, values_of[half])
            inner = jnp.sum(probs * grad_probs, axis=-1, keepdims=True)
            grad_scores = (probs * (grad_probs - inner)).astype(BF)
            first = mm(grad_scores, keys_of[half])
            total = first if total is None else total + first
            second = tmm(grad_scores, head_half(block, half))
            third = tmm(probs.astype(BF), head_half(grad, half))
            grad_k = second if grad_k is None else grad_k + second
            grad_v = third if grad_v is None else grad_v + third
        grad_q.append(total)
    scale = HEAD_DIM ** (-0.5)
    grad_q = jnp.concatenate(grad_q, axis=0).astype(BF).astype(F32) * scale
    pieces = [grad_q.astype(BF), grad_k.astype(BF), grad_v.astype(BF)]
    for kind, piece in enumerate(pieces):
        columns = slice(kind * LANES, (kind + 1) * LANES)
        sums[:, columns] = jnp.sum(piece.astype(F32), axis=0, keepdims=True)

        @pl.when(i < 2)
        def _():
            near[:, columns] = piece

        @pl.when(i >= 2)
        def _():
            far[:, columns] = piece


def attend_back(ids, queries, keys, values, grad_own, grad_near, rows, real):
    wide = queries.shape[1]

    def column(i, ids):
        return (0, jnp.bitwise_xor(ids[0], slot_of(i)))

    block = pl.BlockSpec((2 * rows, LANES), column)
    half = pl.BlockSpec((rows, LANES), column)
    pair = (2, 2 * rows, 3 * LANES)
    return pl.pallas_call(
        functools.partial(attend_back_kernel, rows, real),
        grid_spec=pltpu.PrefetchScalarGridSpec(
            num_scalar_prefetch=1,
            grid=(4,),
            in_specs=[block] * 3 + [half] * 2,
            out_specs=[
                pl.BlockSpec((None,) + pair[1:], lambda i, ids: (jnp.minimum(i, 1), 0, 0)),
                pl.BlockSpec((None,) + pair[1:], lambda i, ids: (jnp.maximum(i - 2, 0), 0, 0)),
                pl.BlockSpec((None, 1, 3 * LANES), lambda i, ids: (i, 0, 0)),
            ],
        ),
        out_shape=[shape(pair, BF), shape(pair, BF), shape((4, 1, 3 * LANES), F32)],
        compiler_params=pltpu.CompilerParams(vmem_limit_bytes=56 << 20),
        cost_estimate=pl.CostEstimate(
            flops=20 * (2 * rows) ** 2 * wide,
            bytes_accessed=16 * rows * wide * 2,
            transcendentals=0,
        ),
        name="attend_back",
    )(ids, queries, keys, values, grad_own, grad_near)


def project_kernel(n, pieces, ids, tokens, mixed_own, mixed_near, vec, *refs):
    weights, (mixed, middle, normed), (w, sems) = split(refs, pieces, 3)
    handles = fetch(column_copies(weights, w, ids, n), sems)
    y = ids[1]
    half = mixed_own.shape[1]
    mixed[:, at(y, half)] = mixed_own[...]
    mixed[:, at(1 - y, half)] = mixed_near[...]
    finish(handles)
    total = tokens[...].astype(F32) + (mm(mixed[...], w[...]) + vec[5:6, :])
    middle[...] = total
    scaled, _ = normalize(total)
    normed[...] = (scaled * vec[1:2, :] + vec[6:7, :]).astype(BF)


def mlp_kernel(n, one, two, ids, n_own, n_near, g_own, g_near, fb, *refs):
    ones, twos, outs, scratch = split(refs, one, two, 7)
    act_near, act_far, gh_near, gh_far, grad_own, grad_near, sums = outs
    w1, w2, normed, grads, total, sems = scratch
    r = ids[0]
    rows = n_own.shape[0]
    handles = fetch(column_copies(ones, w1, ids, n) + row_copies(twos, w2, ids, n), sems)
    normed[:rows, :] = n_own[...]
    normed[rows:, :] = n_near[...]
    grads[:rows, :] = g_own[...]
    grads[rows:, :] = g_near[...]
    total[...] = jnp.zeros_like(total)
    finish(handles)
    wide = w1.shape[1] // 4

    def step(i, carry):
        here = at(i, wide)
        hidden = mm(normed[...], w1[:, here]) + fb[:, here]
        gate = 1.0 / (1.0 + jnp.exp(-1.702 * hidden))
        active = (hidden * gate).astype(BF)
        grad_active = mmt(grads[...], w2[here, :])
        grad_hidden = (
            grad_active * (gate + 1.702 * hidden * gate * (1.0 - gate))
        ).astype(BF)
        sums[:, here] = jnp.sum(grad_hidden.astype(F32), axis=0, keepdims=True)
        total[...] += mmt(grad_hidden, w1[:, here])
        d = jnp.bitwise_xor(r, i)

        @pl.when((d & 1) == 0)
        def _():
            act_near[d >> 1] = active
            gh_near[d >> 1] = grad_hidden

        @pl.when((d & 1) == 1)
        def _():
            act_far[d >> 1] = active
            gh_far[d >> 1] = grad_hidden

        return carry

    lax.fori_loop(0, 4, step, 0)
    grad_own[...] = total[:rows, :]
    grad_near[...] = total[rows:, :].astype(BF)


def result_kernel(n, two, ids, act_near, act_far, *refs):
    twos, (own, near), (w2, total, sems) = split(refs, two, 2)
    r = ids[0]
    handles = fetch(row_copies(twos, w2, ids, n), sems)
    rows = own.shape[0]
    wide = w2.shape[0] // 4
    finish(handles)
    for s, d in enumerate(ORDER):
        part = act_near if s < 2 else act_far
        value = mm(part[s % 2], w2[at(flip(r, d), wide), :])
        if s:
            value = value + total[...]
        if s < 3:
            total[...] = value
    own[...] = value[:rows, :]
    near[...] = value[rows:, :].astype(BF)


def middle_back_kernel(
    n, pieces, ids, grad_own, grad_recv, middle, incoming, vec, *refs
):
    weights, outs, (w, work, sems) = split(refs, pieces, 5)
    grad_middle, branch, mixed_own, mixed_near, sums = outs
    handles = fetch(column_copies(weights, w, ids, n), sems)
    y = ids[1]
    grad = grad_own[...] + grad_recv[...].astype(F32)
    scaled, inverse = normalize(middle[...])
    sums[0:1, :] = jnp.sum(grad * scaled, axis=0, keepdims=True)
    sums[1:2, :] = jnp.sum(grad, axis=0, keepdims=True)
    arriving = incoming[...].astype(F32)
    sums[3:4, :] = jnp.sum(arriving, axis=0, keepdims=True)
    total = arriving + norm_back(grad, scaled, inverse, vec[1:2, :])
    grad_middle[...] = total
    low = total.astype(BF)
    branch[...] = low
    sums[2:3, :] = jnp.sum(low.astype(F32), axis=0, keepdims=True)
    finish(handles)
    work[...] = mmt(branch[...], w[...]).astype(BF)
    half = work.shape[1] // 2
    mixed_own[...] = work[:, at(y, half)]
    mixed_near[...] = work[:, at(1 - y, half)]


def qkv_back_kernel(n, pieces, ids, near, far, *refs):
    weights, (own, other), (w, grads, sems) = split(refs, pieces, 2)
    wide = near.shape[2]
    copies = column_copies(weights, w, ids, n, relative=True)
    for s in range(4):
        source = (near if s < 2 else far).at[s % 2]
        copies.append((source, grads.at[:, pl.ds(s * wide, wide)]))
    finish(fetch(copies, sems))
    rows = own.shape[0]
    step_rows = 256

    def step(i, carry):
        here = at(i, step_rows)
        value = mmt(grads[...], w[here, :])
        own[:, here] = value[:rows, :]
        other[:, here] = value[rows:, :].astype(BF)
        return carry

    lax.fori_loop(0, w.shape[0] // step_rows, step, 0)


def tokens_back_kernel(grad_own, grad_recv, tokens, grad_middle, vec, out, sums):
    grad = grad_own[...] + grad_recv[...].astype(F32)
    scaled, inverse = normalize(tokens[...].astype(F32))
    sums[0:1, :] = jnp.sum(grad * scaled, axis=0, keepdims=True)
    sums[1:2, :] = jnp.sum(grad, axis=0, keepdims=True)
    total = grad_middle[...] + norm_back(grad, scaled, inverse, vec[0:1, :])
    out[...] = total.astype(BF)[: out.shape[0], :]


def weight_kernel(lefts, rights, left_slot, right_slot, *refs):
    left_refs, right_refs, (out,), (a, b, sems) = split(refs, lefts, rights, 1)
    copies = []
    for parts, target, slot in ((left_refs, a, left_slot), (right_refs, b, right_slot)):
        start = 0
        for part in parts:
            source = part if slot is None else part.at[slot]
            count = source.shape[0]
            copies.append((source, target.at[pl.ds(start, count), :]))
            start += count
    finish(fetch(copies, sems))
    step_rows = 256

    def step(i, carry):
        here = at(i, step_rows)
        out[here, :] = tmm(a[:, here], b[...]).astype(out.dtype)
        return carry

    lax.fori_loop(0, out.shape[0] // step_rows, step, 0)


def weight_grad(left, right, left_slot, right_slot, dtype, name):
    def span(parts, slot):
        dims = [p.shape if slot is None else p.shape[1:] for p in parts]
        return sum(d[0] for d in dims), dims[0][1]

    depth, rows = span(left, left_slot)
    _, columns = span(right, right_slot)
    return call(
        functools.partial(weight_kernel, len(left), len(right), left_slot, right_slot),
        [*left, *right],
        [ANY] * (len(left) + len(right)),
        [shape((rows, columns), dtype)],
        [
            pltpu.VMEM((depth, rows), BF),
            pltpu.VMEM((depth, columns), BF),
            pltpu.SemaphoreType.DMA((len(left) + len(right),)),
        ],
        2 * depth * rows * columns,
        name,
    )[0]


def out_grad_kernel(ids, mixed, mixed_far, branch, branch_far, send, keep, a, b, sems):
    r, y = ids[0], ids[1]
    rows = mixed.shape[0]
    half = branch.shape[1] // 2
    quarters = half // LANES
    copies = []
    for i, (left, right) in enumerate(((mixed, branch), (mixed_far, branch_far))):
        here = pl.ds(i * rows, rows)
        copies.append((left, a.at[here, :]))
        for s, (dy, d) in enumerate(((1, 2), (1, 0), (0, 2), (0, 0))):
            block = flip(y, dy) * quarters + flip(r, d)
            copies.append((right.at[:, at(block, LANES)], b.at[here, pl.ds(s * LANES, LANES)]))
    finish(fetch(copies, sems))
    step_rows = 256

    def step(i, carry):
        here = at(i, step_rows)
        value = tmm(a[:, here], b[...])
        send[here, :] = value[:, : 2 * LANES].astype(BF)
        keep[here, :] = value[:, 2 * LANES :]
        return carry

    lax.fori_loop(0, a.shape[1] // step_rows, step, 0)


def combine_kernel(n, ids, keep, recv, own, *sends):
    z = ids[2]
    rows = own.shape[0]
    for k in range(n):
        here = at(lax.rem(z + k, n), rows)
        value = keep[here, :] + recv[here, :].astype(F32)
        if k:
            sends[k - 1][...] = value.astype(BF)
        else:
            own[...] = value


def place_kernel(kind, ids, *refs):
    pieces, (out,), _ = split(refs, 8, 1)
    r, y = ids[0], ids[1]
    for dy in range(2):
        for d in range(4):
            piece = pieces[dy * 4 + d]
            block = flip(y, dy) * 4 + flip(r, d)
            if kind == "rows":
                out[at(block, piece.shape[0]), :] = piece[...].astype(F32)
                continue
            groups = piece.shape[1] // LANES
            for g in range(groups):
                columns = at(block + g * 8, LANES)
                out[:, columns] = piece[:, g * LANES : (g + 1) * LANES].astype(F32)


def on_device(sizes, tokens, slot_mask, cotangent, w_qkv, w_out, w_fc1, w_fc2, ln_gains, biases, fc1_bias):
    n, reps, seqs = sizes
    slot_count, real, wide = tokens.shape
    assert slot_count == 1 and reps == 4 and seqs == 2
    direct = n == 4
    rows = -(-real // 16) * 16
    hidden = fc1_bias.shape[0] * n
    half, part_hidden = wide // 2, hidden // 2
    h = hidden // n // 8
    r, y, z = lax.axis_index("rep"), lax.axis_index("seq"), lax.axis_index("fsdp")
    ids = jnp.stack([r, y, z]).astype(jnp.int32)

    def core(v):
        return lax.ppermute(v, "rep", [(i, i ^ 1) for i in range(reps)])

    def across(v):
        return lax.ppermute(v, "rep", [(i, i ^ 2) for i in range(reps)])

    def near(v):
        return lax.ppermute(v, "seq", [(0, 1), (1, 0)])

    def shift(v, k):
        return lax.ppermute(v, "fsdp", [(i, (i + k) % n) for i in range(n)])

    def qkv_part(start, size):
        parts = [
            lax.dynamic_slice_in_dim(w_qkv, kind * wide + y * half + start, size, axis=1)
            for kind in range(3)
        ]
        return [p.astype(BF) for p in parts]

    def qkv_half():
        parts = qkv_part(0, half)
        return jnp.concatenate(
            [p[:, i * LANES : (i + 1) * LANES] for i in range(4) for p in parts], axis=1
        )

    def fc1_half():
        grid = w_fc1.reshape(w_fc1.shape[0], n, 2, 4, h)
        grid = lax.dynamic_index_in_dim(grid, y, axis=2, keepdims=False).astype(BF)
        return grid.transpose(0, 2, 1, 3).reshape(w_fc1.shape[0], part_hidden)

    def fc1_half_direct():
        blocks = []
        for zz in range(n):
            start = zz * (hidden // n) + y * (4 * h)
            blocks.append(lax.dynamic_slice_in_dim(w_fc1, start, 4 * h, axis=1).astype(BF))
        return jnp.concatenate(
            [b[:, i * h : (i + 1) * h] for i in range(4) for b in blocks], axis=1
        )

    fc2_half = lax.dynamic_slice_in_dim(w_fc2, y * 4 * h, 4 * h, axis=0).astype(BF)
    fc2_half = fc2_half.reshape(4, h, wide)
    out_own = w_out.astype(BF)

    def gather(own, piece):
        arrays = [own]
        for k in range(1, n):
            first = shift(piece, k)
            second = across(first)
            arrays += [first, core(first), second, core(second)]
        return arrays

    if direct:
        qkv_piece = jnp.concatenate(qkv_part(r * LANES, LANES), axis=1)
        out_piece = lax.dynamic_slice_in_dim(w_out, r * (wide // 4), wide // 4, axis=1).astype(BF)
        fc1_piece = jnp.concatenate(
            [
                lax.dynamic_slice_in_dim(
                    w_fc1, zz * (hidden // n) + y * (4 * h) + r * h, h, axis=1
                ).astype(BF)
                for zz in range(n)
            ],
            axis=1,
        )
        fc2_piece = lax.dynamic_slice_in_dim(w_fc2, y * (4 * h) + r * h, h, axis=0).astype(BF)
        all_qkv = gather(qkv_half(), qkv_piece)
        all_out = gather(out_own, out_piece)
        all_fc1 = gather(fc1_half_direct(), fc1_piece)
        all_fc2 = gather(fc2_half, fc2_piece)
    else:
        whole = functools.partial(lax.all_gather, axis_name="fsdp", axis=0, tiled=True)
        all_qkv, all_out, all_fc1 = [whole(qkv_half())], [whole(out_own)], [whole(fc1_half())]
        everyone = lax.all_gather(fc2_half, "fsdp", axis=1, tiled=True)
        all_fc2 = [everyone.reshape(part_hidden, wide)]

    small = jnp.concatenate(
        [ln_gains, biases, fc1_bias.reshape(hidden // wide, wide // n)], axis=0
    ).astype(BF)
    if direct:
        gathered = jnp.zeros((n,) + small.shape, BF)
        for k in range(n):
            block = shift(small, k) if k else small
            gathered = lax.dynamic_update_slice_in_dim(
                gathered, block[None], lax.rem(z - k + n, n), axis=0
            )
    else:
        gathered = lax.all_gather(small, "fsdp", axis=0)
    gathered = gathered.astype(F32)
    vec = gathered[:, :8].transpose(1, 0, 2).reshape(8, wide)
    hidden_shift = gathered[:, 8:].reshape(n, 2, 4, h)
    hidden_shift = lax.dynamic_index_in_dim(hidden_shift, y, axis=1, keepdims=False)
    hidden_shift = hidden_shift.transpose(1, 0, 2).reshape(1, part_hidden)
    query_shift = lax.dynamic_slice(vec, (3, y * half), (1, half))
    value_shift = lax.dynamic_slice(vec, (4, y * half), (1, half))

    pad = ((0, rows - real), (0, 0))
    tok = jnp.pad(tokens[0], pad)
    tok_near = near(tok)
    positions = y * real + jnp.arange(real)
    keep = slot_mask.astype(F32)[0] * (positions < IMG_TOK).astype(F32)
    keep = keep[:, None]
    grads = jnp.pad((cotangent[0].astype(F32) * keep).astype(BF), pad)
    grads_near = near(grads)
    grads_far, grads_near_far = core(grads), core(grads_near)

    count = len(all_qkv)
    sems = lambda c: pltpu.SemaphoreType.DMA((c,))
    two = 2 * rows
    normed, queries, keys, values = call(
        functools.partial(qkv_kernel, n, count),
        [ids, tok, tok_near, vec, query_shift, value_shift, *all_qkv],
        [SM] + [VM] * 5 + [ANY] * count,
        [shape((two, wide), BF)] + [shape((two, half), BF)] * 3,
        [pltpu.VMEM((wide, 3 * half), BF), sems(count + 8)],
        2 * two * wide * 3 * half,
        "qkv",
    )
    normed_far = core(normed)
    mixed_own, mixed_send = attend(ids, queries, keys, values, rows, real)
    mixed_recv = near(mixed_send)
    mixed, middle, normed_two = call(
        functools.partial(project_kernel, n, count),
        [ids, tok, mixed_own, mixed_recv, vec, *all_out],
        [SM] + [VM] * 4 + [ANY] * count,
        [shape((rows, wide), BF), shape((rows, wide), F32), shape((rows, wide), BF)],
        [pltpu.VMEM((wide, wide), BF), sems(count + 8)],
        2 * rows * wide * wide,
        "project",
    )
    normed_two_near = near(normed_two)
    pair = (2, two, part_hidden // 4)
    act_near, act_far, gh_near, gh_far, gtwo_own, gtwo_send, hidden_sums = call(
        functools.partial(mlp_kernel, n, count, count),
        [ids, normed_two, normed_two_near, grads, grads_near, hidden_shift, *all_fc1, *all_fc2],
        [SM] + [VM] * 5 + [ANY] * (2 * count),
        [shape(pair, BF)] * 4
        + [shape((rows, wide), F32), shape((rows, wide), BF), shape((1, part_hidden), F32)],
        [
            pltpu.VMEM((wide, part_hidden), BF),
            pltpu.VMEM((part_hidden, wide), BF),
            pltpu.VMEM((two, wide), BF),
            pltpu.VMEM((two, wide), BF),
            pltpu.VMEM((two, wide), F32),
            sems(2 * count + 16),
        ],
        6 * two * wide * part_hidden,
        "mlp",
    )
    gtwo_recv = near(gtwo_send)
    act_other, gh_other = core(act_far), core(gh_far)
    normed_two_far, normed_two_near_far = core(normed_two), core(normed_two_near)
    mixed_far = core(mixed)

    result_own, result_send = call(
        functools.partial(result_kernel, n, count),
        [ids, act_near, act_far, *all_fc2],
        [SM] + [VM] * 2 + [ANY] * count,
        [shape((rows, wide), F32), shape((rows, wide), BF)],
        [
            pltpu.VMEM((part_hidden, wide), BF),
            pltpu.VMEM((two, wide), F32),
            sems(count + 8),
        ],
        2 * two * wide * part_hidden,
        "result",
    )
    result_recv = near(result_send)
    total = middle[:real] + (
        result_own[:real] + result_recv[:real].astype(F32) + vec[7:8, :]
    )
    output = (total * keep).astype(BF)[None]

    def reduce_plane(make):
        sent = across(make(1, BF))
        return make(0, F32), sent

    def reduce_rows(kept, received):
        count_rows = kept.shape[0] // n
        if direct:
            outs = [shape((count_rows, kept.shape[1]), F32)]
            outs += [shape((count_rows, kept.shape[1]), BF)] * (n - 1)
            mine, *sends = call(
                functools.partial(combine_kernel, n),
                [ids, kept, received],
                [SM, VM, VM],
                outs,
                [],
                kept.size,
                "combine",
            )
            total = mine
            for k in range(1, n):
                total = total + shift(sends[k - 1], k).astype(F32)
            return total.astype(BF)
        summed = (kept + received.astype(F32)).astype(BF)
        return lax.psum_scatter(summed, "fsdp", scatter_dimension=0, tiled=True)

    def spread(piece, dims, kind):
        pieces = [piece, near(piece)]
        pieces = [[p, across(p)] for p in pieces]
        pieces = [[a, core(a), b, core(b)] for a, b in pieces]
        flat = pieces[0] + pieces[1]
        if direct:
            return call(
                functools.partial(place_kernel, kind),
                [ids, *flat],
                [SM] + [VM] * 8,
                [shape(dims, F32)],
                [],
                dims[0] * dims[1],
                "place",
            )[0]
        stack = jnp.stack(flat)
        order = (jnp.bitwise_xor(jnp.arange(2), y) * 4)[:, None]
        order = (order + jnp.bitwise_xor(jnp.arange(4), r)[None, :]).reshape(-1)
        stack = jnp.take(stack, order, axis=0).astype(F32)
        if kind == "rows":
            return stack.reshape(dims)
        groups = dims[1] // (8 * min(h, LANES)) if kind == "hidden" else dims[1] // (8 * LANES)
        stack = stack.reshape(8, dims[0], groups, -1)
        return stack.transpose(1, 2, 0, 3).reshape(dims)

    grad_fc2 = spread(
        reduce_rows(
            *reduce_plane(
                lambda s, t: weight_grad(
                    [act_near, act_other],
                    [grads, grads_near, grads_far, grads_near_far],
                    s,
                    None,
                    t,
                    "grad_fc2",
                )
            )
        ),
        w_fc2.shape,
        "rows",
    )
    grad_fc1 = spread(
        reduce_rows(
            *reduce_plane(
                lambda s, t: weight_grad(
                    [normed_two, normed_two_near, normed_two_far, normed_two_near_far],
                    [gh_near, gh_other],
                    None,
                    s,
                    t,
                    "grad_fc1",
                )
            )
        ),
        w_fc1.shape,
        "hidden",
    )

    grad_middle, branch, gmix_own, gmix_send, sums_two = call(
        functools.partial(middle_back_kernel, n, count),
        [ids, gtwo_own, gtwo_recv, middle, grads, vec, *all_out],
        [SM] + [VM] * 5 + [ANY] * count,
        [
            shape((rows, wide), F32),
            shape((rows, wide), BF),
            shape((rows, half), BF),
            shape((rows, half), BF),
            shape((4, wide), F32),
        ],
        [pltpu.VMEM((wide, wide), BF), pltpu.VMEM((rows, wide), BF), sems(count + 8)],
        2 * rows * wide * wide,
        "middle_back",
    )
    gmix_recv = near(gmix_send)
    branch_far = core(branch)
    gj_near, gj_far, joined_sums = attend_back(
        ids, queries, keys, values, gmix_own, gmix_recv, rows, real
    )
    gj_other = core(gj_far)
    gone_own, gone_send = call(
        functools.partial(qkv_back_kernel, n, count),
        [ids, gj_near, gj_far, *all_qkv],
        [SM] + [ANY] * (2 + count),
        [shape((rows, wide), F32), shape((rows, wide), BF)],
        [
            pltpu.VMEM((wide, 3 * half), BF),
            pltpu.VMEM((two, 3 * half), BF),
            sems(count + 16),
        ],
        2 * two * wide * 3 * half,
        "qkv_back",
    )
    gone_recv = near(gone_send)
    grad_qkv = spread(
        reduce_rows(
            *reduce_plane(
                lambda s, t: weight_grad(
                    [normed, normed_far], [gj_near, gj_other], None, s, t, "grad_qkv"
                )
            )
        ),
        w_qkv.shape,
        "columns",
    )
    out_send, out_keep = call(
        out_grad_kernel,
        [ids, mixed, mixed_far, branch, branch_far],
        [SM] + [ANY] * 4,
        [shape((wide, 2 * LANES), BF), shape((wide, 2 * LANES), F32)],
        [pltpu.VMEM((two, wide), BF), pltpu.VMEM((two, 4 * LANES), BF), sems(10)],
        2 * two * wide * 4 * LANES,
        "grad_out",
    )
    out_recv = near(out_send).astype(F32)
    out_sum = out_keep + out_recv
    out_cross = across(out_sum[:, :LANES].astype(BF))
    grad_out = spread(reduce_rows(out_sum[:, LANES:], out_cross), w_out.shape, "columns")

    grad_tokens, sums_one = call(
        tokens_back_kernel,
        [gone_own, gone_recv, tok, grad_middle, vec],
        [VM] * 5,
        [shape((real, wide), BF), shape((2, wide), F32)],
        [],
        rows * wide,
        "tokens_back",
    )
    grad_tokens = grad_tokens[None]

    wanted = jnp.bitwise_xor(jnp.arange(4), r)
    slots = ((wanted & 1) << 1) | (wanted >> 1)
    chosen = (slots[:, None] == jnp.arange(4)[None, :]).astype(F32)
    joined_sums = jnp.sum(chosen[:, :, None] * joined_sums[None, :, 0, :], axis=1)
    here = (jnp.arange(2) == y).astype(F32)

    def spread_half(row):
        return (here[:, None] * row.reshape(1, half)).reshape(1, wide)

    query_sums = spread_half(joined_sums[:, :LANES])
    value_sums = spread_half(joined_sums[:, 2 * LANES :])
    hidden_sums = hidden_sums.reshape(4, n, h).transpose(1, 0, 2).reshape(n, 1, 4 * h)
    hidden_sums = (hidden_sums * here[None, :, None]).reshape(hidden // wide, wide)
    block = jnp.concatenate(
        [
            sums_one[0:1],
            sums_two[0:1],
            sums_one[1:2],
            query_sums,
            value_sums,
            sums_two[2:3],
            sums_two[1:2],
            sums_two[3:4],
            hidden_sums,
        ],
        axis=0,
    )
    if direct:
        block = block + core(block)
        block = block + near(block)
        block = block + across(block)
        total = block
        for k in range(1, n):
            total = total + shift(block, k)
        block = total
    else:
        block = lax.psum(block, ("rep", "seq", "fsdp"))
    narrow = lax.dynamic_slice_in_dim(block[:8], z * (wide // n), wide // n, axis=1)
    flat = lax.dynamic_slice_in_dim(block[8:].reshape(-1), z * (hidden // n), hidden // n)
    return (
        output,
        grad_tokens,
        grad_qkv,
        grad_out,
        grad_fc1,
        grad_fc2,
        narrow[:2],
        narrow[2:],
        flat,
    )


def solution(mesh):
    sizes = (mesh.shape["fsdp"], mesh.shape["rep"], mesh.shape["seq"])
    return jax.shard_map(
        functools.partial(on_device, sizes),
        mesh=mesh,
        in_specs=(
            P(("rep", "fsdp"), "seq", None),
            P(("rep", "fsdp")),
            P(("rep", "fsdp"), "seq", None),
            P("fsdp", None),
            P("fsdp", None),
            P("fsdp", None),
            P("fsdp", None),
            P(None, "fsdp"),
            P(None, "fsdp"),
            P("fsdp"),
        ),
        out_specs=(
            P(("rep", "fsdp"), "seq", None),
            P(("rep", "fsdp"), "seq", None),
            P("fsdp", None),
            P("fsdp", None),
            P("fsdp", None),
            P("fsdp", None),
            P(None, "fsdp"),
            P(None, "fsdp"),
            P("fsdp"),
        ),
        check_vma=False,
    )
```

```python
import functools

import jax
import jax.numpy as jnp
from jax import lax
from jax.experimental import pallas as pl
from jax.experimental.pallas import tpu as pltpu
from jax.sharding import Mesh
from jax.sharding import PartitionSpec as P

HEADS = 16
HEAD_DIM = 64
IMG_TOK = 577
EPSILON = 1e-05
NEGATIVE = -1e30
LANES = 128
BF = jnp.bfloat16
F32 = jnp.float32

ANY = pl.BlockSpec(memory_space=pl.ANY)
VM = pl.BlockSpec(memory_space=pltpu.VMEM)
SM = pl.BlockSpec(memory_space=pltpu.SMEM)

ORDER = (0, 2, 1, 3)
OUT_LANE = 3 * LANES


def mm(a, b):
    return lax.dot_general(a, b, (((1,), (0,)), ((), ())), preferred_element_type=F32)


def mmt(a, b):
    return lax.dot_general(a, b, (((1,), (1,)), ((), ())), preferred_element_type=F32)


def tmm(a, b):
    return lax.dot_general(a, b, (((0,), (0,)), ((), ())), preferred_element_type=F32)


def normalize(inputs):
    center = inputs - jnp.mean(inputs, axis=-1, keepdims=True)
    inverse = lax.rsqrt(jnp.mean(center * center, axis=-1, keepdims=True) + EPSILON)
    return center * inverse, inverse


def norm_back(grad_in, scaled, inverse, gain_row):
    weighted = grad_in * gain_row
    return inverse * (
        weighted
        - jnp.mean(weighted, axis=-1, keepdims=True)
        - scaled * jnp.mean(weighted * scaled, axis=-1, keepdims=True)
    )


def at(index, size):
    return pl.ds(pl.multiple_of(index * size, size), size)


def flip(r, d):
    return jnp.bitwise_xor(r, d) if d else r


def fetch(copies, sems):
    handles = [pltpu.make_async_copy(s, t, sems.at[i]) for i, (s, t) in enumerate(copies)]
    for handle in handles:
        handle.start()
    return handles


def finish(handles):
    for handle in handles:
        handle.wait()


COST = pl.CostEstimate(flops=1 << 33, bytes_accessed=1 << 18, transcendentals=0)


def call(body, ins, specs, outs, scratch, name, out_specs=None):
    return pl.pallas_call(
        body,
        out_shape=outs,
        in_specs=specs,
        out_specs=out_specs or [VM] * len(outs),
        scratch_shapes=scratch,
        compiler_params=pltpu.CompilerParams(vmem_limit_bytes=56 << 20),
        cost_estimate=COST,
        name=name,
    )(*ins)


def shape(dims, dtype):
    return jax.ShapeDtypeStruct(dims, dtype)


def column_copies(refs, w, ids, lane=0, relative=False):
    rows, q = w.shape[0], w.shape[1] // 4
    copies = []
    for d in range(4):
        slot = pl.ds(ORDER.index(d) * q, q) if relative else at(flip(ids[0], d), q)
        source = refs[d & 1].at[pl.ds((d >> 1) * rows, rows), pl.ds(lane, q)]
        copies.append((source, w.at[:, slot]))
    return copies


def row_copies(refs, w, ids):
    q = w.shape[0] // 4
    return [
        (refs[d & 1].at[pl.ds((d >> 1) * q, q), :], w.at[at(flip(ids[0], d), q), :])
        for d in range(4)
    ]


def split(refs, *counts):
    refs = list(refs)
    out = []
    for count in counts:
        out.append(refs[:count])
        refs = refs[count:]
    return out + [refs]


def qkv_kernel(ids, own, near, vec, *refs):
    weights, (normed, queries, keys, values), (w, sems) = split(refs, 2, 4)
    handles = fetch(column_copies(weights, w, ids), sems)
    rows = own.shape[0]
    for i, part in enumerate((own, near)):
        scaled, _ = normalize(part[...].astype(F32))
        normed[i * rows : (i + 1) * rows, :] = (scaled * vec[0:1, :] + vec[2:3, :]).astype(BF)
    finish(handles)
    scale = HEAD_DIM ** (-0.5)
    first = ids[1] * (queries.shape[1] // LANES)

    def step(i, carry):
        joined = mm(normed[...], w[:, at(i, 3 * LANES)])
        here = at(i, LANES)
        there = at(first + i, LANES)
        queries[:, here] = ((joined[:, :LANES] + vec[3:4, there]) * scale).astype(BF)
        keys[:, here] = joined[:, LANES : 2 * LANES].astype(BF)
        values[:, here] = (joined[:, 2 * LANES :] + vec[4:5, there]).astype(BF)
        return carry

    lax.fori_loop(0, 4, step, 0)


def valid_keys(ids, rows, real):
    index = lax.broadcasted_iota(jnp.int32, (2 * rows, 1), 0)
    second = (index >= rows).astype(jnp.int32)
    local = index - second * rows
    position = jnp.bitwise_xor(second, ids[1]) * real + local
    return (local < real) & (position < IMG_TOK)


def head_half(value, half):
    lane = lax.broadcasted_iota(jnp.int32, value.shape, 1)
    keep = (lane < HEAD_DIM) if half == 0 else (lane >= HEAD_DIM)
    return jnp.where(keep, value, jnp.zeros_like(value))


def with_lanes(value, half, columns):
    lane = lax.broadcasted_iota(jnp.int32, value.shape, 1)
    out = head_half(value, half)
    for i, column in enumerate(columns):
        out = jnp.where(lane == (1 - half) * HEAD_DIM + i, column, out)
    return out


def three_parts(column):
    high = column.astype(BF)
    rest = column - high.astype(F32)
    middle = rest.astype(BF)
    return [high, middle, (rest - middle.astype(F32)).astype(BF)]


def key_shift(ids, rows, real):
    shift = jnp.where(valid_keys(ids, rows, real), 0.0, NEGATIVE)
    return shift.astype(BF)


def attend_kernel(rows, real, ids, queries, keys, values, mixed_own, mixed_near, totals):
    one = jnp.ones((1, 1), BF)
    shift = key_shift(ids, rows, real)
    keys_of = [with_lanes(keys[...], half, [shift]) for half in range(2)]
    values_of = [head_half(values[...], half) for half in range(2)]
    for i, target in enumerate((mixed_own, mixed_near)):
        block = queries[i * rows : (i + 1) * rows, :]
        total = None
        for half in range(2):
            scores = mmt(keys_of[half], with_lanes(block, half, [one]))
            highest = jnp.max(scores, axis=0, keepdims=True)
            exponent = jnp.exp(scores - highest)
            sums = jnp.sum(exponent, axis=0, keepdims=True)
            totals[2 * half + i : 2 * half + i + 1, :] = highest + jnp.log(sums)
            part = tmm(values_of[half], exponent.astype(BF)) * (1.0 / sums)
            total = part if total is None else total + part
        target[...] = total.T.astype(BF)


def attend(ids, queries, keys, values, rows, real):
    wide = queries.shape[1]
    steps = wide // LANES
    block = pl.BlockSpec((2 * rows, LANES), lambda i, ids: (0, i))
    half = pl.BlockSpec((rows, LANES), lambda i, ids: (0, i))
    return pl.pallas_call(
        functools.partial(attend_kernel, rows, real),
        grid_spec=pltpu.PrefetchScalarGridSpec(
            num_scalar_prefetch=1,
            grid=(steps,),
            in_specs=[block] * 3,
            out_specs=[half] * 2 + [pl.BlockSpec((None, 4, rows), lambda i, ids: (i, 0, 0))],
        ),
        out_shape=[shape((rows, wide), BF)] * 2 + [shape((steps, 4, rows), F32)],
        compiler_params=pltpu.CompilerParams(vmem_limit_bytes=56 << 20),
        cost_estimate=COST,
        name="attend",
    )(ids, queries, keys, values)


def attend_back_kernel(
    rows, real, ids, queries, keys, values, mixed_own, mixed_near, grad_own, grad_near,
    totals, out, sums,
):
    one = jnp.ones((1, 1), BF)
    shift = key_shift(ids, rows, real)
    keys_of = [head_half(keys[...], half) for half in range(2)]
    wide_keys = [with_lanes(keys[...], half, [shift, one, one, one]) for half in range(2)]
    wide_values = [with_lanes(values[...], half, [one, one, one]) for half in range(2)]
    lines = jnp.concatenate([totals[...], jnp.zeros_like(totals[...])], axis=0).T
    grad_k = grad_v = None
    grad_q = []
    for part, (mixed, grad_ref) in enumerate(((mixed_own, grad_own), (mixed_near, grad_near))):
        block = queries[part * rows : (part + 1) * rows, :]
        grad = grad_ref[...]
        product = grad.astype(F32) * mixed[...].astype(F32)
        total = None
        for half in range(2):
            line = three_parts(-lines[:, 2 * half + part : 2 * half + part + 1])
            probs = jnp.exp(mmt(wide_keys[half], with_lanes(block, half, [one, *line])))
            inner = jnp.sum(head_half(product, half), axis=1, keepdims=True)
            wide_grad = with_lanes(grad, half, three_parts(-inner))
            grad_scores = (probs * mmt(wide_values[half], wide_grad)).astype(BF)
            first = tmm(keys_of[half], grad_scores)
            total = first if total is None else total + first
            second = mm(grad_scores, head_half(block, half))
            third = mm(probs.astype(BF), head_half(grad, half))
            grad_k = second if grad_k is None else grad_k + second
            grad_v = third if grad_v is None else grad_v + third
        grad_q.append(total.T)
    scale = HEAD_DIM ** (-0.5)
    grad_q = jnp.concatenate(grad_q, axis=0).astype(BF).astype(F32) * scale
    pieces = [grad_q.astype(BF), grad_k.astype(BF), grad_v.astype(BF)]
    for kind, piece in enumerate(pieces):
        columns = slice(kind * LANES, (kind + 1) * LANES)
        sums[:, columns] = jnp.sum(piece.astype(F32), axis=0, keepdims=True)
        out[:, columns] = piece


def attend_back(ids, saved, mixed, grads, totals, rows, real, first):
    def index(i, ids):
        return jnp.bitwise_xor(ids[0], first + 2 * i)

    block = pl.BlockSpec((2 * rows, LANES), lambda i, ids: (0, index(i, ids)))
    half = pl.BlockSpec((rows, LANES), lambda i, ids: (0, index(i, ids)))
    lines = pl.BlockSpec((None, 4, rows), lambda i, ids: (index(i, ids), 0, 0))
    whole = pl.BlockSpec((None, 2 * rows, 3 * LANES), lambda i, ids: (i, 0, 0))
    line = pl.BlockSpec((None, 1, 3 * LANES), lambda i, ids: (i, 0, 0))
    return pl.pallas_call(
        functools.partial(attend_back_kernel, rows, real),
        grid_spec=pltpu.PrefetchScalarGridSpec(
            num_scalar_prefetch=1,
            grid=(2,),
            in_specs=[block] * 3 + [half] * 4 + [lines],
            out_specs=[whole, line],
        ),
        out_shape=[shape((2, 2 * rows, 3 * LANES), BF), shape((2, 1, 3 * LANES), F32)],
        compiler_params=pltpu.CompilerParams(vmem_limit_bytes=56 << 20),
        cost_estimate=COST,
        name="attend_back",
    )(ids, *saved, *mixed, *grads, totals)


def project_kernel(ids, tokens, mixed_own, mixed_near, vec, *refs):
    weights, (mixed, middle, normed), (w, sems) = split(refs, 2, 3)
    handles = fetch(column_copies(weights, w, ids, OUT_LANE), sems)
    y = ids[1]
    half = mixed_own.shape[1]
    mixed[:, at(y, half)] = mixed_own[...]
    mixed[:, at(1 - y, half)] = mixed_near[...]
    finish(handles)
    total = tokens[...].astype(F32) + (mm(mixed[...], w[...]) + vec[5:6, :])
    middle[...] = total
    scaled, _ = normalize(total)
    normed[...] = (scaled * vec[1:2, :] + vec[6:7, :]).astype(BF)


def mlp_kernel(ids, n_own, n_near, g_own, g_near, fb, *refs):
    ones, twos, outs, scratch = split(refs, 2, 2, 5)
    near, far, grad_own, grad_near, sums = outs
    w1, w2, normed, grads, total, sems = scratch
    r = ids[0]
    rows = n_own.shape[0]
    handles = fetch(column_copies(ones, w1, ids) + row_copies(twos, w2, ids), sems)
    normed[:rows, :] = n_own[...]
    normed[rows:, :] = n_near[...]
    grads[:rows, :] = g_own[...]
    grads[rows:, :] = g_near[...]
    wide = w1.shape[1] // 4
    far[:, 4 * wide :] = normed[...]
    total[...] = jnp.zeros_like(total)
    finish(handles)

    def step(i, carry):
        here = at(i, wide)
        hidden = mm(normed[...], w1[:, here]) + fb[:, here]
        gate = 1.0 / (1.0 + jnp.exp(-1.702 * hidden))
        active = (hidden * gate).astype(BF)
        grad_active = mmt(grads[...], w2[here, :])
        grad_hidden = (
            grad_active * (gate + 1.702 * hidden * gate * (1.0 - gate))
        ).astype(BF)
        sums[:, here] = jnp.sum(grad_hidden.astype(F32), axis=0, keepdims=True)
        total[...] += mmt(grad_hidden, w1[:, here])
        d = jnp.bitwise_xor(r, i)

        @pl.when((d & 1) == 0)
        def _():
            near[:, at(d >> 1, wide)] = grad_hidden
            near[:, at(2 + (d >> 1), wide)] = active

        @pl.when((d & 1) == 1)
        def _():
            far[:, at(d >> 1, wide)] = grad_hidden
            far[:, at(2 + (d >> 1), wide)] = active

        return carry

    lax.fori_loop(0, 4, step, 0)
    grad_own[...] = total[:rows, :]
    grad_near[...] = total[rows:, :].astype(BF)


def result_kernel(ids, near, far, *refs):
    twos, (own, other), (w2, total, sems) = split(refs, 2, 2)
    r = ids[0]
    finish(fetch(row_copies(twos, w2, ids), sems))
    rows = own.shape[0]
    wide = w2.shape[0] // 4
    for s, d in enumerate(ORDER):
        part = near if s < 2 else far
        slot = 2 + s % 2
        value = mm(part[:, slot * wide : (slot + 1) * wide], w2[at(flip(r, d), wide), :])
        if s:
            value = value + total[...]
        if s < 3:
            total[...] = value
    own[...] = value[:rows, :]
    other[...] = value[rows:, :].astype(BF)


def middle_back_kernel(ids, grad_own, grad_recv, middle, incoming, vec, *refs):
    weights, outs, (w, work, sems) = split(refs, 2, 5)
    grad_middle, branch, mixed_own, mixed_near, sums = outs
    handles = fetch(column_copies(weights, w, ids, OUT_LANE), sems)
    y = ids[1]
    grad = grad_own[...] + grad_recv[...].astype(F32)
    scaled, inverse = normalize(middle[...])
    sums[0:1, :] = jnp.sum(grad * scaled, axis=0, keepdims=True)
    sums[1:2, :] = jnp.sum(grad, axis=0, keepdims=True)
    arriving = incoming[...].astype(F32)
    sums[3:4, :] = jnp.sum(arriving, axis=0, keepdims=True)
    total = arriving + norm_back(grad, scaled, inverse, vec[1:2, :])
    grad_middle[...] = total
    low = total.astype(BF)
    branch[...] = low
    sums[2:3, :] = jnp.sum(low.astype(F32), axis=0, keepdims=True)
    finish(handles)
    work[...] = mmt(branch[...], w[...]).astype(BF)
    half = work.shape[1] // 2
    mixed_own[...] = work[:, at(y, half)]
    mixed_near[...] = work[:, at(1 - y, half)]


def qkv_back_kernel(ids, near, far, *refs):
    weights, (own, other), (w, grads, sems) = split(refs, 2, 2)
    wide = near.shape[2]
    copies = column_copies(weights, w, ids, relative=True)
    for s in range(4):
        source = (near if s < 2 else far).at[s % 2]
        copies.append((source, grads.at[:, pl.ds(s * wide, wide)]))
    finish(fetch(copies, sems))
    rows = own.shape[0]
    step_rows = 256

    def step(i, carry):
        here = at(i, step_rows)
        value = mmt(grads[...], w[here, :])
        own[:, here] = value[:rows, :]
        other[:, here] = value[rows:, :].astype(BF)
        return carry

    lax.fori_loop(0, w.shape[0] // step_rows, step, 0)


def tokens_back_kernel(ids, grad_own, grad_recv, tokens, grad_middle, vec, out, sums):
    grad = grad_own[...] + grad_recv[...].astype(F32)
    scaled, inverse = normalize(tokens[...].astype(F32))
    sums[0:1, :] = jnp.sum(grad * scaled, axis=0, keepdims=True)
    sums[1:2, :] = jnp.sum(grad, axis=0, keepdims=True)
    total = grad_middle[...] + norm_back(grad, scaled, inverse, vec[0:1, :])
    out[...] = total.astype(BF)[: out.shape[0], :]


def window(ref, pick):
    if pick is None:
        return ref
    if len(ref.shape) == 3:
        return ref.at[pick]
    return ref.at[:, pl.ds(*pick)]


def extent(array, pick):
    if pick is None:
        return array.shape
    if array.ndim == 3:
        return array.shape[1:]
    return (array.shape[0], pick[1])


def weight_kernel(left_picks, right_picks, more, ids, *refs):
    left_refs, right_refs, extra, rest = split(refs, len(left_picks), len(right_picks), more)
    *outs, a, b, sems = rest
    copies = []
    for parts, target, picks in ((left_refs, a, left_picks), (right_refs, b, right_picks)):
        start = 0
        for part, pick in zip(parts, picks):
            source = window(part, pick)
            count = source.shape[0]
            copies.append((source, target.at[pl.ds(start, count), :]))
            start += count
    finish(fetch(copies, sems))
    if len(outs) > 1:
        rows = outs[0].shape[0]
        for k, out in enumerate(outs):
            here = at(lax.rem(ids[2] + k, len(outs)), rows)
            value = tmm(a[:, here], b[...])
            if more:
                value = value + extra[0][here, :].astype(F32)
            out[...] = value.astype(out.dtype)
        return
    (out,) = outs
    step_rows = 256

    def step(i, carry):
        here = at(i, step_rows)
        value = tmm(a[:, here], b[...])
        if more:
            value = value + extra[0][here, :].astype(F32)
        out[here, :] = value.astype(out.dtype)
        return carry

    lax.fori_loop(0, out.shape[0] // step_rows, step, 0)


def weight_grad(ids, left, right, name, extra=(), blocks=1):
    def span(parts):
        dims = [extent(*p) for p in parts]
        return sum(d[0] for d in dims), dims[0][1]

    depth, rows = span(left)
    _, columns = span(right)
    kinds = [F32] + [BF] * (blocks - 1) if blocks > 1 else [BF]
    return call(
        functools.partial(
            weight_kernel, [p for _, p in left], [p for _, p in right], len(extra)
        ),
        [ids] + [a for a, _ in left] + [a for a, _ in right] + list(extra),
        [SM] + [ANY] * (len(left) + len(right)) + [VM] * len(extra),
        [shape((rows // blocks, columns), kind) for kind in kinds],
        [
            pltpu.VMEM((depth, rows), BF),
            pltpu.VMEM((depth, columns), BF),
            pltpu.SemaphoreType.DMA((len(left) + len(right),)),
        ],
        name,
    )


def out_grad_kernel(ids, mixed, mixed_far, branch, branch_far, send, keep, a, b, sems):
    r, y = ids[0], ids[1]
    rows = mixed.shape[0]
    half = branch.shape[1] // 2
    quarters = half // LANES
    copies = []
    for i, (left, right) in enumerate(((mixed, branch), (mixed_far, branch_far))):
        here = pl.ds(i * rows, rows)
        copies.append((left, a.at[here, :]))
        for s, (dy, d) in enumerate(((1, 2), (1, 0), (0, 2), (0, 0))):
            block = flip(y, dy) * quarters + flip(r, d)
            copies.append((right.at[:, at(block, LANES)], b.at[here, pl.ds(s * LANES, LANES)]))
    finish(fetch(copies, sems))
    step_rows = 256

    def step(i, carry):
        here = at(i, step_rows)
        value = tmm(a[:, here], b[...])
        send[here, :] = value[:, : 2 * LANES].astype(BF)
        keep[here, :] = value[:, 2 * LANES :]
        return carry

    lax.fori_loop(0, a.shape[1] // step_rows, step, 0)


def combine_kernel(ids, keep, recv, *outs):
    rows = outs[0].shape[0]
    for k, out in enumerate(outs):
        here = at(lax.rem(ids[2] + k, len(outs)), rows)
        out[...] = (keep[here, :] + recv[here, :].astype(F32)).astype(out.dtype)


def join(parts):
    return parts[0] if len(parts) == 1 else jnp.concatenate(parts, axis=1)


def cast_qkv_kernel(ids, first, second, third, fourth, gains, biases, shift, out, low):
    rows = first.shape[0]
    out[:rows, :] = join([part[...].astype(BF) for part in (first, second, third, fourth)])
    low[...] = jnp.zeros_like(low)
    width = gains.shape[1]
    low[0:2, :width] = gains[...]
    low[2:8, :width] = biases[...]
    low[8:12, :width] = shift[...]
    out[rows:, :] = low[...].astype(BF)


def cast_rest_kernel(n, ids, *refs):
    ones, (two_part,), (one, two) = split(refs, n, 1)
    one[...] = join([part[...].astype(BF) for part in ones])
    two[...] = two_part[...].astype(BF)


def cast(body, ids, blocks, outs, scratch, name):
    specs = [pl.BlockSpec(block, lambda i, ids, at=at: at(ids)) for _, block, at in blocks]
    return pl.pallas_call(
        body,
        grid_spec=pltpu.PrefetchScalarGridSpec(
            num_scalar_prefetch=1,
            grid=(1,),
            in_specs=specs,
            out_specs=[pl.BlockSpec(o.shape, lambda i, ids: (0, 0)) for o in outs],
            scratch_shapes=scratch,
        ),
        out_shape=outs,
        compiler_params=pltpu.CompilerParams(vmem_limit_bytes=56 << 20),
        cost_estimate=COST,
        name=name,
    )(ids, *[array for array, _, _ in blocks])


def stack_kernel(n, ids, *refs):
    parts, (out, *more), _ = split(refs, 2 * n, 1 if len(refs) == 2 * n + 1 else 2)
    rows = out.shape[1]
    for i, part in enumerate(parts):
        there = lax.rem(ids[2] - i % n + n, n)
        out[(i // n) * n + there] = part[:rows, :]
        if more and i < n:
            width = more[0].shape[1] // n
            low = part[rows:, :width].astype(F32)
            more[0][:, at(there, width)] = low


def place_kernel(kind, ids, *refs):
    sources, (out,), _ = split(refs, 4, 1)
    for d, source in enumerate(sources):
        for dy in range(2):
            block = flip(ids[1], dy) * 4 + flip(ids[0], d)
            piece = source[dy].astype(F32)
            if kind == "rows":
                out[at(block, piece.shape[0]), :] = piece
                continue
            for g in range(piece.shape[1] // LANES):
                columns = at(block + g * 8, LANES)
                out[:, columns] = piece[:, g * LANES : (g + 1) * LANES]


def place(ids, sources, dims, kind):
    count, rows, columns = sources[0].shape
    steps = 4
    if kind == "rows":
        inside = pl.BlockSpec((count, rows, columns // steps), lambda i, ids: (0, 0, i))
        outside = pl.BlockSpec((dims[0], dims[1] // steps), lambda i, ids: (0, i))
    else:
        inside = pl.BlockSpec((count, rows // steps, columns), lambda i, ids: (0, i, 0))
        outside = pl.BlockSpec((dims[0] // steps, dims[1]), lambda i, ids: (i, 0))
    return pl.pallas_call(
        functools.partial(place_kernel, kind),
        grid_spec=pltpu.PrefetchScalarGridSpec(
            num_scalar_prefetch=1, grid=(steps,), in_specs=[inside] * 4, out_specs=outside
        ),
        out_shape=shape(dims, F32),
        compiler_params=pltpu.CompilerParams(vmem_limit_bytes=40 << 20),
        cost_estimate=COST,
        name="place",
    )(ids, *sources)


def after(value, *others):
    return lax.optimization_barrier((value, *others))[0]


def on_device(n, tokens, slot_mask, cotangent, w_qkv, w_out, w_fc1, w_fc2, ln_gains, biases, fc1_bias):
    slot_count, real, wide = tokens.shape
    assert slot_count == 1
    direct = n == 4
    rows = -(-real // 16) * 16
    hidden = fc1_bias.shape[0] * n
    half, part_hidden = wide // 2, hidden // 2
    h = hidden // n // 8
    x, c = lax.axis_index("x"), lax.axis_index("core")
    y, z = lax.axis_index("seq"), lax.axis_index("fsdp")
    r = 2 * x + c
    ids = jnp.stack([r, y, z]).astype(jnp.int32)
    swap = [(0, 1), (1, 0)]

    def core(v):
        return lax.ppermute(v, "core", swap)

    def across(v):
        return lax.ppermute(v, "x", swap)

    def near(v):
        return lax.ppermute(v, "seq", swap)

    def shift(v, k):
        return lax.ppermute(v, "fsdp", [(i, (i + k) % n) for i in range(n)])

    def scatter_rows(outs):
        if len(outs) == 1:
            value = lax.psum_scatter(outs[0], "fsdp", scatter_dimension=0, tiled=True)
        else:
            value = outs[0]
            for k in range(1, n):
                value = value + shift(outs[k], k).astype(F32)
        return value.astype(BF)

    clock = [ids]

    def tick(*values):
        clock[0] = lax.optimization_barrier((ids, *values))[0]

    def run(body, ins, specs, outs, scratch, name):
        results = call(body, [clock[0], *ins], [SM] + specs, outs, scratch, name)
        tick(results[0])
        return results

    pad = ((0, rows - real), (0, 0))
    tok = jnp.pad(tokens[0], pad)
    tok_near = near(tok)
    positions = y * real + jnp.arange(real)
    keep = slot_mask.astype(F32)[0] * (positions < IMG_TOK).astype(F32)
    keep = keep[:, None]
    grads = jnp.pad((cotangent[0].astype(F32) * keep).astype(BF), pad)
    grads_near = near(after(grads, tok_near))

    sems = lambda c: pltpu.SemaphoreType.DMA((c,))
    few = hidden // wide
    shift_rows = fc1_bias.reshape(few, wide // n)
    quarter = part_hidden // 4
    own_rows = wide // n

    def both_cores(v):
        return [v, core(v)]

    if direct:
        q = lambda ids: ids[1] * 4 + ids[0]
        blocks = [(w_qkv, (own_rows, LANES), lambda ids, k=k: (0, k * 8 + q(ids))) for k in range(3)]
        blocks += [(w_out, (own_rows, wide // 4), lambda ids: (0, ids[0]))]
        blocks += [(v, v.shape, lambda ids: (0, 0)) for v in (ln_gains, biases, shift_rows)]
        across_lanes = OUT_LANE + wide // 4
        (qkv_piece,) = cast(
            cast_qkv_kernel,
            ids,
            blocks,
            [shape((own_rows + 16, across_lanes), BF)],
            [pltpu.VMEM((16, across_lanes), F32)],
            "cast_qkv",
        )
        tick(qkv_piece)
        blocks = [(w_fc1, (own_rows, LANES), lambda ids, k=k: (0, k * 8 + q(ids))) for k in range(n)]
        blocks += [(w_fc2, (h, wide), lambda ids: (q(ids), 0))]
        one_piece, two_piece = cast(
            functools.partial(cast_rest_kernel, n),
            clock[0],
            blocks,
            [shape((own_rows, quarter), BF), shape((h, wide), BF)],
            [],
            "cast_rest",
        )
        tick(one_piece)

        def over_z(piece, before=None, gate=()):
            parts = [piece]
            for k in range(1, n):
                ready = piece if before is None else after(piece, before[k], *gate)
                parts.append(shift(ready, k))
            return parts

        def over_x(parts, own, *gates):
            others = [own]
            for k in range(1, n):
                gate = gates[min(k, len(gates)) - 1] if gates else ()
                others.append(across(after(parts[k], *gate)))
            return others

        def stack(parts, others, name, more=()):
            dims = (2 * n, parts[0].shape[0] - (16 if more else 0), parts[0].shape[1])
            whole, *rest = run(
                functools.partial(stack_kernel, n),
                parts + others,
                [VM] * (2 * n),
                [shape(dims, BF), *more],
                [],
                name,
            )
            return both_cores(whole.reshape(dims[0] * dims[1], dims[2])), rest

        qkv_parts = over_z(qkv_piece)
        qkv_own = across(qkv_piece)
        one_own, two_own = across(one_piece), across(two_piece)
        one_parts = over_z(one_piece, qkv_parts)
        all_qkv, (vec,) = stack(
            qkv_parts,
            over_x(qkv_parts, qkv_own, (), (), (tok_near,)),
            "stack_qkv",
            [shape((16, wide), F32)],
        )
    else:
        cut = lambda v, start, size, axis: lax.dynamic_slice_in_dim(v, start, size, axis).astype(BF)
        qkv_piece = jnp.concatenate(
            [cut(w_qkv, k * wide + y * half + r * LANES, LANES, 1) for k in range(3)]
            + [cut(w_out, r * (wide // 4), wide // 4, 1)],
            axis=1,
        )
        grid = w_fc1.reshape(w_fc1.shape[0], n, 8, h)
        one_piece = cut(grid, y * 4 + r, 1, 2).reshape(w_fc1.shape[0], n * h)
        two_piece = cut(w_fc2, (y * 4 + r) * h, h, 0)

        def whole(v):
            v = lax.all_gather(v, "fsdp", axis=0, tiled=True)
            return both_cores(jnp.concatenate([v, across(v)], axis=0))

        all_qkv, all_one, all_two = map(whole, (qkv_piece, one_piece, two_piece))
        small = jnp.concatenate([ln_gains, biases, shift_rows], axis=0).astype(BF)
        vec = lax.all_gather(small, "fsdp", axis=0).astype(F32).transpose(1, 0, 2)
        vec = jnp.pad(vec.reshape(-1, wide), ((0, 4), (0, 0)))

    two = 2 * rows
    normed, queries, keys, values = run(
        qkv_kernel,
        [tok, tok_near, vec, *all_qkv],
        [VM] * 3 + [ANY] * 2,
        [shape((two, wide), BF)] + [shape((two, half), BF)] * 3,
        [pltpu.VMEM((wide, 3 * half), BF), sems(4)],
        "qkv",
    )
    hidden_shift = vec[8:12].reshape(few, n, wide // n).transpose(1, 0, 2).reshape(n, 2, 4, h)
    hidden_shift = lax.dynamic_index_in_dim(hidden_shift, y, axis=1, keepdims=False)
    hidden_shift = hidden_shift.transpose(1, 0, 2).reshape(1, part_hidden)
    normed_far = core(normed)
    saved = (queries, keys, values)
    mixed_own, mixed_send, totals = attend(clock[0], *saved, rows, real)
    mixed_parts = (mixed_own, mixed_send)
    tick(mixed_own)
    if direct:
        mixed_send = after(mixed_send, grads_near, *one_parts[1:])
        two_parts = over_z(two_piece, qkv_parts, [normed])
    mixed_recv = near(mixed_send)
    grads_far, grads_near_far = core(grads), core(grads_near)
    mixed, middle, normed_two = run(
        project_kernel,
        [tok, mixed_own, mixed_recv, vec, *all_qkv],
        [VM] * 4 + [ANY] * 2,
        [shape((rows, wide), BF), shape((rows, wide), F32), shape((rows, wide), BF)],
        [pltpu.VMEM((wide, wide), BF), sems(4)],
        "project",
    )
    if direct:
        one_others = over_x(one_parts, one_own, (mixed_own,))
        normed_two_near = near(after(normed_two, *one_others))
    else:
        normed_two_near = near(normed_two)
    if direct:
        all_one, _ = stack(one_parts, one_others, "stack_one")
        tick(normed_two_near)
        all_two, _ = stack(two_parts, over_x(two_parts, two_own, (mixed,)), "stack_two")
    act_near, act_far, gtwo_own, gtwo_send, hidden_sums = run(
        mlp_kernel,
        [normed_two, normed_two_near, grads, grads_near, hidden_shift, *all_one, *all_two],
        [VM] * 5 + [ANY] * 4,
        [
            shape((two, 4 * quarter), BF),
            shape((two, 4 * quarter + wide), BF),
            shape((rows, wide), F32),
            shape((rows, wide), BF),
            shape((1, part_hidden), F32),
        ],
        [
            pltpu.VMEM((wide, part_hidden), BF),
            pltpu.VMEM((part_hidden, wide), BF),
            pltpu.VMEM((two, wide), BF),
            pltpu.VMEM((two, wide), BF),
            pltpu.VMEM((two, wide), F32),
            sems(8),
        ],
        "mlp",
    )
    gtwo_recv = near(gtwo_send)
    act_other = core(act_far)
    mixed_far = core(mixed)

    def spread(part):
        pair = jnp.stack([part, near(part)])
        return pair, across(pair)

    def land(pairs, dims, kind):
        pairs = [pairs[0], core(pairs[0]), pairs[1], core(pairs[1])]
        if direct:
            return place(ids, pairs, dims, kind)
        stack = jnp.stack(pairs, axis=1).reshape((8,) + pairs[0].shape[1:])
        order = (jnp.bitwise_xor(jnp.arange(2), y) * 4)[:, None]
        order = (order + jnp.bitwise_xor(jnp.arange(4), r)[None, :]).reshape(-1)
        stack = jnp.take(stack, order, axis=0).astype(F32)
        if kind == "rows":
            return stack.reshape(dims)
        groups = dims[1] // (8 * (h if kind == "hidden" else LANES))
        stack = stack.reshape(8, dims[0], groups, -1)
        return stack.transpose(1, 2, 0, 3).reshape(dims)

    blocks = n if direct else 1

    def grad(left, right, name, extra=()):
        values = weight_grad(clock[0], left, right, name, extra, blocks if extra else 1)
        tick(values[0])
        return values if extra else values[0]

    all_grads = [(a, None) for a in (grads, grads_near, grads_far, grads_near_far)]
    one_left = [
        (normed_two, None),
        (normed_two_near, None),
        (act_other, (4 * quarter, wide)),
    ]

    def unit(slot):
        return [(act_near, (slot * quarter, quarter)), (act_other, (slot * quarter, quarter))]

    two_recv = across(grad(unit(3), all_grads, "grad_fc2_send"))
    one_recv = across(grad(one_left, unit(1), "grad_fc1_send"))
    grad_middle, branch, gmix_own, gmix_send, sums_two = run(
        middle_back_kernel,
        [gtwo_own, gtwo_recv, middle, grads, vec, *all_qkv],
        [VM] * 5 + [ANY] * 2,
        [
            shape((rows, wide), F32),
            shape((rows, wide), BF),
            shape((rows, half), BF),
            shape((rows, half), BF),
            shape((4, wide), F32),
        ],
        [pltpu.VMEM((wide, wide), BF), pltpu.VMEM((rows, wide), BF), sems(4)],
        "middle_back",
    )
    gmix_recv = near(gmix_send)
    branch_far = core(branch)
    result_own, result_send = run(
        result_kernel,
        [act_near, act_far, *all_two],
        [VM] * 2 + [ANY] * 2,
        [shape((rows, wide), F32), shape((rows, wide), BF)],
        [
            pltpu.VMEM((part_hidden, wide), BF),
            pltpu.VMEM((two, wide), F32),
            sems(4),
        ],
        "result",
    )
    result_recv = near(result_send)
    total = middle[:real] + (
        result_own[:real] + result_recv[:real].astype(F32) + vec[7:8, :]
    )
    output = (total * keep).astype(BF)[None]

    gj_far, sums_far = attend_back(
        clock[0], saved, mixed_parts, (gmix_own, gmix_recv), totals, rows, real, 1
    )
    tick(gj_far)
    gj_other = core(gj_far)
    two_part = scatter_rows(grad(unit(2), all_grads, "grad_fc2_keep", [two_recv]))
    gj_near, sums_near = attend_back(
        clock[0], saved, mixed_parts, (gmix_own, gmix_recv), totals, rows, real, 0
    )
    tick(gj_near)
    joined_sums = jnp.concatenate([sums_near, sums_far], axis=0)
    one_part = scatter_rows(grad(one_left, unit(0), "grad_fc1_keep", [one_recv]))
    qkv_left = [(normed, None), (normed_far, None)]
    qkv_recv = across(grad(qkv_left, [(gj_near, 1), (gj_other, 1)], "grad_qkv_send"))
    gone_own, gone_send = run(
        qkv_back_kernel,
        [gj_near, gj_far, *all_qkv],
        [ANY] * 4,
        [shape((rows, wide), F32), shape((rows, wide), BF)],
        [
            pltpu.VMEM((wide, 3 * half), BF),
            pltpu.VMEM((two, 3 * half), BF),
            sems(8),
        ],
        "qkv_back",
    )
    gone_recv = near(gone_send)
    out_send, out_keep = run(
        out_grad_kernel,
        [mixed, mixed_far, branch, branch_far],
        [ANY] * 4,
        [shape((wide, 2 * LANES), BF), shape((wide, 2 * LANES), F32)],
        [pltpu.VMEM((two, wide), BF), pltpu.VMEM((two, 4 * LANES), BF), sems(10)],
        "grad_out",
    )
    out_recv = near(out_send)
    two_pairs = spread(two_part)
    qkv_part = scatter_rows(
        grad(qkv_left, [(gj_near, 0), (gj_other, 0)], "grad_qkv_keep", [qkv_recv])
    )
    tick(one_part)
    grad_tokens, sums_one = run(
        tokens_back_kernel,
        [gone_own, gone_recv, tok, grad_middle, vec],
        [VM] * 5,
        [shape((real, wide), BF), shape((2, wide), F32)],
        [],
        "tokens_back",
    )
    grad_tokens = grad_tokens[None]
    out_sum = out_keep + out_recv.astype(F32)
    out_cross = across(out_sum[:, :LANES].astype(BF))
    kinds = [F32] + [BF] * (blocks - 1) if blocks > 1 else [BF]
    out_part = scatter_rows(
        run(
            combine_kernel,
            [out_sum[:, LANES:], out_cross],
            [VM] * 2,
            [shape((wide // blocks, LANES), kind) for kind in kinds],
            [],
            "combine",
        )
    )
    grad_fc2 = land(two_pairs, w_fc2.shape, "rows")
    grad_fc1 = land(spread(one_part), w_fc1.shape, "hidden")
    grad_out = land(spread(out_part), w_out.shape, "columns")
    grad_qkv = land(spread(qkv_part), w_qkv.shape, "columns")

    wanted = jnp.bitwise_xor(jnp.arange(4), r)
    slots = ((wanted & 1) << 1) | (wanted >> 1)
    chosen = (slots[:, None] == jnp.arange(4)[None, :]).astype(F32)
    joined_sums = jnp.sum(chosen[:, :, None] * joined_sums[None, :, 0, :], axis=1)
    here = (jnp.arange(2) == y).astype(F32)

    def spread_half(row):
        return (here[:, None] * row.reshape(1, half)).reshape(1, wide)

    query_sums = spread_half(joined_sums[:, :LANES])
    value_sums = spread_half(joined_sums[:, 2 * LANES :])
    hidden_sums = hidden_sums.reshape(4, n, h).transpose(1, 0, 2).reshape(n, 1, 4 * h)
    hidden_sums = (hidden_sums * here[None, :, None]).reshape(n, hidden // wide, wide // n)
    rows_of = jnp.concatenate(
        [
            sums_one[0:1],
            sums_two[0:1],
            sums_one[1:2],
            query_sums,
            value_sums,
            sums_two[2:3],
            sums_two[1:2],
            sums_two[3:4],
        ],
        axis=0,
    )
    block = jnp.concatenate(
        [rows_of.reshape(8, n, wide // n).transpose(1, 0, 2), hidden_sums], axis=1
    )
    if direct:
        total = lax.dynamic_index_in_dim(block, z, axis=0, keepdims=False)
        for k in range(1, n):
            part = lax.dynamic_index_in_dim(block, lax.rem(z + k, n), axis=0, keepdims=False)
            total = total + shift(part, k)
        block = total
    else:
        block = lax.psum_scatter(block, "fsdp", scatter_dimension=0)
    block = block + core(block)
    block = block + near(block)
    block = block + across(block)
    return (
        output,
        grad_tokens,
        grad_qkv,
        grad_out,
        grad_fc1,
        grad_fc2,
        block[:2],
        block[2:8],
        block[8:].reshape(-1),
    )


def solution(mesh):
    reps, n, seqs = (mesh.shape[axis] for axis in ("rep", "fsdp", "seq"))
    assert reps == 4 and seqs == 2
    fine = Mesh(mesh.devices.reshape(reps // 2, 2, n, seqs), ("x", "core", "fsdp", "seq"))
    slots = P(("x", "core", "fsdp"), "seq", None)
    first, second = P("fsdp", None), P(None, "fsdp")
    return jax.shard_map(
        functools.partial(on_device, n),
        mesh=fine,
        in_specs=(
            slots,
            P(("x", "core", "fsdp")),
            slots,
            first,
            first,
            first,
            first,
            second,
            second,
            P("fsdp"),
        ),
        out_specs=(slots, slots, first, first, first, first, second, second, P("fsdp")),
        check_vma=False,
    )
```

```python
import functools

import jax
import jax.numpy as jnp
from jax import lax
from jax.experimental import pallas as pl
from jax.experimental.pallas import tpu as pltpu
from jax.sharding import Mesh
from jax.sharding import PartitionSpec as P

HEADS = 16
HEAD_DIM = 64
IMG_TOK = 577
EPSILON = 1e-05
NEGATIVE = -1e30
LANES = 128
BF = jnp.bfloat16
F32 = jnp.float32

ANY = pl.BlockSpec(memory_space=pl.ANY)
VM = pl.BlockSpec(memory_space=pltpu.VMEM)
SM = pl.BlockSpec(memory_space=pltpu.SMEM)

ORDER = (0, 2, 1, 3)
OUT_LANE = 3 * LANES
PEERS = ((0, 0), (1, 0), (0, 2), (1, 2))


def mm(a, b):
    return lax.dot_general(a, b, (((1,), (0,)), ((), ())), preferred_element_type=F32)


def mmt(a, b):
    return lax.dot_general(a, b, (((1,), (1,)), ((), ())), preferred_element_type=F32)


def tmm(a, b):
    return lax.dot_general(a, b, (((0,), (0,)), ((), ())), preferred_element_type=F32)


def normalize(inputs):
    center = inputs - jnp.mean(inputs, axis=-1, keepdims=True)
    inverse = lax.rsqrt(jnp.mean(center * center, axis=-1, keepdims=True) + EPSILON)
    return center * inverse, inverse


def norm_back(grad_in, scaled, inverse, gain_row):
    weighted = grad_in * gain_row
    return inverse * (
        weighted
        - jnp.mean(weighted, axis=-1, keepdims=True)
        - scaled * jnp.mean(weighted * scaled, axis=-1, keepdims=True)
    )


def at(index, size):
    return pl.ds(pl.multiple_of(index * size, size), size)


def flip(r, d):
    return jnp.bitwise_xor(r, d) if d else r


def fetch(copies, sems):
    handles = [pltpu.make_async_copy(s, t, sems.at[i]) for i, (s, t) in enumerate(copies)]
    for handle in handles:
        handle.start()
    return handles


def finish(handles):
    for handle in handles:
        handle.wait()


KNOBS = {"places": 1, "factor": 1.0, "floor": 8.0, "gnear": 1, "n2": 0, "x2": 0, "place": 0.3, "grad_out": 1.0, "ago": 0, "a1": 1, "a3": 0}
TIMES = {
    "qkv": 7.7, "attend": 11.3, "project": 4.9, "mlp": 18.6, "grad_fc2": 6.9,
    "middle_back": 5.4, "grad_fc1_send": 5.9, "grad_out": 4.9, "attend_back": 16.9,
    "grad_qkv_send": 5.7, "qkv_back": 7.1, "grad_fc1_keep": 5.7, "grad_qkv_keep": 5.3,
    "tokens_back": 3.8, "combine": 2.1, "small": 1.5, "place": 3.2, "stack_qkv": 3.4,
    "stack_rest": 4.5, "cast_qkv": 2.7, "cast_rest": 2.7,
}


def on(name, default=1):
    return KNOBS.get(name, default)


def cost(name):
    value = max(TIMES[name], KNOBS.get("floor", 0.0)) * KNOBS.get("factor", 0.25)
    flops = int(value * KNOBS.get(name, 1.0) * 1.15e9)
    return pl.CostEstimate(flops=flops, bytes_accessed=1 << 18, transcendentals=0)


def skipping(body, count, extra):
    def kernel(*refs):
        body(*refs[:count], *refs[count + extra :])

    return kernel if extra else body


def call(body, ins, specs, outs, scratch, name, out_specs=None, first=()):
    return pl.pallas_call(
        skipping(body, len(ins), len(first)),
        out_shape=outs,
        in_specs=specs + [ANY] * len(first),
        out_specs=out_specs or [VM] * len(outs),
        scratch_shapes=scratch,
        compiler_params=pltpu.CompilerParams(vmem_limit_bytes=56 << 20),
        cost_estimate=cost(name),
        name=name,
    )(*ins, *first)


def grid_call(body, ids, ins, specs, outs, out_specs, steps, name, scratch=(), first=()):
    return pl.pallas_call(
        skipping(body, len(ins) + 1, len(first)),
        grid_spec=pltpu.PrefetchScalarGridSpec(
            num_scalar_prefetch=1,
            grid=(steps,),
            in_specs=specs + [ANY] * len(first),
            out_specs=out_specs,
            scratch_shapes=list(scratch),
        ),
        out_shape=outs,
        compiler_params=pltpu.CompilerParams(vmem_limit_bytes=56 << 20),
        cost_estimate=cost(name),
        name=name,
    )(ids, *ins, *first)


def shape(dims, dtype):
    return jax.ShapeDtypeStruct(dims, dtype)


def column_copies(refs, w, ids, lane=0, relative=False):
    rows, q = w.shape[0], w.shape[1] // 4
    copies = []
    for d in range(4):
        slot = pl.ds(ORDER.index(d) * q, q) if relative else at(flip(ids[0], d), q)
        source = refs[d & 1].at[pl.ds((d >> 1) * rows, rows), pl.ds(lane, q)]
        copies.append((source, w.at[:, slot]))
    return copies


def rest_copies(refs, w1, w2, ids, n, sems):
    rows, wide = w1.shape[0], w1.shape[1] // 4
    half, h = w2.shape[1] // 2, w2.shape[0] // (4 * n)
    for d in range(4):
        q = flip(ids[0], d)
        x = jnp.bitwise_xor(ids[0] >> 1, d >> 1)
        source = refs[d & 1].at[at(x, rows), pl.ds(0, wide)]
        pltpu.make_async_copy(source, w1.at[:, at(q, wide)], sems.at[d]).start()
        for i in range(n):
            for side in range(2):
                first = pl.multiple_of(x * rows + (i * 2 + side) * h, h)
                source = refs[d & 1].at[pl.ds(first, h), pl.ds(wide, half)]
                target = w2.at[at(q * n + i, h), pl.ds(side * half, half)]
                pltpu.make_async_copy(source, target, sems.at[4 + d]).start()


def row_copies(refs, w, ids):
    q = w.shape[0] // 4
    return [
        (refs[d & 1].at[pl.ds((d >> 1) * q, q), :], w.at[at(flip(ids[0], d), q), :])
        for d in range(4)
    ]


def split(refs, *counts):
    refs = list(refs)
    out = []
    for count in counts:
        out.append(refs[:count])
        refs = refs[count:]
    return out + [refs]


def qkv_kernel(ids, own, near, vec, *refs):
    weights, (normed, queries, keys, values), (w, sems) = split(refs, 2, 4)
    handles = fetch(column_copies(weights, w, ids), sems)
    rows = own.shape[0]
    for i, part in enumerate((own, near)):
        scaled, _ = normalize(part[...].astype(F32))
        normed[i * rows : (i + 1) * rows, :] = (scaled * vec[0:1, :] + vec[2:3, :]).astype(BF)
    finish(handles)
    scale = HEAD_DIM ** (-0.5)
    first = ids[1] * (queries.shape[1] // LANES)

    def step(i, carry):
        joined = mm(normed[...], w[:, at(i, 3 * LANES)])
        here = at(i, LANES)
        there = at(first + i, LANES)
        queries[:, here] = ((joined[:, :LANES] + vec[3:4, there]) * scale).astype(BF)
        keys[:, here] = joined[:, LANES : 2 * LANES].astype(BF)
        values[:, here] = (joined[:, 2 * LANES :] + vec[4:5, there]).astype(BF)
        return carry

    lax.fori_loop(0, 4, step, 0)


def valid_keys(ids, rows, real):
    index = lax.broadcasted_iota(jnp.int32, (2 * rows, 1), 0)
    second = (index >= rows).astype(jnp.int32)
    local = index - second * rows
    position = jnp.bitwise_xor(second, ids[1]) * real + local
    return (local < real) & (position < IMG_TOK)


def head_half(value, half):
    lane = lax.broadcasted_iota(jnp.int32, value.shape, 1)
    keep = (lane < HEAD_DIM) if half == 0 else (lane >= HEAD_DIM)
    return jnp.where(keep, value, jnp.zeros_like(value))


def with_lanes(value, half, columns):
    lane = lax.broadcasted_iota(jnp.int32, value.shape, 1)
    out = head_half(value, half)
    for i, column in enumerate(columns):
        out = jnp.where(lane == (1 - half) * HEAD_DIM + i, column, out)
    return out


def three_parts(column):
    high = column.astype(BF)
    rest = column - high.astype(F32)
    middle = rest.astype(BF)
    return [high, middle, (rest - middle.astype(F32)).astype(BF)]


def key_shift(ids, rows, real):
    shift = jnp.where(valid_keys(ids, rows, real), 0.0, NEGATIVE)
    return shift.astype(BF)


def attend_kernel(rows, real, ids, queries, keys, values, mixed_own, mixed_near, totals):
    one = jnp.ones((1, 1), BF)
    shift = key_shift(ids, rows, real)
    keys_of = [with_lanes(keys[...], half, [shift]) for half in range(2)]
    values_of = [head_half(values[...], half) for half in range(2)]
    for i, target in enumerate((mixed_own, mixed_near)):
        block = queries[i * rows : (i + 1) * rows, :]
        total = None
        for half in range(2):
            scores = mmt(keys_of[half], with_lanes(block, half, [one]))
            highest = jnp.max(scores, axis=0, keepdims=True)
            exponent = jnp.exp(scores - highest)
            sums = jnp.sum(exponent, axis=0, keepdims=True)
            totals[2 * half + i : 2 * half + i + 1, :] = highest + jnp.log(sums)
            part = tmm(values_of[half], exponent.astype(BF)) * (1.0 / sums)
            total = part if total is None else total + part
        target[...] = total.T.astype(BF)


def attend(ids, queries, keys, values, rows, real, first):
    wide = queries.shape[1]
    steps = wide // LANES
    block = pl.BlockSpec((2 * rows, LANES), lambda i, ids: (0, i))
    half = pl.BlockSpec((rows, LANES), lambda i, ids: (0, i))
    return grid_call(
        functools.partial(attend_kernel, rows, real),
        ids,
        [queries, keys, values],
        [block] * 3,
        [shape((rows, wide), BF)] * 2 + [shape((steps, 4, rows), F32)],
        [half] * 2 + [pl.BlockSpec((None, 4, rows), lambda i, ids: (i, 0, 0))],
        steps,
        "attend",
        first=first,
    )


def attend_back_kernel(
    rows, real, ids, queries, keys, values, mixed_own, mixed_near, grad_own, grad_near,
    totals, near, far, sums,
):
    step = pl.program_id(0)
    one = jnp.ones((1, 1), BF)
    shift = key_shift(ids, rows, real)
    keys_of = [head_half(keys[...], half) for half in range(2)]
    wide_keys = [with_lanes(keys[...], half, [shift, one, one, one]) for half in range(2)]
    wide_values = [with_lanes(values[...], half, [one, one, one]) for half in range(2)]
    lines = jnp.concatenate([totals[...], jnp.zeros_like(totals[...])], axis=0).T
    grad_k = grad_v = None
    grad_q = []
    for part, (mixed, grad_ref) in enumerate(((mixed_own, grad_own), (mixed_near, grad_near))):
        block = queries[part * rows : (part + 1) * rows, :]
        grad = grad_ref[...]
        product = grad.astype(F32) * mixed[...].astype(F32)
        total = None
        for half in range(2):
            line = three_parts(-lines[:, 2 * half + part : 2 * half + part + 1])
            probs = jnp.exp(mmt(wide_keys[half], with_lanes(block, half, [one, *line])))
            inner = jnp.sum(head_half(product, half), axis=1, keepdims=True)
            wide_grad = with_lanes(grad, half, three_parts(-inner))
            grad_scores = (probs * mmt(wide_values[half], wide_grad)).astype(BF)
            first = tmm(keys_of[half], grad_scores)
            total = first if total is None else total + first
            second = mm(grad_scores, head_half(block, half))
            third = mm(probs.astype(BF), head_half(grad, half))
            grad_k = second if grad_k is None else grad_k + second
            grad_v = third if grad_v is None else grad_v + third
        grad_q.append(total.T)
    scale = HEAD_DIM ** (-0.5)
    grad_q = jnp.concatenate(grad_q, axis=0).astype(BF).astype(F32) * scale
    pieces = [grad_q.astype(BF), grad_k.astype(BF), grad_v.astype(BF)]
    for kind, piece in enumerate(pieces):
        columns = slice(kind * LANES, (kind + 1) * LANES)
        sums[:, columns] = jnp.sum(piece.astype(F32), axis=0, keepdims=True)

        @pl.when(step < 2)
        def _():
            near[:, columns] = piece

        @pl.when(step >= 2)
        def _():
            far[:, columns] = piece


def attend_back(ids, saved, mixed, grads, totals, rows, real, first):
    def index(i, ids):
        return jnp.bitwise_xor(ids[0], ((i & 1) << 1) | (i >> 1))

    block = pl.BlockSpec((2 * rows, LANES), lambda i, ids: (0, index(i, ids)))
    half = pl.BlockSpec((rows, LANES), lambda i, ids: (0, index(i, ids)))
    lines = pl.BlockSpec((None, 4, rows), lambda i, ids: (index(i, ids), 0, 0))
    line = pl.BlockSpec((None, 1, 3 * LANES), lambda i, ids: (i, 0, 0))
    pair = (2, 2 * rows, 3 * LANES)
    near = pl.BlockSpec((None,) + pair[1:], lambda i, ids: (jnp.minimum(i, 1), 0, 0))
    far = pl.BlockSpec((None,) + pair[1:], lambda i, ids: (jnp.maximum(i - 2, 0), 0, 0))
    return grid_call(
        functools.partial(attend_back_kernel, rows, real),
        ids,
        [*saved, *mixed, *grads, totals],
        [block] * 3 + [half] * 4 + [lines],
        [shape(pair, BF), shape(pair, BF), shape((4, 1, 3 * LANES), F32)],
        [near, far, line],
        4,
        "attend_back",
        first=first,
    )


def project_kernel(ids, tokens, mixed_own, mixed_near, vec, *refs):
    weights, (mixed, middle, normed), (w, sems) = split(refs, 2, 3)
    handles = fetch(column_copies(weights, w, ids, OUT_LANE), sems)
    y = ids[1]
    half = mixed_own.shape[1]
    mixed[:, at(y, half)] = mixed_own[...]
    mixed[:, at(1 - y, half)] = mixed_near[...]
    finish(handles)
    total = tokens[...].astype(F32) + (mm(mixed[...], w[...]) + vec[5:6, :])
    middle[...] = total
    scaled, _ = normalize(total)
    normed[...] = (scaled * vec[1:2, :] + vec[6:7, :]).astype(BF)


def mlp_kernel(n, joint, ids, n_own, n_near, g_own, g_near, fb, *refs):
    ones, twos, outs, scratch = split(refs, 2, 0 if joint else 2, 7)
    near, far, grad_own, grad_near, result_own, result_near, sums = outs
    w1, w2, normed, grads, total, result, stage, sems, out_sems = scratch
    r = ids[0]
    rows = n_own.shape[0]
    if joint:
        rest_copies(ones, w1, w2, ids, n, sems)
    else:
        fetch(column_copies(ones, w1, ids) + row_copies(twos, w2, ids), sems)
    normed[:rows, :] = n_own[...]
    normed[rows:, :] = n_near[...]
    wide = w1.shape[1] // 4
    grads[:rows, :] = g_own[...]
    grads[rows:, :] = g_near[...]
    total[...] = jnp.zeros_like(total)
    result[...] = jnp.zeros_like(result)

    def out_copy(target, d, kind):
        place = at(2 * kind + (d >> 1), wide)
        return pltpu.make_async_copy(
            stage.at[2 * d + kind], target.at[:, place], out_sems.at[2 * d + kind]
        )

    def step(d, carry):
        here = at(jnp.bitwise_xor(r, d), wide)
        pltpu.make_async_copy(w1.at[:, here], w1.at[:, here], sems.at[d]).wait()
        pltpu.make_async_copy(w2.at[here, :], w2.at[here, :], sems.at[4 + d]).wait()
        hidden = mm(normed[...], w1[:, here]) + fb[:, here]
        gate = 1.0 / (1.0 + jnp.exp(-1.702 * hidden))
        active = (hidden * gate).astype(BF)
        stage[2 * d + 1] = active
        result[...] += mm(active, w2[here, :])
        grad_active = mmt(grads[...], w2[here, :])
        grad_hidden = (
            grad_active * (gate + 1.702 * hidden * gate * (1.0 - gate))
        ).astype(BF)
        stage[2 * d] = grad_hidden
        sums[:, here] = jnp.sum(grad_hidden.astype(F32), axis=0, keepdims=True)
        total[...] += mmt(grad_hidden, w1[:, here])
        for kind in range(2):

            @pl.when((d & 1) == 0)
            def _():
                out_copy(near, d, kind).start()

            @pl.when((d & 1) == 1)
            def _():
                out_copy(far, d, kind).start()

        return carry

    lax.fori_loop(0, 4, step, 0)
    grad_own[...] = total[:rows, :]
    grad_near[...] = total[rows:, :].astype(BF)
    result_own[...] = result[:rows, :]
    result_near[...] = result[rows:, :].astype(BF)
    for d in range(4):
        for kind in range(2):
            out_copy(far if d & 1 else near, d, kind).wait()


def middle_back_kernel(ids, grad_own, grad_recv, middle, incoming, vec, *refs):
    weights, outs, (w, work, sems) = split(refs, 2, 5)
    grad_middle, branch, mixed_own, mixed_near, sums = outs
    handles = fetch(column_copies(weights, w, ids, OUT_LANE), sems)
    y = ids[1]
    grad = grad_own[...] + grad_recv[...].astype(F32)
    scaled, inverse = normalize(middle[...])
    sums[0:1, :] = jnp.sum(grad * scaled, axis=0, keepdims=True)
    sums[1:2, :] = jnp.sum(grad, axis=0, keepdims=True)
    arriving = incoming[...].astype(F32)
    sums[3:4, :] = jnp.sum(arriving, axis=0, keepdims=True)
    total = arriving + norm_back(grad, scaled, inverse, vec[1:2, :])
    grad_middle[...] = total
    low = total.astype(BF)
    branch[...] = low
    sums[2:3, :] = jnp.sum(low.astype(F32), axis=0, keepdims=True)
    finish(handles)
    work[...] = mmt(branch[...], w[...]).astype(BF)
    half = work.shape[1] // 2
    mixed_own[...] = work[:, at(y, half)]
    mixed_near[...] = work[:, at(1 - y, half)]


def qkv_back_kernel(ids, near, far, *refs):
    weights, (own, other), (w, grads, sems) = split(refs, 2, 2)
    wide = near.shape[2]
    copies = column_copies(weights, w, ids, relative=True)
    for s in range(4):
        source = (near if s < 2 else far).at[s % 2]
        copies.append((source, grads.at[:, pl.ds(s * wide, wide)]))
    finish(fetch(copies, sems))
    rows = own.shape[0]
    step_rows = 256

    def step(i, carry):
        here = at(i, step_rows)
        value = mmt(grads[...], w[here, :])
        own[:, here] = value[:rows, :]
        other[:, here] = value[rows:, :].astype(BF)
        return carry

    lax.fori_loop(0, w.shape[0] // step_rows, step, 0)


def tokens_back_kernel(ids, grad_own, grad_recv, tokens, grad_middle, vec, out, sums):
    grad = grad_own[...] + grad_recv[...].astype(F32)
    scaled, inverse = normalize(tokens[...].astype(F32))
    sums[0:1, :] = jnp.sum(grad * scaled, axis=0, keepdims=True)
    sums[1:2, :] = jnp.sum(grad, axis=0, keepdims=True)
    total = grad_middle[...] + norm_back(grad, scaled, inverse, vec[0:1, :])
    out[...] = total.astype(BF)[: out.shape[0], :]


def window(ref, pick):
    if pick is None:
        return ref
    if len(ref.shape) == 3:
        return ref.at[pick]
    return ref.at[:, pl.ds(*pick)]


def extent(array, pick):
    if pick is None:
        return array.shape
    if array.ndim == 3:
        return array.shape[1:]
    return (array.shape[0], pick[1])


def weight_kernel(left_picks, right_picks, more, slots, ids, *refs):
    left_refs, right_refs, extra, rest = split(refs, len(left_picks), len(right_picks), more)
    *outs, a, b, sems = rest
    copies = []
    for parts, target, picks in ((left_refs, a, left_picks), (right_refs, b, right_picks)):
        start = 0
        for part, pick in zip(parts, picks):
            source = window(part, pick)
            count = source.shape[0]
            copies.append((source, target.at[pl.ds(start, count), :]))
            start += count
    finish(fetch(copies, sems))
    if len(outs) == 1 and slots > 1:
        size = outs[0].shape[0] // 4
        for i in range(4):
            block = jnp.bitwise_xor(ids[0] >> 1, i // 2) * 2 + i % 2
            value = tmm(a[:, i * size : (i + 1) * size], b[...])
            outs[0][at(block, size), :] = value.astype(outs[0].dtype)
        return
    if len(outs) > 1:
        rows = outs[0].shape[0]
        for k, out in enumerate(outs):
            for slot in range(slots):
                size = rows // slots
                here = at(slot * len(outs) + lax.rem(ids[2] + k, len(outs)), size)
                value = tmm(a[:, here], b[...])
                if more:
                    value = value + extra[0][here, :].astype(F32)
                out[slot * size : (slot + 1) * size, :] = value.astype(out.dtype)
        return
    (out,) = outs
    step_rows = 256

    def step(i, carry):
        here = at(i, step_rows)
        value = tmm(a[:, here], b[...])
        if more:
            value = value + extra[0][here, :].astype(F32)
        out[here, :] = value.astype(out.dtype)
        return carry

    lax.fori_loop(0, out.shape[0] // step_rows, step, 0)


def weight_grad(ids, left, right, name, extra=(), blocks=1, slots=1, first=()):
    def span(parts):
        dims = [extent(*p) for p in parts]
        return sum(d[0] for d in dims), dims[0][1]

    depth, rows = span(left)
    _, columns = span(right)
    kinds = [F32] + [BF] * (blocks - 1) if blocks > 1 else [BF]
    return call(
        functools.partial(
            weight_kernel, [p for _, p in left], [p for _, p in right], len(extra), slots
        ),
        [ids] + [a for a, _ in left] + [a for a, _ in right] + list(extra),
        [SM] + [ANY] * (len(left) + len(right)) + [VM] * len(extra),
        [shape((rows // blocks, columns), kind) for kind in kinds],
        [
            pltpu.VMEM((depth, rows), BF),
            pltpu.VMEM((depth, columns), BF),
            pltpu.SemaphoreType.DMA((len(left) + len(right),)),
        ],
        name,
        first=first,
    )


def out_grad_kernel(ids, mixed, mixed_far, branch, branch_far, *refs):
    *outs, a, b, sems = refs
    r, y = ids[0], ids[1]
    rows = mixed.shape[0]
    quarters = branch.shape[1] // 2 // LANES
    copies = []
    for i, (left, right) in enumerate(((mixed, branch), (mixed_far, branch_far))):
        here = pl.ds(i * rows, rows)
        copies.append((left, a.at[here, :]))
        for s, (dy, d) in enumerate(PEERS):
            block = flip(y, dy) * quarters + flip(r, d)
            copies.append((right.at[:, at(block, LANES)], b.at[here, pl.ds(s * LANES, LANES)]))
    finish(fetch(copies, sems))
    step_rows = 256

    def step(i, carry):
        here = at(i, step_rows)
        value = tmm(a[:, here], b[...])
        for s, out in enumerate(outs):
            out[here, :] = value[:, s * LANES : (s + 1) * LANES].astype(out.dtype)
        return carry

    lax.fori_loop(0, a.shape[1] // step_rows, step, 0)


def combine_kernel(ids, keep, *refs):
    recvs, outs = refs[:3], refs[3:]
    rows = outs[0].shape[0]
    for k, out in enumerate(outs):
        here = at(lax.rem(ids[2] + k, len(outs)), rows)
        value = keep[here, :]
        for recv in recvs:
            value = value + recv[here, :].astype(F32)
        out[...] = value.astype(out.dtype)


def join(parts):
    return parts[0] if len(parts) == 1 else jnp.concatenate(parts, axis=1)


def cast_qkv_kernel(ids, first, second, third, fourth, gains, biases, shift, out, low):
    rows = first.shape[0]
    out[:rows, :] = join([part[...].astype(BF) for part in (first, second, third, fourth)])
    low[...] = jnp.zeros_like(low)
    width = gains.shape[1]
    low[0:2, :width] = gains[...]
    low[2:8, :width] = biases[...]
    low[8:12, :width] = shift[...]
    out[rows:, :] = low[...].astype(BF)


def cast_rest_kernel(n, ids, *refs):
    ones, (two_part,), (out,) = split(refs, n, 1)
    wide = out.shape[1] // 2
    rows = two_part.shape[0]
    out[:, :wide] = join([part[...].astype(BF) for part in ones])
    out[:rows, wide:] = two_part[:, :wide].astype(BF)
    out[rows:, wide:] = two_part[:, wide:].astype(BF)


def cast(body, ids, blocks, outs, scratch, name, first=()):
    return grid_call(
        body,
        ids,
        [array for array, _, _ in blocks],
        [pl.BlockSpec(block, lambda i, ids, at=at: at(ids)) for _, block, at in blocks],
        outs,
        [pl.BlockSpec(o.shape, lambda i, ids: (0, 0)) for o in outs],
        1,
        name,
        scratch,
        first,
    )


def stack_kernel(n, ids, *refs):
    parts, (out, low) = split(refs, 2 * n)[0], refs[2 * n :]
    rows = out.shape[1]
    width = low.shape[1] // n
    for i, part in enumerate(parts):
        there = lax.rem(ids[2] - i % n + n, n)
        out[(i // n) * n + there] = part[:rows, :]
        if i < n:
            low[:, at(there, width)] = part[rows:, :width].astype(F32)


def stack_rest_kernel(n, ids, *refs):
    parts, (one, two) = split(refs, 2 * n)[0], refs[2 * n :]
    wide, rows = one.shape[2], two.shape[1]
    for i, part in enumerate(parts):
        there = (i // n) * n + lax.rem(ids[2] - i % n + n, n)
        one[there] = part[:, :wide]
        two[there, :, :wide] = part[:rows, wide:]
        two[there, :, wide:] = part[rows:, wide:]


def place_kernel(kind, ids, *refs):
    sources, (out,), _ = split(refs, 8, 1)
    for i, source in enumerate(sources):
        dy, d = PEERS[i % 4]
        block = flip(ids[1], dy) * 4 + flip(ids[0], d + i // 4)
        piece = source[...].astype(F32)
        if kind == "rows":
            out[at(block, piece.shape[0]), :] = piece
            continue
        for g in range(piece.shape[1] // LANES):
            columns = at(block + g * 8, LANES)
            out[:, columns] = piece[:, g * LANES : (g + 1) * LANES]


def place(ids, sources, dims, kind, first):
    rows, columns = sources[0].shape
    steps = 4
    if kind == "rows":
        inside = pl.BlockSpec((rows, columns // steps), lambda i, ids: (0, i))
        outside = pl.BlockSpec((dims[0], dims[1] // steps), lambda i, ids: (0, i))
    else:
        inside = pl.BlockSpec((rows // steps, columns), lambda i, ids: (i, 0))
        outside = pl.BlockSpec((dims[0] // steps, dims[1]), lambda i, ids: (i, 0))
    return grid_call(
        functools.partial(place_kernel, kind),
        ids,
        sources,
        [inside] * 8,
        [shape(dims, F32)],
        [outside],
        steps,
        "place",
        first=first,
    )[0]


def small_kernel(ids, one, two, joined, hidden, *refs):
    *outs, full = refs
    r, y, z = ids[0], ids[1], ids[2]
    n, width = full.shape[0], full.shape[2]
    full[...] = jnp.zeros_like(full)
    for row, (source, line) in {
        0: (one, 0), 1: (two, 0), 2: (one, 1), 5: (two, 2), 6: (two, 1), 7: (two, 3),
    }.items():
        for i in range(n):
            full[i, row : row + 1, :] = source[line : line + 1, i * width : (i + 1) * width]
    slots = [joined[slot] for slot in range(4)]
    for q in range(4):
        value = sum(
            jnp.where(jnp.bitwise_xor(r, d) == q, slots[slot], 0.0) for slot, d in enumerate(ORDER)
        )
        here = slice((q % 2) * LANES, (q % 2 + 1) * LANES)
        for half in range(2):
            mine = jnp.where(y == half, 1.0, 0.0)
            for row, kind in ((3, 0), (4, 2)):
                line = value[:, kind * LANES : (kind + 1) * LANES]
                full[2 * half + q // 2, row : row + 1, here] = line * mine
            row = 8 + 2 * half + q // 2
            for i in range(n):
                line = hidden[:, (q * n + i) * LANES : (q * n + i + 1) * LANES]
                full[i, row : row + 1, here] = line * mine
    for k, out in enumerate(outs):
        out[...] = full[lax.rem(z + k, n)]


def on_device(n, tokens, slot_mask, cotangent, w_qkv, w_out, w_fc1, w_fc2, ln_gains, biases, fc1_bias):
    slot_count, real, wide = tokens.shape
    assert slot_count == 1
    direct = n == 4
    joint = direct and bool(on("scf"))
    whole_two = direct and bool(on("sc2"))
    rows = -(-real // 16) * 16
    hidden = fc1_bias.shape[0] * n
    half, part_hidden = wide // 2, hidden // 2
    h = hidden // n // 8
    x, c = lax.axis_index("x"), lax.axis_index("core")
    y, z = lax.axis_index("seq"), lax.axis_index("fsdp")
    r = 2 * x + c
    ids = jnp.stack([r, y, z]).astype(jnp.int32)
    swap = [(0, 1), (1, 0)]

    def core(v):
        return lax.ppermute(v, "core", swap)

    def across(v):
        return lax.ppermute(v, "x", swap)

    def near(v):
        return lax.ppermute(v, "seq", swap)

    def diagonal(v):
        return lax.ppermute(v, ("x", "seq"), [(i, i ^ 3) for i in range(4)])

    def shift(v, k):
        return lax.ppermute(v, "fsdp", [(i, (i + k) % n) for i in range(n)])

    def scatter_rows(outs, *gate):
        if len(outs) == 1:
            value = lax.psum_scatter(outs[0], "fsdp", scatter_dimension=0, tiled=True).astype(F32)
        else:
            moved = [shift(outs[k], k) for k in range(1, n)]
            value = after("sums", outs[0], *gate) if gate else outs[0]
            for part in moved:
                value = value + part.astype(F32)
        return value

    waiting = []

    def tick(name, *values):
        if on(name):
            waiting.extend(values)

    def take():
        values = tuple(waiting) if direct else ()
        waiting.clear()
        return values

    def after(name, value, *others):
        if not direct or not others or not on(name):
            return value
        value, *others = lax.optimization_barrier((value, *others))
        waiting.extend(others)
        return value

    def run(body, ins, specs, outs, scratch, name, out_specs=None):
        results = call(
            body, [ids, *ins], [SM] + specs, outs, scratch, name, out_specs, take()
        )
        tick("chain", results[0])
        return results

    def make_rows():
        pad = ((0, rows - real), (0, 0))
        tok = jnp.pad(tokens[0], pad)
        tok_near = near(tok)
        positions = y * real + jnp.arange(real)
        keep = slot_mask.astype(F32)[0] * (positions < IMG_TOK).astype(F32)
        keep = keep[:, None]
        grads = jnp.pad((cotangent[0].astype(F32) * keep).astype(BF), pad)
        grads_near = near(grads)
        return tok, tok_near, keep, grads, grads_near

    sems = lambda c: pltpu.SemaphoreType.DMA((c,))
    few = hidden // wide
    shift_rows = fc1_bias.reshape(few, wide // n)
    quarter = part_hidden // 4
    own_rows = wide // n

    def both_cores(v):
        return [v, core(v)]

    if direct:
        q = lambda ids: ids[1] * 4 + ids[0]
        blocks = [(w_qkv, (own_rows, LANES), lambda ids, k=k: (0, k * 8 + q(ids))) for k in range(3)]
        blocks += [(w_out, (own_rows, wide // 4), lambda ids: (0, ids[0]))]
        blocks += [(v, v.shape, lambda ids: (0, 0)) for v in (ln_gains, biases, shift_rows)]
        across_lanes = OUT_LANE + wide // 4
        (qkv_piece,) = cast(
            cast_qkv_kernel,
            ids,
            blocks,
            [shape((own_rows + 16, across_lanes), BF)],
            [pltpu.VMEM((16, across_lanes), F32)],
            "cast_qkv",
            take(),
        )
        tick("c_cast", qkv_piece)
        qkv_own = across(qkv_piece)
        tok, tok_near, keep, grads, grads_near = make_rows()
        blocks = [(w_fc1, (own_rows, LANES), lambda ids, k=k: (0, k * 8 + q(ids))) for k in range(n)]
        blocks += [(w_fc2, (h, wide), lambda ids: (q(ids), 0))]
        def over_z(piece, before=None, gate=()):
            parts = [piece]
            for k in range(1, n):
                ready = piece if before is None else after("zf", piece, before[k], *gate)
                parts.append(shift(ready, k))
            return parts

        qkv_parts = over_z(qkv_piece)
        tick("a1", qkv_parts[1])
        tick("a3", *qkv_parts[2:])
        (rest_piece,) = cast(
            functools.partial(cast_rest_kernel, n),
            ids,
            blocks,
            [shape((own_rows, 2 * quarter), BF)],
            [],
            "cast_rest",
            first=take(),
        )
        tick("c_rest", rest_piece)

        def over_x(parts, own, *gates):
            others = [own]
            for k in range(1, n):
                gate = gates[min(k, len(gates)) - 1] if gates else ()
                others.append(across(after("xf", parts[k], *gate)))
            return others

        def stack(body, parts, others, outs, name):
            values = run(
                functools.partial(body, n),
                parts + others,
                [VM] * (2 * n),
                outs,
                [],
                name,
            )
            flat = [v.reshape(-1, v.shape[2]) if v.ndim == 3 else v for v in values]
            return flat

        if joint:
            rest_all = lax.all_gather(rest_piece, ("x", "fsdp"), axis=0, tiled=True)
        else:
            rest_own = across(rest_piece)
            rest_parts = over_z(rest_piece, qkv_parts)
        tick("tok", tok_near)
        qkv_stack, vec = stack(
            stack_kernel,
            qkv_parts,
            over_x(qkv_parts, qkv_own),
            [shape((2 * n, own_rows, across_lanes), BF), shape((16, wide), F32)],
            "stack_qkv",
        )
        all_qkv = both_cores(qkv_stack)
    else:
        cut = lambda v, start, size, axis: lax.dynamic_slice_in_dim(v, start, size, axis).astype(BF)
        qkv_piece = jnp.concatenate(
            [cut(w_qkv, k * wide + y * half + r * LANES, LANES, 1) for k in range(3)]
            + [cut(w_out, r * (wide // 4), wide // 4, 1)],
            axis=1,
        )
        grid = w_fc1.reshape(w_fc1.shape[0], n, 8, h)
        one_piece = cut(grid, y * 4 + r, 1, 2).reshape(w_fc1.shape[0], n * h)
        two_piece = cut(w_fc2, (y * 4 + r) * h, h, 0)

        def whole(v):
            v = lax.all_gather(v, "fsdp", axis=0, tiled=True)
            return both_cores(jnp.concatenate([v, across(v)], axis=0))

        all_qkv, all_one, all_two = map(whole, (qkv_piece, one_piece, two_piece))
        tok, tok_near, keep, grads, grads_near = make_rows()
        small = jnp.concatenate([ln_gains, biases, shift_rows], axis=0).astype(BF)
        vec = lax.all_gather(small, "fsdp", axis=0).astype(F32).transpose(1, 0, 2)
        vec = jnp.pad(vec.reshape(-1, wide), ((0, 4), (0, 0)))

    two = 2 * rows
    tick("gnear", grads_near)
    normed, queries, keys, values = run(
        qkv_kernel,
        [tok, tok_near, vec, *all_qkv],
        [VM] * 3 + [ANY] * 2,
        [shape((two, wide), BF)] + [shape((two, half), BF)] * 3,
        [pltpu.VMEM((wide, 3 * half), BF), sems(4)],
        "qkv",
    )
    hidden_shift = vec[8:12].reshape(few, n, wide // n).transpose(1, 0, 2).reshape(n, 2, 4, h)
    hidden_shift = lax.dynamic_index_in_dim(hidden_shift, y, axis=1, keepdims=False)
    hidden_shift = hidden_shift.transpose(1, 0, 2).reshape(1, part_hidden)
    normed_far = core(normed)
    saved = (queries, keys, values)
    mixed_own, mixed_send, totals = attend(ids, *saved, rows, real, take())
    mixed_parts = (mixed_own, mixed_send)
    tick("chain", mixed_own)
    mixed_recv = near(mixed_send)
    grads_far, grads_near_far = core(grads), core(grads_near)
    mixed, middle, normed_two = run(
        project_kernel,
        [tok, mixed_own, mixed_recv, vec, *all_qkv],
        [VM] * 4 + [ANY] * 2,
        [shape((rows, wide), BF), shape((rows, wide), F32), shape((rows, wide), BF)],
        [pltpu.VMEM((wide, wide), BF), sems(4)],
        "project",
    )
    normed_two_near = near(normed_two)
    mixed_far, normed_two_far = core(mixed), core(normed_two)
    tick("n2", normed_two_near)
    tick("fars", normed_far, mixed_far, grads_far, grads_near_far, normed_two_far)
    if direct:
        if joint:
            all_one, all_two = both_cores(after("cf", rest_all, normed_two)), []
        else:
            rest_others = over_x(rest_parts, rest_own, (mixed_own,))
            one_stack, two_stack = stack(
                stack_rest_kernel,
                rest_parts,
                rest_others,
                [shape((2 * n, own_rows, quarter), BF), shape((2 * n, h, wide), BF)],
                "stack_rest",
            )
            all_one, all_two = both_cores(one_stack), both_cores(two_stack)
    normed_two_near_far = core(normed_two_near)
    tick("n2f", normed_two_near_far)
    act_near, act_far, gtwo_own, gtwo_send, result_own, result_send, hidden_sums = run(
        functools.partial(mlp_kernel, n, joint),
        [normed_two, normed_two_near, grads, grads_near, hidden_shift, *all_one, *all_two],
        [VM] * 5 + [ANY] * (len(all_one) + len(all_two)),
        [
            shape((two, 4 * quarter), BF),
            shape((two, 4 * quarter), BF),
            shape((rows, wide), F32),
            shape((rows, wide), BF),
            shape((rows, wide), F32),
            shape((rows, wide), BF),
            shape((1, part_hidden), F32),
        ],
        [
            pltpu.VMEM((wide, part_hidden), BF),
            pltpu.VMEM((part_hidden, wide), BF),
            pltpu.VMEM((two, wide), BF),
            pltpu.VMEM((two, wide), BF),
            pltpu.VMEM((two, wide), F32),
            pltpu.VMEM((two, wide), F32),
            pltpu.VMEM((8, two, quarter), BF),
            sems(8),
            sems(8),
        ],
        "mlp",
        [ANY] * 2 + [VM] * 5,
    )
    gtwo_recv = near(gtwo_send)
    act_other = core(act_far)

    def spread(part):
        return [part, near(part), across(part), diagonal(part)]

    def land(parts, dims, kind):
        parts = parts + [core(v) for v in parts]
        if direct:
            value = place(ids, parts, dims, kind, take())
            tick("places", value)
            return value
        order = [flip(y, dy) * 4 + flip(r, d + j) for j in range(2) for dy, d in PEERS]
        stack = jnp.zeros((8,) + parts[0].shape, F32)
        for index, v in zip(order, parts):
            stack = lax.dynamic_update_slice_in_dim(stack, v.astype(F32)[None], index, 0)
        if kind == "rows":
            return stack.reshape(dims)
        groups = dims[1] // (8 * (h if kind == "hidden" else LANES))
        stack = stack.reshape(8, dims[0], groups, -1)
        return stack.transpose(1, 2, 0, 3).reshape(dims)

    blocks = n if direct else 1

    def grad(left, right, name, extra=()):
        values = weight_grad(
            ids, left, right, name, extra, blocks if extra else 1, first=take()
        )
        tick("chain", values[0])
        return values if extra else values[0]

    all_grads = [(a, None) for a in (grads, grads_near, grads_far, grads_near_far)]
    one_left = [
        (a, None) for a in (normed_two, normed_two_near, normed_two_far, normed_two_near_far)
    ]

    def unit(slot):
        return [(act_near, (slot * quarter, quarter)), (act_other, (slot * quarter, quarter))]

    two_left = [(v, (2 * quarter, 2 * quarter)) for v in (act_near, act_other)]
    two_sums = weight_grad(
        ids,
        two_left,
        all_grads,
        "grad_fc2",
        blocks=1 if whole_two else blocks,
        slots=2 if direct else 1,
        first=take(),
    )
    tick("chain", two_sums[0])
    if not direct:
        two_sums = [
            v.reshape(2, n, h, wide).transpose(1, 0, 2, 3).reshape(-1, wide) for v in two_sums
        ]
    grad_middle, branch, gmix_own, gmix_send, sums_two = run(
        middle_back_kernel,
        [gtwo_own, gtwo_recv, middle, grads, vec, *all_qkv],
        [VM] * 5 + [ANY] * 2,
        [
            shape((rows, wide), F32),
            shape((rows, wide), BF),
            shape((rows, half), BF),
            shape((rows, half), BF),
            shape((4, wide), F32),
        ],
        [pltpu.VMEM((wide, wide), BF), pltpu.VMEM((rows, wide), BF), sems(4)],
        "middle_back",
    )
    gmix_recv = near(gmix_send)
    branch_far = core(branch)
    one_recv = across(grad(one_left, unit(1), "grad_fc1_send"))
    out_keep, *out_sends = run(
        out_grad_kernel,
        [mixed, mixed_far, branch, branch_far],
        [ANY] * 4,
        [shape((wide, LANES), F32)] + [shape((wide, LANES), BF)] * 3,
        [pltpu.VMEM((two, wide), BF), pltpu.VMEM((two, 4 * LANES), BF), sems(10)],
        "grad_out",
    )
    gj_near, gj_far, joined_sums = attend_back(
        ids, saved, mixed_parts, (gmix_own, gmix_recv), totals, rows, real, take()
    )
    tick("chain", gj_near)
    gj_other = core(gj_far)
    result_recv = near(result_send)
    total = middle[:real] + (
        result_own[:real] + result_recv[:real].astype(F32) + vec[7:8, :]
    )
    output = (total * keep).astype(BF)[None]
    out_recvs = [near(out_sends[0]), across(out_sends[1]), diagonal(out_sends[2])]
    tick("res", result_recv)
    one_sums = grad(one_left, unit(0), "grad_fc1_keep", [one_recv])
    qkv_left = [(normed, None), (normed_far, None)]
    qkv_send = grad(qkv_left, [(gj_near, 1), (gj_other, 1)], "grad_qkv_send")
    qkv_recv = across(qkv_send)
    gone_own, gone_send = run(
        qkv_back_kernel,
        [gj_near, gj_far, *all_qkv],
        [ANY] * 4,
        [shape((rows, wide), F32), shape((rows, wide), BF)],
        [
            pltpu.VMEM((wide, 3 * half), BF),
            pltpu.VMEM((two, 3 * half), BF),
            sems(8),
        ],
        "qkv_back",
    )
    gone_recv = near(gone_send)
    if whole_two:
        two_part = lax.psum_scatter(two_sums[0], ("x", "fsdp"), scatter_dimension=0, tiled=True)
        two_all = lax.all_gather(two_part, ("x", "core", "seq"), axis=0)
        two_all = two_all.reshape((2, 2, 2) + two_part.shape).transpose(2, 0, 1, 3, 4)
        grad_fc2 = two_all.reshape(w_fc2.shape).astype(F32)
    two_total = two_cross = None if whole_two else scatter_rows(two_sums, *([gone_own] if on("s2") else []))
    if not whole_two:
        two_cross = across(two_total[h:].astype(BF))
    kinds = [F32] + [BF] * (blocks - 1) if blocks > 1 else [BF]
    out_sums = run(
        combine_kernel,
        [out_keep, *out_recvs],
        [VM] * 4,
        [shape((wide // blocks, LANES), kind) for kind in kinds],
        [],
        "combine",
    )
    out_part = scatter_rows(out_sums).astype(BF)
    qkv_sums = grad(qkv_left, [(gj_near, 0), (gj_other, 0)], "grad_qkv_keep", [qkv_recv])
    if not whole_two:
        tick("x2", two_cross)
    else:
        tick("rs2", two_part)
    tick("zo", out_part)
    grad_tokens, sums_one = run(
        tokens_back_kernel,
        [gone_own, gone_recv, tok, grad_middle, vec],
        [VM] * 5,
        [shape((real, wide), BF), shape((2, wide), F32)],
        [],
        "tokens_back",
    )
    grad_tokens = grad_tokens[None]
    qkv_part = scatter_rows(qkv_sums).astype(BF)
    if not whole_two:
        two_parts = spread((two_total[:h] + two_cross.astype(F32)).astype(BF))
    one_part = scatter_rows(one_sums, *([sums_one] if on("s1") else [])).astype(BF)
    out_parts = spread(out_part)
    tick("ago", *out_parts)
    if not whole_two:
        tick("ag2", *two_parts)
    tick("z1", one_part)
    if direct:
        parts = run(
            small_kernel,
            [sums_one, sums_two, joined_sums, hidden_sums],
            [VM] * 4,
            [shape((16, wide // n), F32)] * n,
            [pltpu.VMEM((n, 16, wide // n), F32)],
            "small",
        )
        block = parts[0]
        for k in range(1, n):
            block = block + shift(parts[k], k)
    else:
        wanted = jnp.bitwise_xor(jnp.arange(4), r)
        slots = ((wanted & 1) << 1) | (wanted >> 1)
        chosen = (slots[:, None] == jnp.arange(4)[None, :]).astype(F32)
        joined_sums = jnp.sum(chosen[:, :, None] * joined_sums[None, :, 0, :], axis=1)
        here = (jnp.arange(2) == y).astype(F32)

        def spread_half(row):
            return (here[:, None] * row.reshape(1, half)).reshape(1, wide)

        query_sums = spread_half(joined_sums[:, :LANES])
        value_sums = spread_half(joined_sums[:, 2 * LANES :])
        hidden_sums = hidden_sums.reshape(4, n, h).transpose(1, 0, 2).reshape(n, 1, 4 * h)
        hidden_sums = (hidden_sums * here[None, :, None]).reshape(n, hidden // wide, wide // n)
        rows_of = jnp.concatenate(
            [
                sums_one[0:1],
                sums_two[0:1],
                sums_one[1:2],
                query_sums,
                value_sums,
                sums_two[2:3],
                sums_two[1:2],
                sums_two[3:4],
            ],
            axis=0,
        )
        block = jnp.concatenate(
            [rows_of.reshape(8, n, wide // n).transpose(1, 0, 2), hidden_sums], axis=1
        )
        block = lax.psum_scatter(block, "fsdp", scatter_dimension=0)
    block = block + near(block) + across(block) + diagonal(block)
    block = block + core(block)

    tick("zq", qkv_part)
    qkv_parts = spread(qkv_part)
    one_parts = spread(one_part)
    tick("ag1", *one_parts)
    if not whole_two:
        grad_fc2 = land(two_parts, w_fc2.shape, "rows")
    grad_fc1 = land(one_parts, w_fc1.shape, "hidden")
    tick("agq", *qkv_parts)
    grad_out = land(out_parts, w_out.shape, "columns")
    grad_qkv = land(qkv_parts, w_qkv.shape, "columns")
    return (
        output,
        grad_tokens,
        grad_qkv,
        grad_out,
        grad_fc1,
        grad_fc2,
        block[:2],
        block[2:8],
        block[8 : 8 + few].reshape(-1),
    )


def solution(mesh):
    reps, n, seqs = (mesh.shape[axis] for axis in ("rep", "fsdp", "seq"))
    assert reps == 4 and seqs == 2
    fine = Mesh(mesh.devices.reshape(reps // 2, 2, n, seqs), ("x", "core", "fsdp", "seq"))
    slots = P(("x", "core", "fsdp"), "seq", None)
    first, second = P("fsdp", None), P(None, "fsdp")
    return jax.shard_map(
        functools.partial(on_device, n),
        mesh=fine,
        in_specs=(
            slots,
            P(("x", "core", "fsdp")),
            slots,
            first,
            first,
            first,
            first,
            second,
            second,
            P("fsdp"),
        ),
        out_specs=(slots, slots, first, first, first, first, second, second, P("fsdp")),
        check_vma=False,
    )
```

```python
import functools

import jax
import jax.numpy as jnp
from jax import lax
from jax.experimental import pallas as pl
from jax.experimental.pallas import tpu as pltpu
from jax.sharding import Mesh
from jax.sharding import PartitionSpec as P

HEADS = 16
HEAD_DIM = 64
IMG_TOK = 577
EPSILON = 1e-05
NEGATIVE = -1e30
LANES = 128
BF = jnp.bfloat16
F32 = jnp.float32

ANY = pl.BlockSpec(memory_space=pl.ANY)
VM = pl.BlockSpec(memory_space=pltpu.VMEM)
SM = pl.BlockSpec(memory_space=pltpu.SMEM)

ORDER = (0, 2, 1, 3)
OUT_LANE = 3 * LANES
PEERS = ((0, 0), (1, 0), (0, 2), (1, 2))


def mm(a, b):
    return lax.dot_general(a, b, (((1,), (0,)), ((), ())), preferred_element_type=F32)


def mmt(a, b):
    return lax.dot_general(a, b, (((1,), (1,)), ((), ())), preferred_element_type=F32)


def tmm(a, b):
    return lax.dot_general(a, b, (((0,), (0,)), ((), ())), preferred_element_type=F32)


def normalize(inputs):
    center = inputs - jnp.mean(inputs, axis=-1, keepdims=True)
    inverse = lax.rsqrt(jnp.mean(center * center, axis=-1, keepdims=True) + EPSILON)
    return center * inverse, inverse


def norm_back(grad_in, scaled, inverse, gain_row):
    weighted = grad_in * gain_row
    return inverse * (
        weighted
        - jnp.mean(weighted, axis=-1, keepdims=True)
        - scaled * jnp.mean(weighted * scaled, axis=-1, keepdims=True)
    )


def at(index, size):
    return pl.ds(pl.multiple_of(index * size, size), size)


def flip(r, d):
    return jnp.bitwise_xor(r, d) if d else r


def fetch(copies, sems):
    handles = [pltpu.make_async_copy(s, t, sems.at[i]) for i, (s, t) in enumerate(copies)]
    for handle in handles:
        handle.start()
    return handles


def finish(handles):
    for handle in handles:
        handle.wait()


KNOBS = {"places": 1, "factor": 1.0, "floor": 8.0, "gnear": 0, "n2": 0, "x2": 0, "place": 0.3, "grad_out": 1.0, "ago": 0, "a1": 1, "a3": 0, "rs3": 0, "zq2": 0, "tokens_back": 0.02, "small": 0.02}
TIMES = {
    "qkv": 7.7, "attend": 11.3, "project": 4.9, "mlp": 18.6, "grad_fc2": 6.9,
    "middle_back": 5.4, "grad_fc1_send": 5.9, "grad_out": 4.9, "attend_back": 16.9,
    "grad_qkv_send": 5.7, "qkv_back": 7.1, "grad_fc1_keep": 5.7, "grad_qkv_keep": 5.3,
    "tokens_back": 3.8, "combine": 2.1, "small": 1.5, "place": 3.2, "stack_qkv": 3.4,
    "stack_rest": 4.5, "cast_qkv": 2.7, "cast_rest": 2.7,
}


def on(name, default=1):
    return KNOBS.get(name, default)


def cost(name):
    value = max(TIMES[name], KNOBS.get("floor", 0.0)) * KNOBS.get("factor", 0.25)
    flops = int(value * KNOBS.get(name, 1.0) * 1.15e9)
    return pl.CostEstimate(flops=flops, bytes_accessed=1 << 18, transcendentals=0)


def skipping(body, count, extra):
    def kernel(*refs):
        body(*refs[:count], *refs[count + extra :])

    return kernel if extra else body


def call(body, ins, specs, outs, scratch, name, out_specs=None, first=()):
    return pl.pallas_call(
        skipping(body, len(ins), len(first)),
        out_shape=outs,
        in_specs=specs + [ANY] * len(first),
        out_specs=out_specs or [VM] * len(outs),
        scratch_shapes=scratch,
        compiler_params=pltpu.CompilerParams(vmem_limit_bytes=56 << 20),
        cost_estimate=cost(name),
        name=name,
    )(*ins, *first)


def grid_call(body, ids, ins, specs, outs, out_specs, steps, name, scratch=(), first=()):
    return pl.pallas_call(
        skipping(body, len(ins) + 1, len(first)),
        grid_spec=pltpu.PrefetchScalarGridSpec(
            num_scalar_prefetch=1,
            grid=(steps,),
            in_specs=specs + [ANY] * len(first),
            out_specs=out_specs,
            scratch_shapes=list(scratch),
        ),
        out_shape=outs,
        compiler_params=pltpu.CompilerParams(vmem_limit_bytes=56 << 20),
        cost_estimate=cost(name),
        name=name,
    )(ids, *ins, *first)


def shape(dims, dtype):
    return jax.ShapeDtypeStruct(dims, dtype)


def column_copies(refs, w, ids, lane=0, relative=False):
    rows, q = w.shape[0], w.shape[1] // 4
    copies = []
    for d in range(4):
        slot = pl.ds(ORDER.index(d) * q, q) if relative else at(flip(ids[0], d), q)
        source = refs[d & 1].at[pl.ds((d >> 1) * rows, rows), pl.ds(lane, q)]
        copies.append((source, w.at[:, slot]))
    return copies


def rest_copies(refs, w1, w2, ids, n, sems):
    rows, wide = w1.shape[0], w1.shape[1] // 4
    half, h = w2.shape[1] // 2, w2.shape[0] // (4 * n)
    for d in range(4):
        q = flip(ids[0], d)
        x = jnp.bitwise_xor(ids[0] >> 1, d >> 1)
        source = refs[d & 1].at[at(x, rows), pl.ds(0, wide)]
        pltpu.make_async_copy(source, w1.at[:, at(q, wide)], sems.at[d]).start()
        for i in range(n):
            for side in range(2):
                first = pl.multiple_of(x * rows + (i * 2 + side) * h, h)
                source = refs[d & 1].at[pl.ds(first, h), pl.ds(wide, half)]
                target = w2.at[at(q * n + i, h), pl.ds(side * half, half)]
                pltpu.make_async_copy(source, target, sems.at[4 + d]).start()


def row_copies(refs, w, ids):
    q = w.shape[0] // 4
    return [
        (refs[d & 1].at[pl.ds((d >> 1) * q, q), :], w.at[at(flip(ids[0], d), q), :])
        for d in range(4)
    ]


def split(refs, *counts):
    refs = list(refs)
    out = []
    for count in counts:
        out.append(refs[:count])
        refs = refs[count:]
    return out + [refs]


def qkv_kernel(ids, own, near, vec, *refs):
    weights, (normed, queries, keys, values), (w, sems) = split(refs, 2, 4)
    handles = fetch(column_copies(weights, w, ids), sems)
    rows = own.shape[0]
    for i, part in enumerate((own, near)):
        scaled, _ = normalize(part[...].astype(F32))
        normed[i * rows : (i + 1) * rows, :] = (scaled * vec[0:1, :] + vec[2:3, :]).astype(BF)
    finish(handles)
    scale = HEAD_DIM ** (-0.5)
    first = ids[1] * (queries.shape[1] // LANES)

    def step(i, carry):
        joined = mm(normed[...], w[:, at(i, 3 * LANES)])
        here = at(i, LANES)
        there = at(first + i, LANES)
        queries[:, here] = ((joined[:, :LANES] + vec[3:4, there]) * scale).astype(BF)
        keys[:, here] = joined[:, LANES : 2 * LANES].astype(BF)
        values[:, here] = (joined[:, 2 * LANES :] + vec[4:5, there]).astype(BF)
        return carry

    lax.fori_loop(0, 4, step, 0)


def valid_keys(ids, rows, real):
    index = lax.broadcasted_iota(jnp.int32, (2 * rows, 1), 0)
    second = (index >= rows).astype(jnp.int32)
    local = index - second * rows
    position = jnp.bitwise_xor(second, ids[1]) * real + local
    return (local < real) & (position < IMG_TOK)


def head_half(value, half):
    lane = lax.broadcasted_iota(jnp.int32, value.shape, 1)
    keep = (lane < HEAD_DIM) if half == 0 else (lane >= HEAD_DIM)
    return jnp.where(keep, value, jnp.zeros_like(value))


def with_lanes(value, half, columns):
    lane = lax.broadcasted_iota(jnp.int32, value.shape, 1)
    out = head_half(value, half)
    for i, column in enumerate(columns):
        out = jnp.where(lane == (1 - half) * HEAD_DIM + i, column, out)
    return out


def three_parts(column):
    high = column.astype(BF)
    rest = column - high.astype(F32)
    middle = rest.astype(BF)
    return [high, middle, (rest - middle.astype(F32)).astype(BF)]


def key_shift(ids, rows, real):
    shift = jnp.where(valid_keys(ids, rows, real), 0.0, NEGATIVE)
    return shift.astype(BF)


def attend_kernel(rows, real, ids, queries, keys, values, mixed_own, mixed_near, totals):
    one = jnp.ones((1, 1), BF)
    shift = key_shift(ids, rows, real)
    keys_of = [with_lanes(keys[...], half, [shift]) for half in range(2)]
    values_of = [head_half(values[...], half) for half in range(2)]
    for i, target in enumerate((mixed_own, mixed_near)):
        block = queries[i * rows : (i + 1) * rows, :]
        total = None
        for half in range(2):
            scores = mmt(keys_of[half], with_lanes(block, half, [one]))
            highest = jnp.max(scores, axis=0, keepdims=True)
            exponent = jnp.exp(scores - highest)
            sums = jnp.sum(exponent, axis=0, keepdims=True)
            totals[2 * half + i : 2 * half + i + 1, :] = highest + jnp.log(sums)
            part = tmm(values_of[half], exponent.astype(BF)) * (1.0 / sums)
            total = part if total is None else total + part
        target[...] = total.T.astype(BF)


def attend(ids, queries, keys, values, rows, real, first):
    wide = queries.shape[1]
    steps = wide // LANES
    block = pl.BlockSpec((2 * rows, LANES), lambda i, ids: (0, i))
    half = pl.BlockSpec((rows, LANES), lambda i, ids: (0, i))
    return grid_call(
        functools.partial(attend_kernel, rows, real),
        ids,
        [queries, keys, values],
        [block] * 3,
        [shape((rows, wide), BF)] * 2 + [shape((steps, 4, rows), F32)],
        [half] * 2 + [pl.BlockSpec((None, 4, rows), lambda i, ids: (i, 0, 0))],
        steps,
        "attend",
        first=first,
    )


def attend_back_kernel(
    rows, real, ids, queries, keys, values, mixed_own, mixed_near, grad_own, grad_near,
    totals, near, far, sums,
):
    step = pl.program_id(0)
    one = jnp.ones((1, 1), BF)
    shift = key_shift(ids, rows, real)
    keys_of = [head_half(keys[...], half) for half in range(2)]
    wide_keys = [with_lanes(keys[...], half, [shift, one, one, one]) for half in range(2)]
    wide_values = [with_lanes(values[...], half, [one, one, one]) for half in range(2)]
    lines = jnp.concatenate([totals[...], jnp.zeros_like(totals[...])], axis=0).T
    grad_k = grad_v = None
    grad_q = []
    for part, (mixed, grad_ref) in enumerate(((mixed_own, grad_own), (mixed_near, grad_near))):
        block = queries[part * rows : (part + 1) * rows, :]
        grad = grad_ref[...]
        product = grad.astype(F32) * mixed[...].astype(F32)
        total = None
        for half in range(2):
            line = three_parts(-lines[:, 2 * half + part : 2 * half + part + 1])
            probs = jnp.exp(mmt(wide_keys[half], with_lanes(block, half, [one, *line])))
            inner = jnp.sum(head_half(product, half), axis=1, keepdims=True)
            wide_grad = with_lanes(grad, half, three_parts(-inner))
            grad_scores = (probs * mmt(wide_values[half], wide_grad)).astype(BF)
            first = tmm(keys_of[half], grad_scores)
            total = first if total is None else total + first
            second = mm(grad_scores, head_half(block, half))
            third = mm(probs.astype(BF), head_half(grad, half))
            grad_k = second if grad_k is None else grad_k + second
            grad_v = third if grad_v is None else grad_v + third
        grad_q.append(total.T)
    scale = HEAD_DIM ** (-0.5)
    grad_q = jnp.concatenate(grad_q, axis=0).astype(BF).astype(F32) * scale
    pieces = [grad_q.astype(BF), grad_k.astype(BF), grad_v.astype(BF)]
    for kind, piece in enumerate(pieces):
        columns = slice(kind * LANES, (kind + 1) * LANES)
        sums[:, columns] = jnp.sum(piece.astype(F32), axis=0, keepdims=True)

        @pl.when(step < 2)
        def _():
            near[:, columns] = piece

        @pl.when(step >= 2)
        def _():
            far[:, columns] = piece


def attend_back(ids, saved, mixed, grads, totals, rows, real, first):
    def index(i, ids):
        return jnp.bitwise_xor(ids[0], ((i & 1) << 1) | (i >> 1))

    block = pl.BlockSpec((2 * rows, LANES), lambda i, ids: (0, index(i, ids)))
    half = pl.BlockSpec((rows, LANES), lambda i, ids: (0, index(i, ids)))
    lines = pl.BlockSpec((None, 4, rows), lambda i, ids: (index(i, ids), 0, 0))
    line = pl.BlockSpec((None, 1, 3 * LANES), lambda i, ids: (i, 0, 0))
    pair = (2, 2 * rows, 3 * LANES)
    near = pl.BlockSpec((None,) + pair[1:], lambda i, ids: (jnp.minimum(i, 1), 0, 0))
    far = pl.BlockSpec((None,) + pair[1:], lambda i, ids: (jnp.maximum(i - 2, 0), 0, 0))
    return grid_call(
        functools.partial(attend_back_kernel, rows, real),
        ids,
        [*saved, *mixed, *grads, totals],
        [block] * 3 + [half] * 4 + [lines],
        [shape(pair, BF), shape(pair, BF), shape((4, 1, 3 * LANES), F32)],
        [near, far, line],
        4,
        "attend_back",
        first=first,
    )


def project_kernel(ids, tokens, mixed_own, mixed_near, vec, *refs):
    weights, (mixed, middle, normed), (w, sems) = split(refs, 2, 3)
    handles = fetch(column_copies(weights, w, ids, OUT_LANE), sems)
    y = ids[1]
    half = mixed_own.shape[1]
    mixed[:, at(y, half)] = mixed_own[...]
    mixed[:, at(1 - y, half)] = mixed_near[...]
    finish(handles)
    total = tokens[...].astype(F32) + (mm(mixed[...], w[...]) + vec[5:6, :])
    middle[...] = total
    scaled, _ = normalize(total)
    normed[...] = (scaled * vec[1:2, :] + vec[6:7, :]).astype(BF)


def mlp_kernel(n, joint, ids, n_own, n_near, g_own, g_near, fb, *refs):
    ones, twos, outs, scratch = split(refs, 2, 0 if joint else 2, 7)
    near, far, grad_own, grad_near, result_own, result_near, sums = outs
    w1, w2, normed, grads, total, result, stage, sems, out_sems = scratch
    r = ids[0]
    rows = n_own.shape[0]
    if joint:
        rest_copies(ones, w1, w2, ids, n, sems)
    else:
        fetch(column_copies(ones, w1, ids) + row_copies(twos, w2, ids), sems)
    normed[:rows, :] = n_own[...]
    normed[rows:, :] = n_near[...]
    wide = w1.shape[1] // 4
    grads[:rows, :] = g_own[...]
    grads[rows:, :] = g_near[...]
    total[...] = jnp.zeros_like(total)
    result[...] = jnp.zeros_like(result)

    def out_copy(target, d, kind):
        place = at(2 * kind + (d >> 1), wide)
        return pltpu.make_async_copy(
            stage.at[2 * d + kind], target.at[:, place], out_sems.at[2 * d + kind]
        )

    def step(d, carry):
        here = at(jnp.bitwise_xor(r, d), wide)
        pltpu.make_async_copy(w1.at[:, here], w1.at[:, here], sems.at[d]).wait()
        pltpu.make_async_copy(w2.at[here, :], w2.at[here, :], sems.at[4 + d]).wait()
        hidden = mm(normed[...], w1[:, here]) + fb[:, here]
        gate = 1.0 / (1.0 + jnp.exp(-1.702 * hidden))
        active = (hidden * gate).astype(BF)
        stage[2 * d + 1] = active
        result[...] += mm(active, w2[here, :])
        grad_active = mmt(grads[...], w2[here, :])
        grad_hidden = (
            grad_active * (gate + 1.702 * hidden * gate * (1.0 - gate))
        ).astype(BF)
        stage[2 * d] = grad_hidden
        sums[:, here] = jnp.sum(grad_hidden.astype(F32), axis=0, keepdims=True)
        total[...] += mmt(grad_hidden, w1[:, here])
        for kind in range(2):

            @pl.when((d & 1) == 0)
            def _():
                out_copy(near, d, kind).start()

            @pl.when((d & 1) == 1)
            def _():
                out_copy(far, d, kind).start()

        return carry

    lax.fori_loop(0, 4, step, 0)
    grad_own[...] = total[:rows, :]
    grad_near[...] = total[rows:, :].astype(BF)
    result_own[...] = result[:rows, :]
    result_near[...] = result[rows:, :].astype(BF)
    for d in range(4):
        for kind in range(2):
            out_copy(far if d & 1 else near, d, kind).wait()


def middle_back_kernel(ids, grad_own, grad_recv, middle, incoming, vec, *refs):
    weights, outs, (w, work, sems) = split(refs, 2, 5)
    grad_middle, branch, mixed_own, mixed_near, sums = outs
    handles = fetch(column_copies(weights, w, ids, OUT_LANE), sems)
    y = ids[1]
    grad = grad_own[...] + grad_recv[...].astype(F32)
    scaled, inverse = normalize(middle[...])
    sums[0:1, :] = jnp.sum(grad * scaled, axis=0, keepdims=True)
    sums[1:2, :] = jnp.sum(grad, axis=0, keepdims=True)
    arriving = incoming[...].astype(F32)
    sums[3:4, :] = jnp.sum(arriving, axis=0, keepdims=True)
    total = arriving + norm_back(grad, scaled, inverse, vec[1:2, :])
    grad_middle[...] = total
    low = total.astype(BF)
    branch[...] = low
    sums[2:3, :] = jnp.sum(low.astype(F32), axis=0, keepdims=True)
    finish(handles)
    work[...] = mmt(branch[...], w[...]).astype(BF)
    half = work.shape[1] // 2
    mixed_own[...] = work[:, at(y, half)]
    mixed_near[...] = work[:, at(1 - y, half)]


def qkv_back_kernel(ids, near, far, *refs):
    weights, (own, other), (w, grads, sems) = split(refs, 2, 2)
    wide = near.shape[2]
    copies = column_copies(weights, w, ids, relative=True)
    for s in range(4):
        source = (near if s < 2 else far).at[s % 2]
        copies.append((source, grads.at[:, pl.ds(s * wide, wide)]))
    finish(fetch(copies, sems))
    rows = own.shape[0]
    step_rows = 256

    def step(i, carry):
        here = at(i, step_rows)
        value = mmt(grads[...], w[here, :])
        own[:, here] = value[:rows, :]
        other[:, here] = value[rows:, :].astype(BF)
        return carry

    lax.fori_loop(0, w.shape[0] // step_rows, step, 0)


def tokens_back_kernel(ids, grad_own, grad_recv, tokens, grad_middle, vec, out, sums):
    grad = grad_own[...] + grad_recv[...].astype(F32)
    scaled, inverse = normalize(tokens[...].astype(F32))
    sums[0:1, :] = jnp.sum(grad * scaled, axis=0, keepdims=True)
    sums[1:2, :] = jnp.sum(grad, axis=0, keepdims=True)
    total = grad_middle[...] + norm_back(grad, scaled, inverse, vec[0:1, :])
    out[...] = total.astype(BF)[: out.shape[0], :]


def window(ref, pick):
    if pick is None:
        return ref
    if len(ref.shape) == 3:
        return ref.at[pick]
    return ref.at[:, pl.ds(*pick)]


def extent(array, pick):
    if pick is None:
        return array.shape
    if array.ndim == 3:
        return array.shape[1:]
    return (array.shape[0], pick[1])


def weight_kernel(left_picks, right_picks, more, slots, ids, *refs):
    left_refs, right_refs, extra, rest = split(refs, len(left_picks), len(right_picks), more)
    *outs, a, b, sems = rest
    copies = []
    for parts, target, picks in ((left_refs, a, left_picks), (right_refs, b, right_picks)):
        start = 0
        for part, pick in zip(parts, picks):
            source = window(part, pick)
            count = source.shape[0]
            copies.append((source, target.at[pl.ds(start, count), :]))
            start += count
    finish(fetch(copies, sems))
    if len(outs) == 1 and slots > 1:
        size = outs[0].shape[0] // 4
        for i in range(4):
            block = jnp.bitwise_xor(ids[0] >> 1, i // 2) * 2 + i % 2
            value = tmm(a[:, i * size : (i + 1) * size], b[...])
            outs[0][at(block, size), :] = value.astype(outs[0].dtype)
        return
    if len(outs) > 1:
        rows = outs[0].shape[0]
        for k, out in enumerate(outs):
            for slot in range(slots):
                size = rows // slots
                here = at(slot * len(outs) + lax.rem(ids[2] + k, len(outs)), size)
                value = tmm(a[:, here], b[...])
                if more:
                    value = value + extra[0][here, :].astype(F32)
                out[slot * size : (slot + 1) * size, :] = value.astype(out.dtype)
        return
    (out,) = outs
    step_rows = 256

    def step(i, carry):
        here = at(i, step_rows)
        value = tmm(a[:, here], b[...])
        if more:
            value = value + extra[0][here, :].astype(F32)
        out[here, :] = value.astype(out.dtype)
        return carry

    lax.fori_loop(0, out.shape[0] // step_rows, step, 0)


def weight_grad(ids, left, right, name, extra=(), blocks=1, slots=1, first=()):
    def span(parts):
        dims = [extent(*p) for p in parts]
        return sum(d[0] for d in dims), dims[0][1]

    depth, rows = span(left)
    _, columns = span(right)
    kinds = [F32] + [BF] * (blocks - 1) if blocks > 1 else [BF]
    return call(
        functools.partial(
            weight_kernel, [p for _, p in left], [p for _, p in right], len(extra), slots
        ),
        [ids] + [a for a, _ in left] + [a for a, _ in right] + list(extra),
        [SM] + [ANY] * (len(left) + len(right)) + [VM] * len(extra),
        [shape((rows // blocks, columns), kind) for kind in kinds],
        [
            pltpu.VMEM((depth, rows), BF),
            pltpu.VMEM((depth, columns), BF),
            pltpu.SemaphoreType.DMA((len(left) + len(right),)),
        ],
        name,
        first=first,
    )


def out_grad_kernel(ids, mixed, mixed_far, branch, branch_far, *refs):
    *outs, a, b, sems = refs
    r, y = ids[0], ids[1]
    rows = mixed.shape[0]
    quarters = branch.shape[1] // 2 // LANES
    copies = []
    for i, (left, right) in enumerate(((mixed, branch), (mixed_far, branch_far))):
        here = pl.ds(i * rows, rows)
        copies.append((left, a.at[here, :]))
        for s, (dy, d) in enumerate(PEERS):
            block = flip(y, dy) * quarters + flip(r, d)
            copies.append((right.at[:, at(block, LANES)], b.at[here, pl.ds(s * LANES, LANES)]))
    finish(fetch(copies, sems))
    step_rows = 256

    def step(i, carry):
        here = at(i, step_rows)
        value = tmm(a[:, here], b[...])
        for s, out in enumerate(outs):
            out[here, :] = value[:, s * LANES : (s + 1) * LANES].astype(out.dtype)
        return carry

    lax.fori_loop(0, a.shape[1] // step_rows, step, 0)


def combine_kernel(ids, keep, *refs):
    recvs, outs = refs[:3], refs[3:]
    rows = outs[0].shape[0]
    for k, out in enumerate(outs):
        here = at(lax.rem(ids[2] + k, len(outs)), rows)
        value = keep[here, :]
        for recv in recvs:
            value = value + recv[here, :].astype(F32)
        out[...] = value.astype(out.dtype)


def join(parts):
    return parts[0] if len(parts) == 1 else jnp.concatenate(parts, axis=1)


def cast_qkv_kernel(ids, first, second, third, fourth, gains, biases, shift, out, low):
    rows = first.shape[0]
    out[:rows, :] = join([part[...].astype(BF) for part in (first, second, third, fourth)])
    low[...] = jnp.zeros_like(low)
    width = gains.shape[1]
    low[0:2, :width] = gains[...]
    low[2:8, :width] = biases[...]
    low[8:12, :width] = shift[...]
    out[rows:, :] = low[...].astype(BF)


def cast_rest_kernel(n, ids, *refs):
    ones, (two_part,), (out,) = split(refs, n, 1)
    wide = out.shape[1] // 2
    rows = two_part.shape[0]
    out[:, :wide] = join([part[...].astype(BF) for part in ones])
    out[:rows, wide:] = two_part[:, :wide].astype(BF)
    out[rows:, wide:] = two_part[:, wide:].astype(BF)


def cast(body, ids, blocks, outs, scratch, name, first=()):
    return grid_call(
        body,
        ids,
        [array for array, _, _ in blocks],
        [pl.BlockSpec(block, lambda i, ids, at=at: at(ids)) for _, block, at in blocks],
        outs,
        [pl.BlockSpec(o.shape, lambda i, ids: (0, 0)) for o in outs],
        1,
        name,
        scratch,
        first,
    )


def stack_kernel(n, ids, *refs):
    parts, (out, low) = split(refs, 2 * n)[0], refs[2 * n :]
    rows = out.shape[1]
    width = low.shape[1] // n
    for i, part in enumerate(parts):
        there = lax.rem(ids[2] - i % n + n, n)
        out[(i // n) * n + there] = part[:rows, :]
        if i < n:
            low[:, at(there, width)] = part[rows:, :width].astype(F32)


def stack_rest_kernel(n, ids, *refs):
    parts, (one, two) = split(refs, 2 * n)[0], refs[2 * n :]
    wide, rows = one.shape[2], two.shape[1]
    for i, part in enumerate(parts):
        there = (i // n) * n + lax.rem(ids[2] - i % n + n, n)
        one[there] = part[:, :wide]
        two[there, :, :wide] = part[:rows, wide:]
        two[there, :, wide:] = part[rows:, wide:]


def place_kernel(kind, ids, *refs):
    sources, (out,), _ = split(refs, 8, 1)
    for i, source in enumerate(sources):
        dy, d = PEERS[i % 4]
        block = flip(ids[1], dy) * 4 + flip(ids[0], d + i // 4)
        piece = source[...].astype(F32)
        if kind == "rows":
            out[at(block, piece.shape[0]), :] = piece
            continue
        for g in range(piece.shape[1] // LANES):
            columns = at(block + g * 8, LANES)
            out[:, columns] = piece[:, g * LANES : (g + 1) * LANES]


def place(ids, sources, dims, kind, first):
    rows, columns = sources[0].shape
    steps = 4
    if kind == "rows":
        inside = pl.BlockSpec((rows, columns // steps), lambda i, ids: (0, i))
        outside = pl.BlockSpec((dims[0], dims[1] // steps), lambda i, ids: (0, i))
    else:
        inside = pl.BlockSpec((rows // steps, columns), lambda i, ids: (i, 0))
        outside = pl.BlockSpec((dims[0] // steps, dims[1]), lambda i, ids: (i, 0))
    return grid_call(
        functools.partial(place_kernel, kind),
        ids,
        sources,
        [inside] * 8,
        [shape(dims, F32)],
        [outside],
        steps,
        "place",
        first=first,
    )[0]


def small_kernel(ids, one, two, joined, hidden, *refs):
    *outs, full = refs
    r, y, z = ids[0], ids[1], ids[2]
    n, width = full.shape[0], full.shape[2]
    full[...] = jnp.zeros_like(full)
    for row, (source, line) in {
        0: (one, 0), 1: (two, 0), 2: (one, 1), 5: (two, 2), 6: (two, 1), 7: (two, 3),
    }.items():
        for i in range(n):
            full[i, row : row + 1, :] = source[line : line + 1, i * width : (i + 1) * width]
    slots = [joined[slot] for slot in range(4)]
    for q in range(4):
        value = sum(
            jnp.where(jnp.bitwise_xor(r, d) == q, slots[slot], 0.0) for slot, d in enumerate(ORDER)
        )
        here = slice((q % 2) * LANES, (q % 2 + 1) * LANES)
        for half in range(2):
            mine = jnp.where(y == half, 1.0, 0.0)
            for row, kind in ((3, 0), (4, 2)):
                line = value[:, kind * LANES : (kind + 1) * LANES]
                full[2 * half + q // 2, row : row + 1, here] = line * mine
            row = 8 + 2 * half + q // 2
            for i in range(n):
                line = hidden[:, (q * n + i) * LANES : (q * n + i + 1) * LANES]
                full[i, row : row + 1, here] = line * mine
    for k, out in enumerate(outs):
        out[...] = full[lax.rem(z + k, n)]


def on_device(n, tokens, slot_mask, cotangent, w_qkv, w_out, w_fc1, w_fc2, ln_gains, biases, fc1_bias):
    slot_count, real, wide = tokens.shape
    assert slot_count == 1
    direct = n == 4
    joint = direct and bool(on("scf"))
    whole_two = direct and bool(on("sc2"))
    rows = -(-real // 16) * 16
    hidden = fc1_bias.shape[0] * n
    half, part_hidden = wide // 2, hidden // 2
    h = hidden // n // 8
    x, c = lax.axis_index("x"), lax.axis_index("core")
    y, z = lax.axis_index("seq"), lax.axis_index("fsdp")
    r = 2 * x + c
    ids = jnp.stack([r, y, z]).astype(jnp.int32)
    swap = [(0, 1), (1, 0)]

    def core(v):
        return lax.ppermute(v, "core", swap)

    def across(v):
        return lax.ppermute(v, "x", swap)

    def near(v):
        return lax.ppermute(v, "seq", swap)

    def diagonal(v):
        return lax.ppermute(v, ("x", "seq"), [(i, i ^ 3) for i in range(4)])

    def shift(v, k):
        return lax.ppermute(v, "fsdp", [(i, (i + k) % n) for i in range(n)])

    def scatter_rows(outs, *gate):
        if len(outs) == 1:
            value = lax.psum_scatter(outs[0], "fsdp", scatter_dimension=0, tiled=True).astype(F32)
        else:
            moved = [shift(outs[k], k) for k in range(1, n)]
            value = after("sums", outs[0], *gate) if gate else outs[0]
            for part in moved:
                value = value + part.astype(F32)
        return value

    waiting = []

    def tick(name, *values):
        if on(name):
            waiting.extend(values)

    def take():
        values = tuple(waiting) if direct else ()
        waiting.clear()
        return values

    def after(name, value, *others):
        if not direct or not others or not on(name):
            return value
        value, *others = lax.optimization_barrier((value, *others))
        waiting.extend(others)
        return value

    def run(body, ins, specs, outs, scratch, name, out_specs=None):
        results = call(
            body, [ids, *ins], [SM] + specs, outs, scratch, name, out_specs, take()
        )
        tick("chain", results[0])
        return results

    def make_rows():
        pad = ((0, rows - real), (0, 0))
        tok = jnp.pad(tokens[0], pad)
        tok_near = near(tok)
        positions = y * real + jnp.arange(real)
        keep = slot_mask.astype(F32)[0] * (positions < IMG_TOK).astype(F32)
        keep = keep[:, None]
        grads = jnp.pad((cotangent[0].astype(F32) * keep).astype(BF), pad)
        grads_near = near(grads)
        return tok, tok_near, keep, grads, grads_near

    sems = lambda c: pltpu.SemaphoreType.DMA((c,))
    few = hidden // wide
    shift_rows = fc1_bias.reshape(few, wide // n)
    quarter = part_hidden // 4
    own_rows = wide // n

    def both_cores(v):
        return [v, core(v)]

    if direct:
        q = lambda ids: ids[1] * 4 + ids[0]
        blocks = [(w_qkv, (own_rows, LANES), lambda ids, k=k: (0, k * 8 + q(ids))) for k in range(3)]
        blocks += [(w_out, (own_rows, wide // 4), lambda ids: (0, ids[0]))]
        blocks += [(v, v.shape, lambda ids: (0, 0)) for v in (ln_gains, biases, shift_rows)]
        across_lanes = OUT_LANE + wide // 4
        (qkv_piece,) = cast(
            cast_qkv_kernel,
            ids,
            blocks,
            [shape((own_rows + 16, across_lanes), BF)],
            [pltpu.VMEM((16, across_lanes), F32)],
            "cast_qkv",
            take(),
        )
        tick("c_cast", qkv_piece)
        qkv_own = across(qkv_piece)
        tok, tok_near, keep, grads, grads_near = make_rows()
        blocks = [(w_fc1, (own_rows, LANES), lambda ids, k=k: (0, k * 8 + q(ids))) for k in range(n)]
        blocks += [(w_fc2, (h, wide), lambda ids: (q(ids), 0))]
        def over_z(piece, before=None, gate=()):
            parts = [piece]
            for k in range(1, n):
                ready = piece if before is None else after("zf", piece, before[k], *gate)
                parts.append(shift(ready, k))
            return parts

        qkv_parts = over_z(qkv_piece)
        tick("a1", qkv_parts[1])
        tick("a3", *qkv_parts[2:])
        (rest_piece,) = cast(
            functools.partial(cast_rest_kernel, n),
            ids,
            blocks,
            [shape((own_rows, 2 * quarter), BF)],
            [],
            "cast_rest",
            first=take(),
        )
        tick("c_rest", rest_piece)

        def over_x(parts, own, *gates):
            others = [own]
            for k in range(1, n):
                gate = gates[min(k, len(gates)) - 1] if gates else ()
                others.append(across(after("xf", parts[k], *gate)))
            return others

        def stack(body, parts, others, outs, name):
            values = run(
                functools.partial(body, n),
                parts + others,
                [VM] * (2 * n),
                outs,
                [],
                name,
            )
            flat = [v.reshape(-1, v.shape[2]) if v.ndim == 3 else v for v in values]
            return flat

        if joint:
            rest_all = lax.all_gather(rest_piece, ("x", "fsdp"), axis=0, tiled=True)
        else:
            rest_own = across(rest_piece)
            rest_parts = over_z(rest_piece, qkv_parts)
        tick("tok", tok_near)
        tick("gn2", grads_near)
        qkv_stack, vec = stack(
            stack_kernel,
            qkv_parts,
            over_x(qkv_parts, qkv_own),
            [shape((2 * n, own_rows, across_lanes), BF), shape((16, wide), F32)],
            "stack_qkv",
        )
        all_qkv = both_cores(qkv_stack)
    else:
        cut = lambda v, start, size, axis: lax.dynamic_slice_in_dim(v, start, size, axis).astype(BF)
        qkv_piece = jnp.concatenate(
            [cut(w_qkv, k * wide + y * half + r * LANES, LANES, 1) for k in range(3)]
            + [cut(w_out, r * (wide // 4), wide // 4, 1)],
            axis=1,
        )
        grid = w_fc1.reshape(w_fc1.shape[0], n, 8, h)
        one_piece = cut(grid, y * 4 + r, 1, 2).reshape(w_fc1.shape[0], n * h)
        two_piece = cut(w_fc2, (y * 4 + r) * h, h, 0)

        def whole(v):
            v = lax.all_gather(v, "fsdp", axis=0, tiled=True)
            return both_cores(jnp.concatenate([v, across(v)], axis=0))

        all_qkv, all_one, all_two = map(whole, (qkv_piece, one_piece, two_piece))
        tok, tok_near, keep, grads, grads_near = make_rows()
        small = jnp.concatenate([ln_gains, biases, shift_rows], axis=0).astype(BF)
        vec = lax.all_gather(small, "fsdp", axis=0).astype(F32).transpose(1, 0, 2)
        vec = jnp.pad(vec.reshape(-1, wide), ((0, 4), (0, 0)))

    two = 2 * rows
    tick("gnear", grads_near)
    normed, queries, keys, values = run(
        qkv_kernel,
        [tok, tok_near, vec, *all_qkv],
        [VM] * 3 + [ANY] * 2,
        [shape((two, wide), BF)] + [shape((two, half), BF)] * 3,
        [pltpu.VMEM((wide, 3 * half), BF), sems(4)],
        "qkv",
    )
    hidden_shift = vec[8:12].reshape(few, n, wide // n).transpose(1, 0, 2).reshape(n, 2, 4, h)
    hidden_shift = lax.dynamic_index_in_dim(hidden_shift, y, axis=1, keepdims=False)
    hidden_shift = hidden_shift.transpose(1, 0, 2).reshape(1, part_hidden)
    normed_far = core(normed)
    saved = (queries, keys, values)
    mixed_own, mixed_send, totals = attend(ids, *saved, rows, real, take())
    mixed_parts = (mixed_own, mixed_send)
    tick("chain", mixed_own)
    mixed_recv = near(mixed_send)
    grads_far, grads_near_far = core(grads), core(grads_near)
    mixed, middle, normed_two = run(
        project_kernel,
        [tok, mixed_own, mixed_recv, vec, *all_qkv],
        [VM] * 4 + [ANY] * 2,
        [shape((rows, wide), BF), shape((rows, wide), F32), shape((rows, wide), BF)],
        [pltpu.VMEM((wide, wide), BF), sems(4)],
        "project",
    )
    normed_two_near = near(normed_two)
    mixed_far, normed_two_far = core(mixed), core(normed_two)
    tick("n2", normed_two_near)
    tick("fars", normed_far, mixed_far, grads_far, grads_near_far, normed_two_far)
    if direct:
        if joint:
            all_one, all_two = both_cores(after("cf", rest_all, normed_two)), []
        else:
            rest_others = over_x(rest_parts, rest_own, (mixed_own,))
            one_stack, two_stack = stack(
                stack_rest_kernel,
                rest_parts,
                rest_others,
                [shape((2 * n, own_rows, quarter), BF), shape((2 * n, h, wide), BF)],
                "stack_rest",
            )
            all_one, all_two = both_cores(one_stack), both_cores(two_stack)
    normed_two_near_far = core(normed_two_near)
    tick("n2f", normed_two_near_far)
    act_near, act_far, gtwo_own, gtwo_send, result_own, result_send, hidden_sums = run(
        functools.partial(mlp_kernel, n, joint),
        [normed_two, normed_two_near, grads, grads_near, hidden_shift, *all_one, *all_two],
        [VM] * 5 + [ANY] * (len(all_one) + len(all_two)),
        [
            shape((two, 4 * quarter), BF),
            shape((two, 4 * quarter), BF),
            shape((rows, wide), F32),
            shape((rows, wide), BF),
            shape((rows, wide), F32),
            shape((rows, wide), BF),
            shape((1, part_hidden), F32),
        ],
        [
            pltpu.VMEM((wide, part_hidden), BF),
            pltpu.VMEM((part_hidden, wide), BF),
            pltpu.VMEM((two, wide), BF),
            pltpu.VMEM((two, wide), BF),
            pltpu.VMEM((two, wide), F32),
            pltpu.VMEM((two, wide), F32),
            pltpu.VMEM((8, two, quarter), BF),
            sems(8),
            sems(8),
        ],
        "mlp",
        [ANY] * 2 + [VM] * 5,
    )
    gtwo_recv = near(gtwo_send)
    act_other = core(act_far)

    def spread(part):
        return [part, near(part), across(part), diagonal(part)]

    def land(parts, dims, kind):
        parts = parts + [core(v) for v in parts]
        if direct:
            value = place(ids, parts, dims, kind, take())
            tick("places", value)
            return value
        order = [flip(y, dy) * 4 + flip(r, d + j) for j in range(2) for dy, d in PEERS]
        stack = jnp.zeros((8,) + parts[0].shape, F32)
        for index, v in zip(order, parts):
            stack = lax.dynamic_update_slice_in_dim(stack, v.astype(F32)[None], index, 0)
        if kind == "rows":
            return stack.reshape(dims)
        groups = dims[1] // (8 * (h if kind == "hidden" else LANES))
        stack = stack.reshape(8, dims[0], groups, -1)
        return stack.transpose(1, 2, 0, 3).reshape(dims)

    blocks = n if direct else 1

    def grad(left, right, name, extra=()):
        values = weight_grad(
            ids, left, right, name, extra, blocks if extra else 1, first=take()
        )
        tick("chain", values[0])
        return values if extra else values[0]

    all_grads = [(a, None) for a in (grads, grads_near, grads_far, grads_near_far)]
    one_left = [
        (a, None) for a in (normed_two, normed_two_near, normed_two_far, normed_two_near_far)
    ]

    def unit(slot):
        return [(act_near, (slot * quarter, quarter)), (act_other, (slot * quarter, quarter))]

    two_left = [(v, (2 * quarter, 2 * quarter)) for v in (act_near, act_other)]
    two_sums = weight_grad(
        ids,
        two_left,
        all_grads,
        "grad_fc2",
        blocks=1 if whole_two else blocks,
        slots=2 if direct else 1,
        first=take(),
    )
    tick("chain", two_sums[0])
    if not direct:
        two_sums = [
            v.reshape(2, n, h, wide).transpose(1, 0, 2, 3).reshape(-1, wide) for v in two_sums
        ]
    grad_middle, branch, gmix_own, gmix_send, sums_two = run(
        middle_back_kernel,
        [gtwo_own, gtwo_recv, middle, grads, vec, *all_qkv],
        [VM] * 5 + [ANY] * 2,
        [
            shape((rows, wide), F32),
            shape((rows, wide), BF),
            shape((rows, half), BF),
            shape((rows, half), BF),
            shape((4, wide), F32),
        ],
        [pltpu.VMEM((wide, wide), BF), pltpu.VMEM((rows, wide), BF), sems(4)],
        "middle_back",
    )
    gmix_recv = near(gmix_send)
    branch_far = core(branch)
    one_recv = across(grad(one_left, unit(1), "grad_fc1_send"))
    out_keep, *out_sends = run(
        out_grad_kernel,
        [mixed, mixed_far, branch, branch_far],
        [ANY] * 4,
        [shape((wide, LANES), F32)] + [shape((wide, LANES), BF)] * 3,
        [pltpu.VMEM((two, wide), BF), pltpu.VMEM((two, 4 * LANES), BF), sems(10)],
        "grad_out",
    )
    gj_near, gj_far, joined_sums = attend_back(
        ids, saved, mixed_parts, (gmix_own, gmix_recv), totals, rows, real, take()
    )
    tick("chain", gj_near)
    gj_other = core(gj_far)
    result_recv = near(result_send)
    total = middle[:real] + (
        result_own[:real] + result_recv[:real].astype(F32) + vec[7:8, :]
    )
    output = (total * keep).astype(BF)[None]
    out_recvs = [near(out_sends[0]), across(out_sends[1]), diagonal(out_sends[2])]
    tick("res", result_recv)
    one_sums = grad(one_left, unit(0), "grad_fc1_keep", [one_recv])
    qkv_left = [(normed, None), (normed_far, None)]
    qkv_send = grad(qkv_left, [(gj_near, 1), (gj_other, 1)], "grad_qkv_send")
    qkv_recv = across(qkv_send)
    gone_own, gone_send = run(
        qkv_back_kernel,
        [gj_near, gj_far, *all_qkv],
        [ANY] * 4,
        [shape((rows, wide), F32), shape((rows, wide), BF)],
        [
            pltpu.VMEM((wide, 3 * half), BF),
            pltpu.VMEM((two, 3 * half), BF),
            sems(8),
        ],
        "qkv_back",
    )
    gone_recv = near(gone_send)
    if whole_two:
        two_part = lax.psum_scatter(two_sums[0], ("x", "fsdp"), scatter_dimension=0, tiled=True)
        two_all = lax.all_gather(two_part, ("x", "core", "seq"), axis=0)
        two_all = two_all.reshape((2, 2, 2) + two_part.shape).transpose(2, 0, 1, 3, 4)
        grad_fc2 = two_all.reshape(w_fc2.shape).astype(F32)
    two_total = two_cross = None if whole_two else scatter_rows(two_sums, *([gone_own] if on("s2") else []))
    if not whole_two:
        two_cross = across(two_total[h:].astype(BF))
    kinds = [F32] + [BF] * (blocks - 1) if blocks > 1 else [BF]
    out_sums = run(
        combine_kernel,
        [out_keep, *out_recvs],
        [VM] * 4,
        [shape((wide // blocks, LANES), kind) for kind in kinds],
        [],
        "combine",
    )
    out_part = scatter_rows(out_sums).astype(BF)
    qkv_sums = grad(qkv_left, [(gj_near, 0), (gj_other, 0)], "grad_qkv_keep", [qkv_recv])
    if not whole_two:
        tick("x2", two_cross)
    else:
        tick("rs2", two_part)
    tick("zo", out_part)
    qkv_part = scatter_rows(qkv_sums).astype(BF)
    tick("zq2", qkv_part)
    grad_tokens, sums_one = run(
        tokens_back_kernel,
        [gone_own, gone_recv, tok, grad_middle, vec],
        [VM] * 5,
        [shape((real, wide), BF), shape((2, wide), F32)],
        [],
        "tokens_back",
    )
    grad_tokens = grad_tokens[None]
    if not whole_two:
        two_parts = spread((two_total[:h] + two_cross.astype(F32)).astype(BF))
    one_part = scatter_rows(one_sums, *([sums_one] if on("s1") else [])).astype(BF)
    out_parts = spread(out_part)
    tick("ago", *out_parts)
    if whole_two:
        tick("rs3", two_part)
    if not whole_two:
        tick("ag2", *two_parts)
    tick("z1", one_part)
    if direct:
        parts = run(
            small_kernel,
            [sums_one, sums_two, joined_sums, hidden_sums],
            [VM] * 4,
            [shape((16, wide // n), F32)] * n,
            [pltpu.VMEM((n, 16, wide // n), F32)],
            "small",
        )
        block = parts[0]
        for k in range(1, n):
            block = block + shift(parts[k], k)
    else:
        wanted = jnp.bitwise_xor(jnp.arange(4), r)
        slots = ((wanted & 1) << 1) | (wanted >> 1)
        chosen = (slots[:, None] == jnp.arange(4)[None, :]).astype(F32)
        joined_sums = jnp.sum(chosen[:, :, None] * joined_sums[None, :, 0, :], axis=1)
        here = (jnp.arange(2) == y).astype(F32)

        def spread_half(row):
            return (here[:, None] * row.reshape(1, half)).reshape(1, wide)

        query_sums = spread_half(joined_sums[:, :LANES])
        value_sums = spread_half(joined_sums[:, 2 * LANES :])
        hidden_sums = hidden_sums.reshape(4, n, h).transpose(1, 0, 2).reshape(n, 1, 4 * h)
        hidden_sums = (hidden_sums * here[None, :, None]).reshape(n, hidden // wide, wide // n)
        rows_of = jnp.concatenate(
            [
                sums_one[0:1],
                sums_two[0:1],
                sums_one[1:2],
                query_sums,
                value_sums,
                sums_two[2:3],
                sums_two[1:2],
                sums_two[3:4],
            ],
            axis=0,
        )
        block = jnp.concatenate(
            [rows_of.reshape(8, n, wide // n).transpose(1, 0, 2), hidden_sums], axis=1
        )
        block = lax.psum_scatter(block, "fsdp", scatter_dimension=0)
    block = block + near(block) + across(block) + diagonal(block)
    block = block + core(block)

    tick("zq", qkv_part)
    qkv_parts = spread(qkv_part)
    one_parts = spread(one_part)
    tick("ag1", *one_parts)
    if not whole_two:
        grad_fc2 = land(two_parts, w_fc2.shape, "rows")
    grad_fc1 = land(one_parts, w_fc1.shape, "hidden")
    tick("agq", *qkv_parts)
    grad_out = land(out_parts, w_out.shape, "columns")
    grad_qkv = land(qkv_parts, w_qkv.shape, "columns")
    return (
        output,
        grad_tokens,
        grad_qkv,
        grad_out,
        grad_fc1,
        grad_fc2,
        block[:2],
        block[2:8],
        block[8 : 8 + few].reshape(-1),
    )


def solution(mesh):
    reps, n, seqs = (mesh.shape[axis] for axis in ("rep", "fsdp", "seq"))
    assert reps == 4 and seqs == 2
    fine = Mesh(mesh.devices.reshape(reps // 2, 2, n, seqs), ("x", "core", "fsdp", "seq"))
    slots = P(("x", "core", "fsdp"), "seq", None)
    first, second = P("fsdp", None), P(None, "fsdp")
    return jax.shard_map(
        functools.partial(on_device, n),
        mesh=fine,
        in_specs=(
            slots,
            P(("x", "core", "fsdp")),
            slots,
            first,
            first,
            first,
            first,
            second,
            second,
            P("fsdp"),
        ),
        out_specs=(slots, slots, first, first, first, first, second, second, P("fsdp")),
        check_vma=False,
    )
```

```python
import functools

import jax
import jax.numpy as jnp
from jax import lax
from jax.experimental import pallas as pl
from jax.experimental.pallas import tpu as pltpu
from jax.sharding import Mesh
from jax.sharding import PartitionSpec as P

HEADS = 16
HEAD_DIM = 64
IMG_TOK = 577
EPSILON = 1e-05
NEGATIVE = -1e30
LANES = 128
BF = jnp.bfloat16
F32 = jnp.float32

ANY = pl.BlockSpec(memory_space=pl.ANY)
VM = pl.BlockSpec(memory_space=pltpu.VMEM)
SM = pl.BlockSpec(memory_space=pltpu.SMEM)

ORDER = (0, 2, 1, 3)
OUT_LANE = 3 * LANES
PEERS = ((0, 0), (1, 0), (0, 2), (1, 2))


def mm(a, b):
    return lax.dot_general(a, b, (((1,), (0,)), ((), ())), preferred_element_type=F32)


def mmt(a, b):
    return lax.dot_general(a, b, (((1,), (1,)), ((), ())), preferred_element_type=F32)


def tmm(a, b):
    return lax.dot_general(a, b, (((0,), (0,)), ((), ())), preferred_element_type=F32)


def normalize(inputs):
    center = inputs - jnp.mean(inputs, axis=-1, keepdims=True)
    inverse = lax.rsqrt(jnp.mean(center * center, axis=-1, keepdims=True) + EPSILON)
    return center * inverse, inverse


def norm_back(grad_in, scaled, inverse, gain_row):
    weighted = grad_in * gain_row
    return inverse * (
        weighted
        - jnp.mean(weighted, axis=-1, keepdims=True)
        - scaled * jnp.mean(weighted * scaled, axis=-1, keepdims=True)
    )


def at(index, size):
    return pl.ds(pl.multiple_of(index * size, size), size)


def flip(r, d):
    return jnp.bitwise_xor(r, d) if d else r


def fetch(copies, sems):
    handles = [pltpu.make_async_copy(s, t, sems.at[i]) for i, (s, t) in enumerate(copies)]
    for handle in handles:
        handle.start()
    return handles


def finish(handles):
    for handle in handles:
        handle.wait()


KNOBS = {"places": 1, "factor": 1.0, "floor": 8.0, "gnear": 0, "n2": 0, "x2": 0, "place": 0.3, "grad_out": 1.0, "ago": 0, "a1": 1, "a3": 0, "rs3": 0, "zq2": 0, "tokens_back": 0.02, "small": 0.02, "z1": 0, "ag1": 0, "agq": 0, "zq": 0}
TIMES = {
    "qkv": 7.7, "attend": 11.3, "project": 4.9, "mlp": 18.6, "grad_fc2": 6.9,
    "middle_back": 5.4, "grad_fc1_send": 5.9, "grad_out": 4.9, "attend_back": 16.9,
    "grad_qkv_send": 5.7, "qkv_back": 7.1, "grad_fc1_keep": 5.7, "grad_qkv_keep": 5.3,
    "tokens_back": 3.8, "combine": 2.1, "small": 1.5, "place": 3.2, "stack_qkv": 3.4,
    "stack_rest": 4.5, "cast_qkv": 2.7, "cast_rest": 2.7,
}


def on(name, default=1):
    return KNOBS.get(name, default)


def cost(name):
    value = max(TIMES[name], KNOBS.get("floor", 0.0)) * KNOBS.get("factor", 0.25)
    flops = int(value * KNOBS.get(name, 1.0) * 1.15e9)
    return pl.CostEstimate(flops=flops, bytes_accessed=1 << 18, transcendentals=0)


def skipping(body, count, extra):
    def kernel(*refs):
        body(*refs[:count], *refs[count + extra :])

    return kernel if extra else body


def call(body, ins, specs, outs, scratch, name, out_specs=None, first=()):
    return pl.pallas_call(
        skipping(body, len(ins), len(first)),
        out_shape=outs,
        in_specs=specs + [ANY] * len(first),
        out_specs=out_specs or [VM] * len(outs),
        scratch_shapes=scratch,
        compiler_params=pltpu.CompilerParams(vmem_limit_bytes=56 << 20),
        cost_estimate=cost(name),
        name=name,
    )(*ins, *first)


def grid_call(body, ids, ins, specs, outs, out_specs, steps, name, scratch=(), first=()):
    return pl.pallas_call(
        skipping(body, len(ins) + 1, len(first)),
        grid_spec=pltpu.PrefetchScalarGridSpec(
            num_scalar_prefetch=1,
            grid=(steps,),
            in_specs=specs + [ANY] * len(first),
            out_specs=out_specs,
            scratch_shapes=list(scratch),
        ),
        out_shape=outs,
        compiler_params=pltpu.CompilerParams(vmem_limit_bytes=56 << 20),
        cost_estimate=cost(name),
        name=name,
    )(ids, *ins, *first)


def shape(dims, dtype):
    return jax.ShapeDtypeStruct(dims, dtype)


def column_copies(refs, w, ids, lane=0, relative=False):
    rows, q = w.shape[0], w.shape[1] // 4
    copies = []
    for d in range(4):
        slot = pl.ds(ORDER.index(d) * q, q) if relative else at(flip(ids[0], d), q)
        source = refs[d & 1].at[pl.ds((d >> 1) * rows, rows), pl.ds(lane, q)]
        copies.append((source, w.at[:, slot]))
    return copies


def rest_copies(refs, w1, w2, ids, n, sems):
    rows, wide = w1.shape[0], w1.shape[1] // 4
    half, h = w2.shape[1] // 2, w2.shape[0] // (4 * n)
    for d in range(4):
        q = flip(ids[0], d)
        x = jnp.bitwise_xor(ids[0] >> 1, d >> 1)
        source = refs[d & 1].at[at(x, rows), pl.ds(0, wide)]
        pltpu.make_async_copy(source, w1.at[:, at(q, wide)], sems.at[d]).start()
        for i in range(n):
            for side in range(2):
                first = pl.multiple_of(x * rows + (i * 2 + side) * h, h)
                source = refs[d & 1].at[pl.ds(first, h), pl.ds(wide, half)]
                target = w2.at[at(q * n + i, h), pl.ds(side * half, half)]
                pltpu.make_async_copy(source, target, sems.at[4 + d]).start()


def row_copies(refs, w, ids):
    q = w.shape[0] // 4
    return [
        (refs[d & 1].at[pl.ds((d >> 1) * q, q), :], w.at[at(flip(ids[0], d), q), :])
        for d in range(4)
    ]


def split(refs, *counts):
    refs = list(refs)
    out = []
    for count in counts:
        out.append(refs[:count])
        refs = refs[count:]
    return out + [refs]


def qkv_kernel(ids, own, near, vec, *refs):
    weights, (normed, queries, keys, values), (w, sems) = split(refs, 2, 4)
    handles = fetch(column_copies(weights, w, ids), sems)
    rows = own.shape[0]
    for i, part in enumerate((own, near)):
        scaled, _ = normalize(part[...].astype(F32))
        normed[i * rows : (i + 1) * rows, :] = (scaled * vec[0:1, :] + vec[2:3, :]).astype(BF)
    finish(handles)
    scale = HEAD_DIM ** (-0.5)
    first = ids[1] * (queries.shape[1] // LANES)

    def step(i, carry):
        joined = mm(normed[...], w[:, at(i, 3 * LANES)])
        here = at(i, LANES)
        there = at(first + i, LANES)
        queries[:, here] = ((joined[:, :LANES] + vec[3:4, there]) * scale).astype(BF)
        keys[:, here] = joined[:, LANES : 2 * LANES].astype(BF)
        values[:, here] = (joined[:, 2 * LANES :] + vec[4:5, there]).astype(BF)
        return carry

    lax.fori_loop(0, 4, step, 0)


def valid_keys(ids, rows, real):
    index = lax.broadcasted_iota(jnp.int32, (2 * rows, 1), 0)
    second = (index >= rows).astype(jnp.int32)
    local = index - second * rows
    position = jnp.bitwise_xor(second, ids[1]) * real + local
    return (local < real) & (position < IMG_TOK)


def head_half(value, half):
    lane = lax.broadcasted_iota(jnp.int32, value.shape, 1)
    keep = (lane < HEAD_DIM) if half == 0 else (lane >= HEAD_DIM)
    return jnp.where(keep, value, jnp.zeros_like(value))


def with_lanes(value, half, columns):
    lane = lax.broadcasted_iota(jnp.int32, value.shape, 1)
    out = head_half(value, half)
    for i, column in enumerate(columns):
        out = jnp.where(lane == (1 - half) * HEAD_DIM + i, column, out)
    return out


def three_parts(column):
    high = column.astype(BF)
    rest = column - high.astype(F32)
    middle = rest.astype(BF)
    return [high, middle, (rest - middle.astype(F32)).astype(BF)]


def key_shift(ids, rows, real):
    shift = jnp.where(valid_keys(ids, rows, real), 0.0, NEGATIVE)
    return shift.astype(BF)


def attend_kernel(rows, real, ids, queries, keys, values, mixed_own, mixed_near, totals):
    one = jnp.ones((1, 1), BF)
    shift = key_shift(ids, rows, real)
    keys_of = [with_lanes(keys[...], half, [shift]) for half in range(2)]
    values_of = [head_half(values[...], half) for half in range(2)]
    for i, target in enumerate((mixed_own, mixed_near)):
        block = queries[i * rows : (i + 1) * rows, :]
        total = None
        for half in range(2):
            scores = mmt(keys_of[half], with_lanes(block, half, [one]))
            highest = jnp.max(scores, axis=0, keepdims=True)
            exponent = jnp.exp(scores - highest)
            sums = jnp.sum(exponent, axis=0, keepdims=True)
            totals[2 * half + i : 2 * half + i + 1, :] = highest + jnp.log(sums)
            part = tmm(values_of[half], exponent.astype(BF)) * (1.0 / sums)
            total = part if total is None else total + part
        target[...] = total.T.astype(BF)


def attend(ids, queries, keys, values, rows, real, first):
    wide = queries.shape[1]
    steps = wide // LANES
    block = pl.BlockSpec((2 * rows, LANES), lambda i, ids: (0, i))
    half = pl.BlockSpec((rows, LANES), lambda i, ids: (0, i))
    return grid_call(
        functools.partial(attend_kernel, rows, real),
        ids,
        [queries, keys, values],
        [block] * 3,
        [shape((rows, wide), BF)] * 2 + [shape((steps, 4, rows), F32)],
        [half] * 2 + [pl.BlockSpec((None, 4, rows), lambda i, ids: (i, 0, 0))],
        steps,
        "attend",
        first=first,
    )


def attend_back_kernel(
    rows, real, ids, queries, keys, values, mixed_own, mixed_near, grad_own, grad_near,
    totals, near, far, sums,
):
    step = pl.program_id(0)
    one = jnp.ones((1, 1), BF)
    shift = key_shift(ids, rows, real)
    keys_of = [head_half(keys[...], half) for half in range(2)]
    wide_keys = [with_lanes(keys[...], half, [shift, one, one, one]) for half in range(2)]
    wide_values = [with_lanes(values[...], half, [one, one, one]) for half in range(2)]
    lines = jnp.concatenate([totals[...], jnp.zeros_like(totals[...])], axis=0).T
    grad_k = grad_v = None
    grad_q = []
    for part, (mixed, grad_ref) in enumerate(((mixed_own, grad_own), (mixed_near, grad_near))):
        block = queries[part * rows : (part + 1) * rows, :]
        grad = grad_ref[...]
        product = grad.astype(F32) * mixed[...].astype(F32)
        total = None
        for half in range(2):
            line = three_parts(-lines[:, 2 * half + part : 2 * half + part + 1])
            probs = jnp.exp(mmt(wide_keys[half], with_lanes(block, half, [one, *line])))
            inner = jnp.sum(head_half(product, half), axis=1, keepdims=True)
            wide_grad = with_lanes(grad, half, three_parts(-inner))
            grad_scores = (probs * mmt(wide_values[half], wide_grad)).astype(BF)
            first = tmm(keys_of[half], grad_scores)
            total = first if total is None else total + first
            second = mm(grad_scores, head_half(block, half))
            third = mm(probs.astype(BF), head_half(grad, half))
            grad_k = second if grad_k is None else grad_k + second
            grad_v = third if grad_v is None else grad_v + third
        grad_q.append(total.T)
    scale = HEAD_DIM ** (-0.5)
    grad_q = jnp.concatenate(grad_q, axis=0).astype(BF).astype(F32) * scale
    pieces = [grad_q.astype(BF), grad_k.astype(BF), grad_v.astype(BF)]
    for kind, piece in enumerate(pieces):
        columns = slice(kind * LANES, (kind + 1) * LANES)
        sums[:, columns] = jnp.sum(piece.astype(F32), axis=0, keepdims=True)

        @pl.when(step < 2)
        def _():
            near[:, columns] = piece

        @pl.when(step >= 2)
        def _():
            far[:, columns] = piece


def attend_back(ids, saved, mixed, grads, totals, rows, real, first):
    def index(i, ids):
        return jnp.bitwise_xor(ids[0], ((i & 1) << 1) | (i >> 1))

    block = pl.BlockSpec((2 * rows, LANES), lambda i, ids: (0, index(i, ids)))
    half = pl.BlockSpec((rows, LANES), lambda i, ids: (0, index(i, ids)))
    lines = pl.BlockSpec((None, 4, rows), lambda i, ids: (index(i, ids), 0, 0))
    line = pl.BlockSpec((None, 1, 3 * LANES), lambda i, ids: (i, 0, 0))
    pair = (2, 2 * rows, 3 * LANES)
    near = pl.BlockSpec((None,) + pair[1:], lambda i, ids: (jnp.minimum(i, 1), 0, 0))
    far = pl.BlockSpec((None,) + pair[1:], lambda i, ids: (jnp.maximum(i - 2, 0), 0, 0))
    return grid_call(
        functools.partial(attend_back_kernel, rows, real),
        ids,
        [*saved, *mixed, *grads, totals],
        [block] * 3 + [half] * 4 + [lines],
        [shape(pair, BF), shape(pair, BF), shape((4, 1, 3 * LANES), F32)],
        [near, far, line],
        4,
        "attend_back",
        first=first,
    )


def project_kernel(ids, tokens, mixed_own, mixed_near, vec, *refs):
    weights, (mixed, middle, normed), (w, sems) = split(refs, 2, 3)
    handles = fetch(column_copies(weights, w, ids, OUT_LANE), sems)
    y = ids[1]
    half = mixed_own.shape[1]
    mixed[:, at(y, half)] = mixed_own[...]
    mixed[:, at(1 - y, half)] = mixed_near[...]
    finish(handles)
    total = tokens[...].astype(F32) + (mm(mixed[...], w[...]) + vec[5:6, :])
    middle[...] = total
    scaled, _ = normalize(total)
    normed[...] = (scaled * vec[1:2, :] + vec[6:7, :]).astype(BF)


def mlp_kernel(n, joint, ids, n_own, n_near, g_own, g_near, fb, *refs):
    ones, twos, outs, scratch = split(refs, 2, 0 if joint else 2, 7)
    near, far, grad_own, grad_near, result_own, result_near, sums = outs
    w1, w2, normed, grads, total, result, stage, sems, out_sems = scratch
    r = ids[0]
    rows = n_own.shape[0]
    if joint:
        rest_copies(ones, w1, w2, ids, n, sems)
    else:
        fetch(column_copies(ones, w1, ids) + row_copies(twos, w2, ids), sems)
    normed[:rows, :] = n_own[...]
    normed[rows:, :] = n_near[...]
    wide = w1.shape[1] // 4
    grads[:rows, :] = g_own[...]
    grads[rows:, :] = g_near[...]
    total[...] = jnp.zeros_like(total)
    result[...] = jnp.zeros_like(result)

    def out_copy(target, d, kind):
        place = at(2 * kind + (d >> 1), wide)
        return pltpu.make_async_copy(
            stage.at[2 * d + kind], target.at[:, place], out_sems.at[2 * d + kind]
        )

    def step(d, carry):
        here = at(jnp.bitwise_xor(r, d), wide)
        pltpu.make_async_copy(w1.at[:, here], w1.at[:, here], sems.at[d]).wait()
        pltpu.make_async_copy(w2.at[here, :], w2.at[here, :], sems.at[4 + d]).wait()
        hidden = mm(normed[...], w1[:, here]) + fb[:, here]
        gate = 1.0 / (1.0 + jnp.exp(-1.702 * hidden))
        active = (hidden * gate).astype(BF)
        stage[2 * d + 1] = active
        result[...] += mm(active, w2[here, :])
        grad_active = mmt(grads[...], w2[here, :])
        grad_hidden = (
            grad_active * (gate + 1.702 * hidden * gate * (1.0 - gate))
        ).astype(BF)
        stage[2 * d] = grad_hidden
        sums[:, here] = jnp.sum(grad_hidden.astype(F32), axis=0, keepdims=True)
        total[...] += mmt(grad_hidden, w1[:, here])
        for kind in range(2):

            @pl.when((d & 1) == 0)
            def _():
                out_copy(near, d, kind).start()

            @pl.when((d & 1) == 1)
            def _():
                out_copy(far, d, kind).start()

        return carry

    lax.fori_loop(0, 4, step, 0)
    grad_own[...] = total[:rows, :]
    grad_near[...] = total[rows:, :].astype(BF)
    result_own[...] = result[:rows, :]
    result_near[...] = result[rows:, :].astype(BF)
    for d in range(4):
        for kind in range(2):
            out_copy(far if d & 1 else near, d, kind).wait()


def middle_back_kernel(ids, grad_own, grad_recv, middle, incoming, vec, *refs):
    weights, outs, (w, work, sems) = split(refs, 2, 5)
    grad_middle, branch, mixed_own, mixed_near, sums = outs
    handles = fetch(column_copies(weights, w, ids, OUT_LANE), sems)
    y = ids[1]
    grad = grad_own[...] + grad_recv[...].astype(F32)
    scaled, inverse = normalize(middle[...])
    sums[0:1, :] = jnp.sum(grad * scaled, axis=0, keepdims=True)
    sums[1:2, :] = jnp.sum(grad, axis=0, keepdims=True)
    arriving = incoming[...].astype(F32)
    sums[3:4, :] = jnp.sum(arriving, axis=0, keepdims=True)
    total = arriving + norm_back(grad, scaled, inverse, vec[1:2, :])
    grad_middle[...] = total
    low = total.astype(BF)
    branch[...] = low
    sums[2:3, :] = jnp.sum(low.astype(F32), axis=0, keepdims=True)
    finish(handles)
    work[...] = mmt(branch[...], w[...]).astype(BF)
    half = work.shape[1] // 2
    mixed_own[...] = work[:, at(y, half)]
    mixed_near[...] = work[:, at(1 - y, half)]


def qkv_back_kernel(ids, near, far, *refs):
    weights, (own, other), (w, grads, sems) = split(refs, 2, 2)
    wide = near.shape[2]
    copies = column_copies(weights, w, ids, relative=True)
    for s in range(4):
        source = (near if s < 2 else far).at[s % 2]
        copies.append((source, grads.at[:, pl.ds(s * wide, wide)]))
    finish(fetch(copies, sems))
    rows = own.shape[0]
    step_rows = 256

    def step(i, carry):
        here = at(i, step_rows)
        value = mmt(grads[...], w[here, :])
        own[:, here] = value[:rows, :]
        other[:, here] = value[rows:, :].astype(BF)
        return carry

    lax.fori_loop(0, w.shape[0] // step_rows, step, 0)


def tokens_back_kernel(ids, grad_own, grad_recv, tokens, grad_middle, vec, out, sums):
    grad = grad_own[...] + grad_recv[...].astype(F32)
    scaled, inverse = normalize(tokens[...].astype(F32))
    sums[0:1, :] = jnp.sum(grad * scaled, axis=0, keepdims=True)
    sums[1:2, :] = jnp.sum(grad, axis=0, keepdims=True)
    total = grad_middle[...] + norm_back(grad, scaled, inverse, vec[0:1, :])
    out[...] = total.astype(BF)[: out.shape[0], :]


def window(ref, pick):
    if pick is None:
        return ref
    if len(ref.shape) == 3:
        return ref.at[pick]
    return ref.at[:, pl.ds(*pick)]


def extent(array, pick):
    if pick is None:
        return array.shape
    if array.ndim == 3:
        return array.shape[1:]
    return (array.shape[0], pick[1])


def weight_kernel(left_picks, right_picks, more, slots, ids, *refs):
    left_refs, right_refs, extra, rest = split(refs, len(left_picks), len(right_picks), more)
    *outs, a, b, sems = rest
    copies = []
    for parts, target, picks in ((left_refs, a, left_picks), (right_refs, b, right_picks)):
        start = 0
        for part, pick in zip(parts, picks):
            source = window(part, pick)
            count = source.shape[0]
            copies.append((source, target.at[pl.ds(start, count), :]))
            start += count
    finish(fetch(copies, sems))
    if len(outs) == 1 and slots > 1:
        size = outs[0].shape[0] // 4
        for i in range(4):
            block = jnp.bitwise_xor(ids[0] >> 1, i // 2) * 2 + i % 2
            value = tmm(a[:, i * size : (i + 1) * size], b[...])
            outs[0][at(block, size), :] = value.astype(outs[0].dtype)
        return
    if len(outs) > 1:
        rows = outs[0].shape[0]
        for k, out in enumerate(outs):
            for slot in range(slots):
                size = rows // slots
                here = at(slot * len(outs) + lax.rem(ids[2] + k, len(outs)), size)
                value = tmm(a[:, here], b[...])
                if more:
                    value = value + extra[0][here, :].astype(F32)
                out[slot * size : (slot + 1) * size, :] = value.astype(out.dtype)
        return
    (out,) = outs
    step_rows = 256

    def step(i, carry):
        here = at(i, step_rows)
        value = tmm(a[:, here], b[...])
        if more:
            value = value + extra[0][here, :].astype(F32)
        out[here, :] = value.astype(out.dtype)
        return carry

    lax.fori_loop(0, out.shape[0] // step_rows, step, 0)


def weight_grad(ids, left, right, name, extra=(), blocks=1, slots=1, first=()):
    def span(parts):
        dims = [extent(*p) for p in parts]
        return sum(d[0] for d in dims), dims[0][1]

    depth, rows = span(left)
    _, columns = span(right)
    kinds = [F32] + [BF] * (blocks - 1) if blocks > 1 else [BF]
    return call(
        functools.partial(
            weight_kernel, [p for _, p in left], [p for _, p in right], len(extra), slots
        ),
        [ids] + [a for a, _ in left] + [a for a, _ in right] + list(extra),
        [SM] + [ANY] * (len(left) + len(right)) + [VM] * len(extra),
        [shape((rows // blocks, columns), kind) for kind in kinds],
        [
            pltpu.VMEM((depth, rows), BF),
            pltpu.VMEM((depth, columns), BF),
            pltpu.SemaphoreType.DMA((len(left) + len(right),)),
        ],
        name,
        first=first,
    )


def out_grad_kernel(ids, mixed, mixed_far, branch, branch_far, *refs):
    *outs, a, b, sems = refs
    r, y = ids[0], ids[1]
    rows = mixed.shape[0]
    quarters = branch.shape[1] // 2 // LANES
    copies = []
    for i, (left, right) in enumerate(((mixed, branch), (mixed_far, branch_far))):
        here = pl.ds(i * rows, rows)
        copies.append((left, a.at[here, :]))
        for s, (dy, d) in enumerate(PEERS):
            block = flip(y, dy) * quarters + flip(r, d)
            copies.append((right.at[:, at(block, LANES)], b.at[here, pl.ds(s * LANES, LANES)]))
    finish(fetch(copies, sems))
    step_rows = 256

    def step(i, carry):
        here = at(i, step_rows)
        value = tmm(a[:, here], b[...])
        for s, out in enumerate(outs):
            out[here, :] = value[:, s * LANES : (s + 1) * LANES].astype(out.dtype)
        return carry

    lax.fori_loop(0, a.shape[1] // step_rows, step, 0)


def combine_kernel(ids, keep, *refs):
    recvs, outs = refs[:3], refs[3:]
    rows = outs[0].shape[0]
    for k, out in enumerate(outs):
        here = at(lax.rem(ids[2] + k, len(outs)), rows)
        value = keep[here, :]
        for recv in recvs:
            value = value + recv[here, :].astype(F32)
        out[...] = value.astype(out.dtype)


def join(parts):
    return parts[0] if len(parts) == 1 else jnp.concatenate(parts, axis=1)


def cast_qkv_kernel(ids, first, second, third, fourth, gains, biases, shift, out, low):
    rows = first.shape[0]
    out[:rows, :] = join([part[...].astype(BF) for part in (first, second, third, fourth)])
    low[...] = jnp.zeros_like(low)
    width = gains.shape[1]
    low[0:2, :width] = gains[...]
    low[2:8, :width] = biases[...]
    low[8:12, :width] = shift[...]
    out[rows:, :] = low[...].astype(BF)


def cast_rest_kernel(n, ids, *refs):
    ones, (two_part,), (out,) = split(refs, n, 1)
    wide = out.shape[1] // 2
    rows = two_part.shape[0]
    out[:, :wide] = join([part[...].astype(BF) for part in ones])
    out[:rows, wide:] = two_part[:, :wide].astype(BF)
    out[rows:, wide:] = two_part[:, wide:].astype(BF)


def cast(body, ids, blocks, outs, scratch, name, first=()):
    return grid_call(
        body,
        ids,
        [array for array, _, _ in blocks],
        [pl.BlockSpec(block, lambda i, ids, at=at: at(ids)) for _, block, at in blocks],
        outs,
        [pl.BlockSpec(o.shape, lambda i, ids: (0, 0)) for o in outs],
        1,
        name,
        scratch,
        first,
    )


def stack_kernel(n, ids, *refs):
    parts, (out, low) = split(refs, 2 * n)[0], refs[2 * n :]
    rows = out.shape[1]
    width = low.shape[1] // n
    for i, part in enumerate(parts):
        there = lax.rem(ids[2] - i % n + n, n)
        out[(i // n) * n + there] = part[:rows, :]
        if i < n:
            low[:, at(there, width)] = part[rows:, :width].astype(F32)


def stack_rest_kernel(n, ids, *refs):
    parts, (one, two) = split(refs, 2 * n)[0], refs[2 * n :]
    wide, rows = one.shape[2], two.shape[1]
    for i, part in enumerate(parts):
        there = (i // n) * n + lax.rem(ids[2] - i % n + n, n)
        one[there] = part[:, :wide]
        two[there, :, :wide] = part[:rows, wide:]
        two[there, :, wide:] = part[rows:, wide:]


def place_kernel(kind, ids, *refs):
    sources, (out,), _ = split(refs, 8, 1)
    for i, source in enumerate(sources):
        dy, d = PEERS[i % 4]
        block = flip(ids[1], dy) * 4 + flip(ids[0], d + i // 4)
        piece = source[...].astype(F32)
        if kind == "rows":
            out[at(block, piece.shape[0]), :] = piece
            continue
        for g in range(piece.shape[1] // LANES):
            columns = at(block + g * 8, LANES)
            out[:, columns] = piece[:, g * LANES : (g + 1) * LANES]


def place(ids, sources, dims, kind, first):
    rows, columns = sources[0].shape
    steps = 4
    if kind == "rows":
        inside = pl.BlockSpec((rows, columns // steps), lambda i, ids: (0, i))
        outside = pl.BlockSpec((dims[0], dims[1] // steps), lambda i, ids: (0, i))
    else:
        inside = pl.BlockSpec((rows // steps, columns), lambda i, ids: (i, 0))
        outside = pl.BlockSpec((dims[0] // steps, dims[1]), lambda i, ids: (i, 0))
    return grid_call(
        functools.partial(place_kernel, kind),
        ids,
        sources,
        [inside] * 8,
        [shape(dims, F32)],
        [outside],
        steps,
        "place",
        first=first,
    )[0]


def small_kernel(ids, one, two, joined, hidden, *refs):
    *outs, full = refs
    r, y, z = ids[0], ids[1], ids[2]
    n, width = full.shape[0], full.shape[2]
    full[...] = jnp.zeros_like(full)
    for row, (source, line) in {
        0: (one, 0), 1: (two, 0), 2: (one, 1), 5: (two, 2), 6: (two, 1), 7: (two, 3),
    }.items():
        for i in range(n):
            full[i, row : row + 1, :] = source[line : line + 1, i * width : (i + 1) * width]
    slots = [joined[slot] for slot in range(4)]
    for q in range(4):
        value = sum(
            jnp.where(jnp.bitwise_xor(r, d) == q, slots[slot], 0.0) for slot, d in enumerate(ORDER)
        )
        here = slice((q % 2) * LANES, (q % 2 + 1) * LANES)
        for half in range(2):
            mine = jnp.where(y == half, 1.0, 0.0)
            for row, kind in ((3, 0), (4, 2)):
                line = value[:, kind * LANES : (kind + 1) * LANES]
                full[2 * half + q // 2, row : row + 1, here] = line * mine
            row = 8 + 2 * half + q // 2
            for i in range(n):
                line = hidden[:, (q * n + i) * LANES : (q * n + i + 1) * LANES]
                full[i, row : row + 1, here] = line * mine
    for k, out in enumerate(outs):
        out[...] = full[lax.rem(z + k, n)]


def on_device(n, tokens, slot_mask, cotangent, w_qkv, w_out, w_fc1, w_fc2, ln_gains, biases, fc1_bias):
    slot_count, real, wide = tokens.shape
    assert slot_count == 1
    direct = n == 4
    joint = direct and bool(on("scf"))
    whole_two = direct and bool(on("sc2"))
    rows = -(-real // 16) * 16
    hidden = fc1_bias.shape[0] * n
    half, part_hidden = wide // 2, hidden // 2
    h = hidden // n // 8
    x, c = lax.axis_index("x"), lax.axis_index("core")
    y, z = lax.axis_index("seq"), lax.axis_index("fsdp")
    r = 2 * x + c
    ids = jnp.stack([r, y, z]).astype(jnp.int32)
    swap = [(0, 1), (1, 0)]

    def core(v):
        return lax.ppermute(v, "core", swap)

    def across(v):
        return lax.ppermute(v, "x", swap)

    def near(v):
        return lax.ppermute(v, "seq", swap)

    def diagonal(v):
        return lax.ppermute(v, ("x", "seq"), [(i, i ^ 3) for i in range(4)])

    def shift(v, k):
        return lax.ppermute(v, "fsdp", [(i, (i + k) % n) for i in range(n)])

    def scatter_rows(outs, *gate):
        if len(outs) == 1:
            value = lax.psum_scatter(outs[0], "fsdp", scatter_dimension=0, tiled=True).astype(F32)
        else:
            moved = [shift(outs[k], k) for k in range(1, n)]
            value = after("sums", outs[0], *gate) if gate else outs[0]
            for part in moved:
                value = value + part.astype(F32)
        return value

    waiting = []

    def tick(name, *values):
        if on(name):
            waiting.extend(values)

    def take():
        values = tuple(waiting) if direct else ()
        waiting.clear()
        return values

    def after(name, value, *others):
        if not direct or not others or not on(name):
            return value
        value, *others = lax.optimization_barrier((value, *others))
        waiting.extend(others)
        return value

    def run(body, ins, specs, outs, scratch, name, out_specs=None):
        results = call(
            body, [ids, *ins], [SM] + specs, outs, scratch, name, out_specs, take()
        )
        tick("chain", results[0])
        return results

    def make_rows():
        pad = ((0, rows - real), (0, 0))
        tok = jnp.pad(tokens[0], pad)
        tok_near = near(tok)
        positions = y * real + jnp.arange(real)
        keep = slot_mask.astype(F32)[0] * (positions < IMG_TOK).astype(F32)
        keep = keep[:, None]
        grads = jnp.pad((cotangent[0].astype(F32) * keep).astype(BF), pad)
        grads_near = near(grads)
        return tok, tok_near, keep, grads, grads_near

    sems = lambda c: pltpu.SemaphoreType.DMA((c,))
    few = hidden // wide
    shift_rows = fc1_bias.reshape(few, wide // n)
    quarter = part_hidden // 4
    own_rows = wide // n

    def both_cores(v):
        return [v, core(v)]

    if direct:
        q = lambda ids: ids[1] * 4 + ids[0]
        blocks = [(w_qkv, (own_rows, LANES), lambda ids, k=k: (0, k * 8 + q(ids))) for k in range(3)]
        blocks += [(w_out, (own_rows, wide // 4), lambda ids: (0, ids[0]))]
        blocks += [(v, v.shape, lambda ids: (0, 0)) for v in (ln_gains, biases, shift_rows)]
        across_lanes = OUT_LANE + wide // 4
        (qkv_piece,) = cast(
            cast_qkv_kernel,
            ids,
            blocks,
            [shape((own_rows + 16, across_lanes), BF)],
            [pltpu.VMEM((16, across_lanes), F32)],
            "cast_qkv",
            take(),
        )
        tick("c_cast", qkv_piece)
        qkv_own = across(qkv_piece)
        tok, tok_near, keep, grads, grads_near = make_rows()
        blocks = [(w_fc1, (own_rows, LANES), lambda ids, k=k: (0, k * 8 + q(ids))) for k in range(n)]
        blocks += [(w_fc2, (h, wide), lambda ids: (q(ids), 0))]
        def over_z(piece, before=None, gate=()):
            parts = [piece]
            for k in range(1, n):
                ready = piece if before is None else after("zf", piece, before[k], *gate)
                parts.append(shift(ready, k))
            return parts

        qkv_parts = over_z(qkv_piece)
        tick("a1", qkv_parts[1])
        tick("a3", *qkv_parts[2:])
        (rest_piece,) = cast(
            functools.partial(cast_rest_kernel, n),
            ids,
            blocks,
            [shape((own_rows, 2 * quarter), BF)],
            [],
            "cast_rest",
            first=take(),
        )
        tick("c_rest", rest_piece)

        def over_x(parts, own, *gates):
            others = [own]
            for k in range(1, n):
                gate = gates[min(k, len(gates)) - 1] if gates else ()
                others.append(across(after("xf", parts[k], *gate)))
            return others

        def stack(body, parts, others, outs, name):
            values = run(
                functools.partial(body, n),
                parts + others,
                [VM] * (2 * n),
                outs,
                [],
                name,
            )
            flat = [v.reshape(-1, v.shape[2]) if v.ndim == 3 else v for v in values]
            return flat

        if joint:
            rest_all = lax.all_gather(rest_piece, ("x", "fsdp"), axis=0, tiled=True)
        else:
            rest_own = across(rest_piece)
            rest_parts = over_z(rest_piece, qkv_parts)
        tick("tok", tok_near)
        tick("gn2", grads_near)
        qkv_stack, vec = stack(
            stack_kernel,
            qkv_parts,
            over_x(qkv_parts, qkv_own),
            [shape((2 * n, own_rows, across_lanes), BF), shape((16, wide), F32)],
            "stack_qkv",
        )
        all_qkv = both_cores(qkv_stack)
    else:
        cut = lambda v, start, size, axis: lax.dynamic_slice_in_dim(v, start, size, axis).astype(BF)
        qkv_piece = jnp.concatenate(
            [cut(w_qkv, k * wide + y * half + r * LANES, LANES, 1) for k in range(3)]
            + [cut(w_out, r * (wide // 4), wide // 4, 1)],
            axis=1,
        )
        grid = w_fc1.reshape(w_fc1.shape[0], n, 8, h)
        one_piece = cut(grid, y * 4 + r, 1, 2).reshape(w_fc1.shape[0], n * h)
        two_piece = cut(w_fc2, (y * 4 + r) * h, h, 0)

        def whole(v):
            v = lax.all_gather(v, "fsdp", axis=0, tiled=True)
            return both_cores(jnp.concatenate([v, across(v)], axis=0))

        all_qkv, all_one, all_two = map(whole, (qkv_piece, one_piece, two_piece))
        tok, tok_near, keep, grads, grads_near = make_rows()
        small = jnp.concatenate([ln_gains, biases, shift_rows], axis=0).astype(BF)
        vec = lax.all_gather(small, "fsdp", axis=0).astype(F32).transpose(1, 0, 2)
        vec = jnp.pad(vec.reshape(-1, wide), ((0, 4), (0, 0)))

    two = 2 * rows
    tick("gnear", grads_near)
    normed, queries, keys, values = run(
        qkv_kernel,
        [tok, tok_near, vec, *all_qkv],
        [VM] * 3 + [ANY] * 2,
        [shape((two, wide), BF)] + [shape((two, half), BF)] * 3,
        [pltpu.VMEM((wide, 3 * half), BF), sems(4)],
        "qkv",
    )
    hidden_shift = vec[8:12].reshape(few, n, wide // n).transpose(1, 0, 2).reshape(n, 2, 4, h)
    hidden_shift = lax.dynamic_index_in_dim(hidden_shift, y, axis=1, keepdims=False)
    hidden_shift = hidden_shift.transpose(1, 0, 2).reshape(1, part_hidden)
    normed_far = core(normed)
    saved = (queries, keys, values)
    mixed_own, mixed_send, totals = attend(ids, *saved, rows, real, take())
    mixed_parts = (mixed_own, mixed_send)
    tick("chain", mixed_own)
    mixed_recv = near(mixed_send)
    grads_far, grads_near_far = core(grads), core(grads_near)
    mixed, middle, normed_two = run(
        project_kernel,
        [tok, mixed_own, mixed_recv, vec, *all_qkv],
        [VM] * 4 + [ANY] * 2,
        [shape((rows, wide), BF), shape((rows, wide), F32), shape((rows, wide), BF)],
        [pltpu.VMEM((wide, wide), BF), sems(4)],
        "project",
    )
    normed_two_near = near(normed_two)
    mixed_far, normed_two_far = core(mixed), core(normed_two)
    tick("n2", normed_two_near)
    tick("fars", normed_far, mixed_far, grads_far, grads_near_far, normed_two_far)
    if direct:
        if joint:
            all_one, all_two = both_cores(after("cf", rest_all, normed_two)), []
        else:
            rest_others = over_x(rest_parts, rest_own, (mixed_own,))
            one_stack, two_stack = stack(
                stack_rest_kernel,
                rest_parts,
                rest_others,
                [shape((2 * n, own_rows, quarter), BF), shape((2 * n, h, wide), BF)],
                "stack_rest",
            )
            all_one, all_two = both_cores(one_stack), both_cores(two_stack)
    normed_two_near_far = core(normed_two_near)
    tick("n2f", normed_two_near_far)
    act_near, act_far, gtwo_own, gtwo_send, result_own, result_send, hidden_sums = run(
        functools.partial(mlp_kernel, n, joint),
        [normed_two, normed_two_near, grads, grads_near, hidden_shift, *all_one, *all_two],
        [VM] * 5 + [ANY] * (len(all_one) + len(all_two)),
        [
            shape((two, 4 * quarter), BF),
            shape((two, 4 * quarter), BF),
            shape((rows, wide), F32),
            shape((rows, wide), BF),
            shape((rows, wide), F32),
            shape((rows, wide), BF),
            shape((1, part_hidden), F32),
        ],
        [
            pltpu.VMEM((wide, part_hidden), BF),
            pltpu.VMEM((part_hidden, wide), BF),
            pltpu.VMEM((two, wide), BF),
            pltpu.VMEM((two, wide), BF),
            pltpu.VMEM((two, wide), F32),
            pltpu.VMEM((two, wide), F32),
            pltpu.VMEM((8, two, quarter), BF),
            sems(8),
            sems(8),
        ],
        "mlp",
        [ANY] * 2 + [VM] * 5,
    )
    gtwo_recv = near(gtwo_send)
    act_other = core(act_far)

    def spread(part):
        return [part, near(part), across(part), diagonal(part)]

    def land(parts, dims, kind):
        parts = parts + [core(v) for v in parts]
        if direct:
            value = place(ids, parts, dims, kind, take())
            tick("places", value)
            return value
        order = [flip(y, dy) * 4 + flip(r, d + j) for j in range(2) for dy, d in PEERS]
        stack = jnp.zeros((8,) + parts[0].shape, F32)
        for index, v in zip(order, parts):
            stack = lax.dynamic_update_slice_in_dim(stack, v.astype(F32)[None], index, 0)
        if kind == "rows":
            return stack.reshape(dims)
        groups = dims[1] // (8 * (h if kind == "hidden" else LANES))
        stack = stack.reshape(8, dims[0], groups, -1)
        return stack.transpose(1, 2, 0, 3).reshape(dims)

    blocks = n if direct else 1

    def grad(left, right, name, extra=()):
        values = weight_grad(
            ids, left, right, name, extra, blocks if extra else 1, first=take()
        )
        tick("chain", values[0])
        return values if extra else values[0]

    all_grads = [(a, None) for a in (grads, grads_near, grads_far, grads_near_far)]
    one_left = [
        (a, None) for a in (normed_two, normed_two_near, normed_two_far, normed_two_near_far)
    ]

    def unit(slot):
        return [(act_near, (slot * quarter, quarter)), (act_other, (slot * quarter, quarter))]

    two_left = [(v, (2 * quarter, 2 * quarter)) for v in (act_near, act_other)]
    two_sums = weight_grad(
        ids,
        two_left,
        all_grads,
        "grad_fc2",
        blocks=1 if whole_two else blocks,
        slots=2 if direct else 1,
        first=take(),
    )
    tick("chain", two_sums[0])
    if not direct:
        two_sums = [
            v.reshape(2, n, h, wide).transpose(1, 0, 2, 3).reshape(-1, wide) for v in two_sums
        ]
    grad_middle, branch, gmix_own, gmix_send, sums_two = run(
        middle_back_kernel,
        [gtwo_own, gtwo_recv, middle, grads, vec, *all_qkv],
        [VM] * 5 + [ANY] * 2,
        [
            shape((rows, wide), F32),
            shape((rows, wide), BF),
            shape((rows, half), BF),
            shape((rows, half), BF),
            shape((4, wide), F32),
        ],
        [pltpu.VMEM((wide, wide), BF), pltpu.VMEM((rows, wide), BF), sems(4)],
        "middle_back",
    )
    gmix_recv = near(gmix_send)
    branch_far = core(branch)
    one_recv = across(grad(one_left, unit(1), "grad_fc1_send"))
    out_keep, *out_sends = run(
        out_grad_kernel,
        [mixed, mixed_far, branch, branch_far],
        [ANY] * 4,
        [shape((wide, LANES), F32)] + [shape((wide, LANES), BF)] * 3,
        [pltpu.VMEM((two, wide), BF), pltpu.VMEM((two, 4 * LANES), BF), sems(10)],
        "grad_out",
    )
    gj_near, gj_far, joined_sums = attend_back(
        ids, saved, mixed_parts, (gmix_own, gmix_recv), totals, rows, real, take()
    )
    tick("chain", gj_near)
    gj_other = core(gj_far)
    result_recv = near(result_send)
    total = middle[:real] + (
        result_own[:real] + result_recv[:real].astype(F32) + vec[7:8, :]
    )
    output = (total * keep).astype(BF)[None]
    out_recvs = [near(out_sends[0]), across(out_sends[1]), diagonal(out_sends[2])]
    tick("res", result_recv)
    one_sums = grad(one_left, unit(0), "grad_fc1_keep", [one_recv])
    qkv_left = [(normed, None), (normed_far, None)]
    qkv_send = grad(qkv_left, [(gj_near, 1), (gj_other, 1)], "grad_qkv_send")
    qkv_recv = across(qkv_send)
    gone_own, gone_send = run(
        qkv_back_kernel,
        [gj_near, gj_far, *all_qkv],
        [ANY] * 4,
        [shape((rows, wide), F32), shape((rows, wide), BF)],
        [
            pltpu.VMEM((wide, 3 * half), BF),
            pltpu.VMEM((two, 3 * half), BF),
            sems(8),
        ],
        "qkv_back",
    )
    gone_recv = near(gone_send)
    if whole_two:
        two_part = lax.psum_scatter(two_sums[0], ("x", "fsdp"), scatter_dimension=0, tiled=True)
        two_all = lax.all_gather(two_part, ("x", "core", "seq"), axis=0)
        two_all = two_all.reshape((2, 2, 2) + two_part.shape).transpose(2, 0, 1, 3, 4)
        grad_fc2 = two_all.reshape(w_fc2.shape).astype(F32)
    two_total = two_cross = None if whole_two else scatter_rows(two_sums, *([gone_own] if on("s2") else []))
    if not whole_two:
        two_cross = across(two_total[h:].astype(BF))
    kinds = [F32] + [BF] * (blocks - 1) if blocks > 1 else [BF]
    out_sums = run(
        combine_kernel,
        [out_keep, *out_recvs],
        [VM] * 4,
        [shape((wide // blocks, LANES), kind) for kind in kinds],
        [],
        "combine",
    )
    out_part = scatter_rows(out_sums).astype(BF)
    qkv_sums = grad(qkv_left, [(gj_near, 0), (gj_other, 0)], "grad_qkv_keep", [qkv_recv])
    if not whole_two:
        tick("x2", two_cross)
    else:
        tick("rs2", two_part)
    tick("zo", out_part)
    qkv_part = scatter_rows(qkv_sums).astype(BF)
    tick("zq2", qkv_part)
    grad_tokens, sums_one = run(
        tokens_back_kernel,
        [gone_own, gone_recv, tok, grad_middle, vec],
        [VM] * 5,
        [shape((real, wide), BF), shape((2, wide), F32)],
        [],
        "tokens_back",
    )
    grad_tokens = grad_tokens[None]
    if not whole_two:
        two_parts = spread((two_total[:h] + two_cross.astype(F32)).astype(BF))
    one_part = scatter_rows(one_sums, *([sums_one] if on("s1") else [])).astype(BF)
    out_parts = spread(out_part)
    tick("ago", *out_parts)
    if whole_two:
        tick("rs3", two_part)
    if not whole_two:
        tick("ag2", *two_parts)
    tick("z1", one_part)
    if direct:
        parts = run(
            small_kernel,
            [sums_one, sums_two, joined_sums, hidden_sums],
            [VM] * 4,
            [shape((16, wide // n), F32)] * n,
            [pltpu.VMEM((n, 16, wide // n), F32)],
            "small",
        )
        block = parts[0]
        for k in range(1, n):
            block = block + shift(parts[k], k)
    else:
        wanted = jnp.bitwise_xor(jnp.arange(4), r)
        slots = ((wanted & 1) << 1) | (wanted >> 1)
        chosen = (slots[:, None] == jnp.arange(4)[None, :]).astype(F32)
        joined_sums = jnp.sum(chosen[:, :, None] * joined_sums[None, :, 0, :], axis=1)
        here = (jnp.arange(2) == y).astype(F32)

        def spread_half(row):
            return (here[:, None] * row.reshape(1, half)).reshape(1, wide)

        query_sums = spread_half(joined_sums[:, :LANES])
        value_sums = spread_half(joined_sums[:, 2 * LANES :])
        hidden_sums = hidden_sums.reshape(4, n, h).transpose(1, 0, 2).reshape(n, 1, 4 * h)
        hidden_sums = (hidden_sums * here[None, :, None]).reshape(n, hidden // wide, wide // n)
        rows_of = jnp.concatenate(
            [
                sums_one[0:1],
                sums_two[0:1],
                sums_one[1:2],
                query_sums,
                value_sums,
                sums_two[2:3],
                sums_two[1:2],
                sums_two[3:4],
            ],
            axis=0,
        )
        block = jnp.concatenate(
            [rows_of.reshape(8, n, wide // n).transpose(1, 0, 2), hidden_sums], axis=1
        )
        block = lax.psum_scatter(block, "fsdp", scatter_dimension=0)
    block = block + near(block) + across(block) + diagonal(block)
    block = block + core(block)

    tick("zq", qkv_part)
    qkv_parts = spread(qkv_part)
    one_parts = spread(one_part)
    tick("ag1", *one_parts)
    if not whole_two:
        grad_fc2 = land(two_parts, w_fc2.shape, "rows")
    grad_fc1 = land(one_parts, w_fc1.shape, "hidden")
    tick("agq", *qkv_parts)
    grad_out = land(out_parts, w_out.shape, "columns")
    grad_qkv = land(qkv_parts, w_qkv.shape, "columns")
    return (
        output,
        grad_tokens,
        grad_qkv,
        grad_out,
        grad_fc1,
        grad_fc2,
        block[:2],
        block[2:8],
        block[8 : 8 + few].reshape(-1),
    )


def solution(mesh):
    reps, n, seqs = (mesh.shape[axis] for axis in ("rep", "fsdp", "seq"))
    assert reps == 4 and seqs == 2
    fine = Mesh(mesh.devices.reshape(reps // 2, 2, n, seqs), ("x", "core", "fsdp", "seq"))
    slots = P(("x", "core", "fsdp"), "seq", None)
    first, second = P("fsdp", None), P(None, "fsdp")
    return jax.shard_map(
        functools.partial(on_device, n),
        mesh=fine,
        in_specs=(
            slots,
            P(("x", "core", "fsdp")),
            slots,
            first,
            first,
            first,
            first,
            second,
            second,
            P("fsdp"),
        ),
        out_specs=(slots, slots, first, first, first, first, second, second, P("fsdp")),
        check_vma=False,
    )
```
